256 devices in a mesh: dp: 16 (over y, x), expert: 16 (over z, core).
Axes of the slice: x: 4, y: 4, z: 8, core: 2. Of those that a mesh axis runs over, the one named last changes fastest.
Arguments:
- tokens: bfloat16 [65536, 1024], P(('dp', 'expert')), may hold values from -24 to 24
- cotangent: bfloat16 [65536, 1024], P(('dp', 'expert')), may hold values from -6 to 6
- gates: bfloat16 [65536, 2], P(('dp', 'expert')), may hold values from 0.099609375 to 1
- expert_ids: int32 [65536, 2], P(('dp', 'expert')), may hold values from 0 to 15, all different within a row; in each aligned block of 128 rows (0 to 127, 128 to 255, ...) at most 32 rows name the same one
- expert_weights: bfloat16 [16, 3, 1024, 768], P('expert'), may hold values from -0.1875 to 0.1875
Outputs:
- tokens_grad: bfloat16 [65536, 1024], P(('dp', 'expert'))
- gates_grad: bfloat16 [65536, 2], P(('dp', 'expert'))
- weights_grad: bfloat16 [16, 3, 1024, 768], P('expert', None, 'dp')
The draws below stay inside these ranges and needn't reach their ends.
Inputs may be any that keep to these rules, and one draw needn't show every extreme that they name: `expert_ids`: within each micro-batch of 128 tokens of one device no expert is named by more than 32 routes, a bound that some block reaches; the two ids of a token differ.
All inputs are finite; a program needn't handle non-finite values.
Results may differ from the reference program's by a relative error of at most 0.017.
Values may be sent and summed in bfloat16 or wider, within the bound.
A program may use at most 64 MiB of HBM per device.

```python
import math
import jax
import jax.numpy as jnp
import numpy as np
from jax import lax

D = 1024
FF = 768
MICRO = 2
MB_TOK = 128
E = 16
CAP = 32
TOKENS = 65536
N_DP = 16
N_EXPERT = 16


def with_spikes(result, stream_key, source, target, parts, factor):
    owner, partner = [(jnp.arange(result.shape[axis_at]) // (result.shape[axis_at] // parts)).reshape([-1 if axis == axis_at else 1 for axis in range(result.ndim)]) for axis_at in (source, target)]
    chosen = jax.random.permutation(stream_key, parts)[partner]
    strong = (owner == chosen) | (owner == (partner + parts // 2) % parts)
    return jnp.where(strong, factor * result, result)


def shard_levels(own_key, extent, shards, low, top_value):
    factor_of, own = 1.0, jax.random.fold_in(own_key, 6)
    for axis_at, shards_of in shards:
        heights = jnp.exp(jax.random.uniform(jax.random.fold_in(own, axis_at), (shards_of,), jnp.float32, low / len(shards), top_value / len(shards)))
        factor_of = factor_of * jnp.repeat(heights, extent[axis_at] // shards_of).reshape([-1 if axis == axis_at else 1 for axis in range(len(extent))])
    return factor_of


def routed_block(own_key, own, number, rows, count, top, most, skew):
    order = jax.random.permutation(own_key, count)
    heavy_load, usual = load_shares(count, rows * top, most, skew, True), load_shares(count, rows * top, most, skew, False)
    places = jnp.arange(count)

    def named(lengths, rotation):
        used = int((lengths > 0).sum())
        fixed = max(1, used // 4)
        moved = fixed + (places - fixed + rotation * (used - fixed)) % max(1, count - fixed)
        return jnp.zeros((count,), jnp.int32).at[order[jnp.where(places < fixed, places, moved)]].set(jnp.asarray(lengths, jnp.int32))

    lengths = jnp.where(number % 4 == 0, named(heavy_load, number // 4), named(usual, number - number // 4 - 1))
    mixed = jax.random.permutation(jax.random.fold_in(own, 3), count)
    giver, taker = mixed[0:count // 2 * 2:2], mixed[1:count // 2 * 2:2]
    room = jnp.minimum(lengths[giver] - 1, most - lengths[taker]) // 2
    room = jnp.where((giver == order[0]) | (taker == order[0]) | (lengths[taker] == 0), 0, jnp.maximum(room, 0))
    moved = jax.random.randint(jax.random.fold_in(own, 4), (count // 2,), 0, 1 << 20) % (room + 1)
    lengths = lengths.at[giver].add(-moved).at[taker].add(moved)
    labels = jnp.searchsorted(jnp.cumsum(lengths), jnp.arange(rows * top), side="right").astype(jnp.int32)
    listing = labels.reshape(top, rows).T
    listing = listing[jax.random.permutation(jax.random.fold_in(own, 1), rows)]
    rotation = jax.random.randint(jax.random.fold_in(own, 2), (rows, 1), 0, top)
    return jnp.take_along_axis(listing, (jnp.arange(top)[None, :] + rotation) % top, axis=1)


def load_shares(count, total, limit, slope, full):
    portions = [(1 << 20) // math.isqrt(rank ** slope) + 1 for rank in range(1, count + 1)]
    largest = limit if full else min(limit, max(-(-total // count), total * portions[0] // sum(portions)))
    least = 1 if total - largest >= count - 1 else 0
    given, rest = [largest] + [least] * (count - 1), total - largest - least * (count - 1)
    while rest > 0:
        free = [i for i in range(1, count) if given[i] < largest] or [i for i in range(1, count) if given[i] < limit]
        whole, budget = sum([portions[i] for i in free]), rest
        for i in free:
            addition = min(limit - given[i], max(1, budget * portions[i] // whole), rest)
            given[i] = given[i] + addition
            rest = rest - addition
    return np.array(given)


def bell_draw(own_key, shape, width, reach, shards=(), kind=jnp.bfloat16):
    values = width * jax.random.normal(own_key, shape, jnp.float32)
    if shards:
        values = values * shard_levels(own_key, shape, shards, -0.22, 0.18)
    return jnp.clip(values, -reach, reach).astype(kind)


def noise_with(key, dims, scale, most, pieces, heavy, kind=jnp.bfloat16):
    values = scale * jax.random.normal(key, dims, jnp.float32)
    if pieces:
        values = values * shard_levels(key, dims, pieces, -0.22, 0.18)
    return jnp.clip(with_spikes(values, jax.random.fold_in(key, 3), *heavy), -most, most).astype(kind)


def setup_inputs(seed: int = 0) -> dict:
    arg_keys = jax.random.split(jax.random.key(seed), 6)
    tokens = noise_with(arg_keys[0], (TOKENS, D), 1.0, 24.0, ((0, 256),), (0, 1, 256, 6.0))
    cotangent = bell_draw(arg_keys[1], (TOKENS, D), 1.0, 6.0, ((0, 256),))
    gates = jnp.clip(0.099609375 + 0.9003906 * jax.random.uniform(arg_keys[2], (TOKENS, 2), jnp.float32) ** shard_levels(arg_keys[2], (TOKENS, 2), ((0, 256),), -0.2, 0.2), 0.099609375, 1.0).astype(jnp.bfloat16)
    expert_ids_keys = jax.random.split(jax.random.fold_in(arg_keys[3], 1), TOKENS // MB_TOK)
    expert_ids_turns = jax.random.permutation(jax.random.fold_in(arg_keys[3], 3), TOKENS // MB_TOK)
    expert_ids = jax.vmap(lambda own, number: routed_block(jax.random.fold_in(arg_keys[3], 2), own, number, MB_TOK, E, 2, CAP, 2))(expert_ids_keys, expert_ids_turns).reshape((TOKENS, 2))
    expert_weights = bell_draw(arg_keys[4], (E, 3, D, FF), D ** -0.5, 0.1875, ((0, 16),))
    return {"tokens": tokens, "cotangent": cotangent, "gates": gates, "expert_ids": expert_ids, "expert_weights": expert_weights}


def route_slots(ids_block, expert_count, capacity):
    flat_ids = ids_block.reshape(-1).astype(jnp.int32)
    one_hot = (flat_ids[:, None] == jnp.arange(expert_count, dtype=jnp.int32)[None, :]).astype(jnp.int32)
    earlier = jnp.cumsum(one_hot, axis=0) - one_hot
    rank_slot = jnp.sum(earlier * one_hot, axis=1).astype(jnp.int32)
    route_slot = (flat_ids * capacity + rank_slot).astype(jnp.int32)
    routes = jnp.arange(flat_ids.shape[0], dtype=jnp.int32)
    slot_route = jnp.zeros((expert_count * capacity,), jnp.int32).at[route_slot].set(routes)
    filled = jnp.zeros((expert_count * capacity,), jnp.int32).at[route_slot].set(1)
    return route_slot, slot_route, filled


def pack_rows(inputs, cotan, gate_vals, slot_route, filled, expert_count, capacity):
    token_index = (slot_route // 2).astype(jnp.int32)
    keeps = filled > 0
    feature_width = inputs.shape[1]
    rows_in = jnp.where(keeps[:, None], jnp.take(inputs, token_index, axis=0), jnp.zeros((), inputs.dtype))
    rows_cot = jnp.where(keeps[:, None], jnp.take(cotan, token_index, axis=0), jnp.zeros((), cotan.dtype))
    rows_gate = jnp.where(keeps, jnp.take(gate_vals.reshape(-1), slot_route), jnp.zeros((), gate_vals.dtype))
    return (rows_in.reshape(expert_count, capacity, feature_width),
            rows_cot.reshape(expert_count, capacity, feature_width),
            rows_gate.reshape(expert_count, capacity))


def expert_backward(rows_in, rows_cot, rows_gate, weights):
    w_gate = weights[0]
    w_up = weights[1]
    w_down = weights[2]
    contract_last = (((1,), (1,)), ((), ()))
    contract_first = (((0,), (0,)), ((), ()))
    pre_gate = jnp.dot(rows_in, w_gate, preferred_element_type=jnp.float32)
    pre_up = jnp.dot(rows_in, w_up, preferred_element_type=jnp.float32)
    sigmoid_gate = jax.nn.sigmoid(pre_gate)
    activated = pre_gate * sigmoid_gate
    hidden = (activated * pre_up).astype(jnp.bfloat16)
    output = lax.dot_general(hidden, w_down, contract_last, preferred_element_type=jnp.float32)
    gate_grad = jnp.sum(output * rows_cot.astype(jnp.float32), axis=1).astype(jnp.bfloat16)
    scaled = (rows_gate.astype(jnp.float32)[:, None] * rows_cot.astype(jnp.float32)).astype(jnp.bfloat16)
    hidden_grad = jnp.dot(scaled, w_down, preferred_element_type=jnp.float32)
    grad_pre_gate = (hidden_grad * pre_up * sigmoid_gate * (1.0 + pre_gate * (1.0 - sigmoid_gate))).astype(jnp.bfloat16)
    grad_pre_up = (hidden_grad * activated).astype(jnp.bfloat16)
    input_grad = (lax.dot_general(grad_pre_gate, w_gate, contract_last, preferred_element_type=jnp.float32)
                  + lax.dot_general(grad_pre_up, w_up, contract_last, preferred_element_type=jnp.float32)).astype(jnp.bfloat16)
    weight_grad = jnp.stack([
        lax.dot_general(rows_in, grad_pre_gate, contract_first, preferred_element_type=jnp.float32),
        lax.dot_general(rows_in, grad_pre_up, contract_first, preferred_element_type=jnp.float32),
        lax.dot_general(scaled, hidden, contract_first, preferred_element_type=jnp.float32)])
    return input_grad, gate_grad, weight_grad


def reference(tokens, cotangent, gates, expert_ids, expert_weights):
    expert_count = E
    capacity = CAP
    feature_width = D
    blocks_in = tokens.reshape(N_DP, N_EXPERT, MICRO, MB_TOK, feature_width)
    blocks_cot = cotangent.reshape(N_DP, N_EXPERT, MICRO, MB_TOK, feature_width)
    blocks_gate = gates.reshape(N_DP, N_EXPERT, MICRO, MB_TOK, 2)
    blocks_ids = expert_ids.reshape(N_DP, N_EXPERT, MICRO, MB_TOK, 2)

    def one_batch(batch_in, batch_cot, batch_gate, batch_ids):
        route_slot, slot_route, filled = route_slots(batch_ids, expert_count, capacity)
        rows_in, rows_cot, rows_gate = pack_rows(batch_in, batch_cot, batch_gate, slot_route, filled, expert_count, capacity)
        return rows_in, rows_cot, rows_gate, route_slot

    def unpack(grad_flat, gate_flat, route_slot):
        routed = jnp.take(grad_flat, route_slot, axis=0).astype(jnp.float32).reshape(MB_TOK, 2, feature_width)
        return jnp.sum(routed, axis=1).astype(jnp.bfloat16), jnp.take(gate_flat, route_slot).reshape(MB_TOK, 2)

    def one_row(grad_total, row_block):
        row_in, row_cot, row_gate, row_ids = row_block
        rows_in, rows_cot, rows_gate, route_slot = jax.vmap(jax.vmap(one_batch))(row_in, row_cot, row_gate, row_ids)
        rows_in = jnp.transpose(rows_in, (2, 0, 1, 3, 4)).reshape(expert_count, -1, feature_width)
        rows_cot = jnp.transpose(rows_cot, (2, 0, 1, 3, 4)).reshape(expert_count, -1, feature_width)
        rows_gate = jnp.transpose(rows_gate, (2, 0, 1, 3)).reshape(expert_count, -1)
        input_grad, gate_grad, weight_grad = lax.map(lambda packed_rows: expert_backward(*packed_rows),
                                                     (rows_in, rows_cot, rows_gate, expert_weights))
        rounded = lax.optimization_barrier(weight_grad.astype(jnp.bfloat16))
        grad_total = grad_total + rounded.astype(jnp.float32)
        back_in = jnp.transpose(input_grad.reshape(expert_count, N_EXPERT, MICRO, capacity, feature_width),
                                (1, 2, 0, 3, 4)).reshape(N_EXPERT, MICRO, expert_count * capacity, feature_width)
        back_gate = jnp.transpose(gate_grad.reshape(expert_count, N_EXPERT, MICRO, capacity),
                                  (1, 2, 0, 3)).reshape(N_EXPERT, MICRO, expert_count * capacity)
        token_grad, gate_out = jax.vmap(jax.vmap(unpack))(back_in, back_gate, route_slot)
        return grad_total, (token_grad, gate_out)

    start = jnp.zeros((expert_count, 3, feature_width, FF), jnp.float32)
    grad_total, (token_grad, gate_out) = lax.scan(one_row, start, (blocks_in, blocks_cot, blocks_gate, blocks_ids))
    return (token_grad.reshape(TOKENS, feature_width), gate_out.reshape(TOKENS, 2), grad_total.astype(jnp.bfloat16))
```

```python
import jax
import jax.numpy as jnp
from jax import lax
from jax.sharding import PartitionSpec as P

MICRO = 2
PAD = 128

F32 = jnp.float32
BF16 = jnp.bfloat16

CONTRACT_LAST = (((1,), (1,)), ((), ()))
CONTRACT_FIRST = (((0,), (0,)), ((), ()))


def mm(a, b):
    return jnp.dot(a, b, preferred_element_type=F32)


def route_masks(ids_block, expert_count, capacity):
    flat_ids = ids_block.reshape(-1)
    one_hot = (flat_ids[:, None] == jnp.arange(expert_count, dtype=jnp.int32)[None, :]).astype(
        jnp.int32
    )
    earlier = jnp.cumsum(one_hot, axis=0) - one_hot
    rank_slot = jnp.sum(earlier * one_hot, axis=1)
    route_slot = (flat_ids * capacity + rank_slot).reshape(-1, 2)
    position = jnp.arange(expert_count * capacity, dtype=jnp.int32)[:, None]
    return position == route_slot[None, :, 0], position == route_slot[None, :, 1]


def expert_step(recv, w_gate, w_up, w_down, width):
    rows_in = recv[:, :width]
    scaled = recv[:, width:]
    pre_gate = mm(rows_in, w_gate)
    pre_up = mm(rows_in, w_up)
    sigmoid_gate = jax.nn.sigmoid(pre_gate)
    activated = pre_gate * sigmoid_gate
    hidden = (activated * pre_up).astype(BF16)
    hidden_grad = mm(scaled, w_down)
    gate_sum = jnp.sum(hidden.astype(F32) * hidden_grad, axis=1)
    grad_pre_gate = (
        hidden_grad * pre_up * sigmoid_gate * (1.0 + pre_gate * (1.0 - sigmoid_gate))
    ).astype(BF16)
    grad_pre_up = (hidden_grad * activated).astype(BF16)
    input_grad = (
        lax.dot_general(grad_pre_gate, w_gate, CONTRACT_LAST, preferred_element_type=F32)
        + lax.dot_general(grad_pre_up, w_up, CONTRACT_LAST, preferred_element_type=F32)
    ).astype(BF16)
    grads = (
        lax.dot_general(rows_in, grad_pre_gate, CONTRACT_FIRST, preferred_element_type=F32),
        lax.dot_general(rows_in, grad_pre_up, CONTRACT_FIRST, preferred_element_type=F32),
        lax.dot_general(scaled, hidden, CONTRACT_FIRST, preferred_element_type=F32),
    )
    high = gate_sum.astype(BF16)
    low = (gate_sum - high.astype(F32)).astype(BF16)
    tail = jnp.concatenate(
        [high[:, None], low[:, None], jnp.zeros((recv.shape[0], PAD - 2), BF16)], axis=1
    )
    return jnp.concatenate([input_grad, tail], axis=1), grads


def on_device(tokens, cotangent, gates, expert_ids, expert_weights):
    n_expert = lax.axis_size("expert")
    expert_count = n_expert * expert_weights.shape[0]
    batch_rows = tokens.shape[0] // MICRO
    capacity = max(2, 4 * batch_rows // expert_count)
    width = tokens.shape[1]
    w_gate, w_up, w_down = expert_weights[0, 0], expert_weights[0, 1], expert_weights[0, 2]

    token_parts, gate_parts = [], []
    totals = None
    for micro_index in range(MICRO):
        lower = micro_index * batch_rows
        upper = lower + batch_rows
        first, second = route_masks(expert_ids[lower:upper], expert_count, capacity)
        both = (first | second).astype(BF16)
        cot = cotangent[lower:upper].astype(F32)
        gate = gates[lower:upper].astype(F32)
        scaled_first = (gate[:, 0:1] * cot).astype(BF16)
        scaled_second = (gate[:, 1:2] * cot).astype(BF16)
        rows_in = mm(both, tokens[lower:upper]).astype(BF16)
        rows_scaled = (
            mm(first.astype(BF16), scaled_first) + mm(second.astype(BF16), scaled_second)
        ).astype(BF16)
        payload = jnp.concatenate([rows_in, rows_scaled], axis=1).reshape(
            n_expert, -1, 2 * width
        )
        recv = lax.all_to_all(payload, "expert", 0, 0, tiled=True).reshape(-1, 2 * width)
        back, grads = expert_step(recv, w_gate, w_up, w_down, width)
        totals = grads if totals is None else tuple(t + g for t, g in zip(totals, grads))
        ret = lax.all_to_all(
            back.reshape(n_expert, -1, width + PAD), "expert", 0, 0, tiled=True
        ).reshape(-1, width + PAD)
        token_grad = lax.dot_general(
            both, ret[:, :width], CONTRACT_FIRST, preferred_element_type=F32
        ).astype(BF16)
        gate_sum = ret[:, width].astype(F32) + ret[:, width + 1].astype(F32)
        sum_first = jnp.sum(jnp.where(first, gate_sum[:, None], 0.0), axis=0)
        sum_second = jnp.sum(jnp.where(second, gate_sum[:, None], 0.0), axis=0)
        gate_grad = jnp.stack([sum_first / gate[:, 0], sum_second / gate[:, 1]], axis=1)
        token_parts.append(token_grad)
        gate_parts.append(gate_grad.astype(BF16))

    rounded = jnp.stack(totals).astype(BF16)[None]
    weights_grad = lax.psum_scatter(rounded, "dp", scatter_dimension=2, tiled=True)
    return (
        jnp.concatenate(token_parts, axis=0),
        jnp.concatenate(gate_parts, axis=0),
        weights_grad,
    )


def solution(mesh):
    placed = (
        P(("dp", "expert"), None),
        P(("dp", "expert"), None),
        P(("dp", "expert"), None),
        P(("dp", "expert"), None),
        P("expert", None, None, None),
    )
    return jax.shard_map(
        on_device,
        mesh=mesh,
        in_specs=placed,
        out_specs=(
            P(("dp", "expert"), None),
            P(("dp", "expert"), None),
            P("expert", None, "dp", None),
        ),
        check_vma=False,
    )
```

```python
import jax
import jax.numpy as jnp
from jax import lax
from jax.experimental import pallas as pl
from jax.experimental.pallas import tpu as pltpu
from jax.sharding import PartitionSpec as P

MICRO = 2
PAD = 128

F32 = jnp.float32
BF16 = jnp.bfloat16

CONTRACT_LAST = (((1,), (1,)), ((), ()))
CONTRACT_FIRST = (((0,), (0,)), ((), ()))
MESH = pl.DeviceIdType.MESH


def mm(a, b):
    return jnp.dot(a, b, preferred_element_type=F32)


def route_masks(ids_block, expert_count, capacity):
    flat_ids = ids_block.reshape(-1)
    one_hot = (flat_ids[:, None] == jnp.arange(expert_count, dtype=jnp.int32)[None, :]).astype(
        jnp.int32
    )
    earlier = jnp.cumsum(one_hot, axis=0) - one_hot
    rank_slot = jnp.sum(earlier * one_hot, axis=1)
    route_slot = (flat_ids * capacity + rank_slot).reshape(-1, 2)
    position = jnp.arange(expert_count * capacity, dtype=jnp.int32)[:, None]
    return position == route_slot[None, :, 0], position == route_slot[None, :, 1]


def expert_step(recv, w_gate, w_up, w_down, width):
    rows_in = recv[:, :width]
    scaled = recv[:, width:]
    pre_gate = mm(rows_in, w_gate)
    pre_up = mm(rows_in, w_up)
    sigmoid_gate = jax.nn.sigmoid(pre_gate)
    activated = pre_gate * sigmoid_gate
    hidden = (activated * pre_up).astype(BF16)
    hidden_grad = mm(scaled, w_down)
    gate_sum = jnp.sum(hidden.astype(F32) * hidden_grad, axis=1)
    grad_pre_gate = (
        hidden_grad * pre_up * sigmoid_gate * (1.0 + pre_gate * (1.0 - sigmoid_gate))
    ).astype(BF16)
    grad_pre_up = (hidden_grad * activated).astype(BF16)
    input_grad = (
        lax.dot_general(grad_pre_gate, w_gate, CONTRACT_LAST, preferred_element_type=F32)
        + lax.dot_general(grad_pre_up, w_up, CONTRACT_LAST, preferred_element_type=F32)
    ).astype(BF16)
    grads = (
        lax.dot_general(rows_in, grad_pre_gate, CONTRACT_FIRST, preferred_element_type=F32),
        lax.dot_general(rows_in, grad_pre_up, CONTRACT_FIRST, preferred_element_type=F32),
        lax.dot_general(scaled, hidden, CONTRACT_FIRST, preferred_element_type=F32),
    )
    high = gate_sum.astype(BF16)
    low = (gate_sum - high.astype(F32)).astype(BF16)
    tail = jnp.concatenate(
        [high[:, None], low[:, None], jnp.zeros((recv.shape[0], PAD - 2), BF16)], axis=1
    )
    return jnp.concatenate([input_grad, tail], axis=1), grads


def exchange_kernel(p0_ref, p1_ref, w_ref, ret0_ref, ret1_ref, grad_ref,
                    r0, r1, b0, b1, send_sem, recv_sem):
    n = lax.axis_size("expert")
    me = lax.axis_index("expert")
    row = lax.axis_index("dp")
    chunk = p0_ref.shape[0] // n
    width = w_ref.shape[1]

    barrier = pltpu.get_barrier_semaphore()
    for k in range(1, n):
        peer = lax.rem(me + k, n)
        pl.semaphore_signal(barrier, inc=1, device_id=(row, peer), device_id_type=MESH)
    pl.semaphore_wait(barrier, n - 1)

    def send(src, dst, phase):
        mine = pl.ds(pl.multiple_of(me * chunk, chunk), chunk)
        local = pltpu.make_async_copy(src.at[mine], dst.at[mine], recv_sem.at[phase])
        local.start()
        for k in range(1, n):
            peer = lax.rem(me + k, n)
            rows = pl.ds(pl.multiple_of(peer * chunk, chunk), chunk)
            pltpu.make_async_remote_copy(
                src_ref=src.at[rows],
                dst_ref=dst.at[mine],
                send_sem=send_sem.at[phase],
                recv_sem=recv_sem.at[phase],
                device_id=(row, peer),
                device_id_type=MESH,
            ).start()

    def wait_recv(dst, phase):
        pltpu.make_async_copy(dst, dst, recv_sem.at[phase]).wait()

    def wait_send(src, phase):
        rest = pl.ds(0, (n - 1) * chunk)
        pltpu.make_async_copy(src.at[rest], src.at[rest], send_sem.at[phase]).wait()

    def compute(recv, back, first):
        rows_in = recv[:, :width]
        scaled = recv[:, width:]
        w_gate = w_ref[0]
        w_up = w_ref[1]
        w_down = w_ref[2]
        pre_gate = mm(rows_in, w_gate)
        pre_up = mm(rows_in, w_up)
        sigmoid_gate = jax.nn.sigmoid(pre_gate)
        activated = pre_gate * sigmoid_gate
        hidden = (activated * pre_up).astype(BF16)
        hidden_grad = mm(scaled, w_down)
        gate_sum = jnp.sum(hidden.astype(F32) * hidden_grad, axis=1, keepdims=True)
        grad_pre_gate = (
            hidden_grad * pre_up * sigmoid_gate * (1.0 + pre_gate * (1.0 - sigmoid_gate))
        ).astype(BF16)
        grad_pre_up = (hidden_grad * activated).astype(BF16)
        input_grad = (
            lax.dot_general(grad_pre_gate, w_gate, CONTRACT_LAST, preferred_element_type=F32)
            + lax.dot_general(grad_pre_up, w_up, CONTRACT_LAST, preferred_element_type=F32)
        ).astype(BF16)
        back[:, :width] = input_grad
        high = gate_sum.astype(BF16).astype(F32)
        low = gate_sum - high
        column = lax.broadcasted_iota(jnp.int32, (recv.shape[0], PAD), 1)
        tail = jnp.where(column == 0, high, jnp.where(column == 1, low, 0.0))
        back[:, width:] = tail.astype(BF16)
        grads = (
            lax.dot_general(rows_in, grad_pre_gate, CONTRACT_FIRST, preferred_element_type=F32),
            lax.dot_general(rows_in, grad_pre_up, CONTRACT_FIRST, preferred_element_type=F32),
            lax.dot_general(scaled, hidden, CONTRACT_FIRST, preferred_element_type=F32),
        )
        for index, value in enumerate(grads):
            if first:
                grad_ref[index] = value
            else:
                grad_ref[index] += value

    send(p0_ref, r0, 0)
    wait_recv(r0, 0)
    send(p1_ref, r1, 1)
    compute(r0, b0, True)
    send(b0, ret0_ref, 2)
    wait_recv(r1, 1)
    compute(r1, b1, False)
    send(b1, ret1_ref, 3)
    wait_recv(ret0_ref, 2)
    wait_recv(ret1_ref, 3)
    wait_send(p0_ref, 0)
    wait_send(p1_ref, 1)
    wait_send(b0, 2)
    wait_send(b1, 3)


def exchange(p0, p1, weights):
    slots, full = p0.shape
    width = weights.shape[1]
    back = jax.ShapeDtypeStruct((slots, width + PAD), BF16)
    vmem = pl.BlockSpec(memory_space=pltpu.VMEM)
    return pl.pallas_call(
        exchange_kernel,
        out_shape=(back, back, jax.ShapeDtypeStruct(weights.shape, F32)),
        in_specs=[vmem] * 3,
        out_specs=(vmem, vmem, vmem),
        scratch_shapes=[
            pltpu.VMEM((slots, full), BF16),
            pltpu.VMEM((slots, full), BF16),
            pltpu.VMEM((slots, width + PAD), BF16),
            pltpu.VMEM((slots, width + PAD), BF16),
            pltpu.SemaphoreType.DMA((4,)),
            pltpu.SemaphoreType.DMA((4,)),
        ],
        compiler_params=pltpu.CompilerParams(
            collective_id=0, has_side_effects=True, vmem_limit_bytes=60 * 1024 * 1024
        ),
    )(p0, p1, weights)


def on_device(tokens, cotangent, gates, expert_ids, expert_weights):
    n_expert = lax.axis_size("expert")
    expert_count = n_expert * expert_weights.shape[0]
    batch_rows = tokens.shape[0] // MICRO
    capacity = max(2, 4 * batch_rows // expert_count)
    width = tokens.shape[1]

    masks, gate_list, payloads = [], [], []
    for micro_index in range(MICRO):
        lower = micro_index * batch_rows
        upper = lower + batch_rows
        first, second = route_masks(expert_ids[lower:upper], expert_count, capacity)
        both = (first | second).astype(BF16)
        cot = cotangent[lower:upper].astype(F32)
        gate = gates[lower:upper].astype(F32)
        scaled_first = (gate[:, 0:1] * cot).astype(BF16)
        scaled_second = (gate[:, 1:2] * cot).astype(BF16)
        rows_in = mm(both, tokens[lower:upper]).astype(BF16)
        rows_scaled = (
            mm(first.astype(BF16), scaled_first) + mm(second.astype(BF16), scaled_second)
        ).astype(BF16)
        payloads.append(jnp.concatenate([rows_in, rows_scaled], axis=1))
        masks.append((first, second, both))
        gate_list.append(gate)

    ret0, ret1, totals = exchange(payloads[0], payloads[1], expert_weights[0])

    token_parts, gate_parts = [], []
    for (first, second, both), gate, ret in zip(masks, gate_list, (ret0, ret1)):
        token_grad = lax.dot_general(
            both, ret[:, :width], CONTRACT_FIRST, preferred_element_type=F32
        ).astype(BF16)
        gate_sum = ret[:, width].astype(F32) + ret[:, width + 1].astype(F32)
        sum_first = jnp.sum(jnp.where(first, gate_sum[:, None], 0.0), axis=0)
        sum_second = jnp.sum(jnp.where(second, gate_sum[:, None], 0.0), axis=0)
        gate_grad = jnp.stack([sum_first / gate[:, 0], sum_second / gate[:, 1]], axis=1)
        token_parts.append(token_grad)
        gate_parts.append(gate_grad.astype(BF16))

    rounded = totals.astype(BF16)[None]
    weights_grad = lax.psum_scatter(rounded, "dp", scatter_dimension=2, tiled=True)
    return (
        jnp.concatenate(token_parts, axis=0),
        jnp.concatenate(gate_parts, axis=0),
        weights_grad,
    )


def solution(mesh):
    placed = (
        P(("dp", "expert"), None),
        P(("dp", "expert"), None),
        P(("dp", "expert"), None),
        P(("dp", "expert"), None),
        P("expert", None, None, None),
    )
    return jax.shard_map(
        on_device,
        mesh=mesh,
        in_specs=placed,
        out_specs=(
            P(("dp", "expert"), None),
            P(("dp", "expert"), None),
            P("expert", None, "dp", None),
        ),
        check_vma=False,
    )
```

```python
import jax
import jax.numpy as jnp
from jax import lax
from jax.experimental import pallas as pl
from jax.experimental.pallas import tpu as pltpu
from jax.sharding import PartitionSpec as P

MICRO = 2
PAD = 128

F32 = jnp.float32
BF16 = jnp.bfloat16

CONTRACT_LAST = (((1,), (1,)), ((), ()))
CONTRACT_FIRST = (((0,), (0,)), ((), ()))
MESH = pl.DeviceIdType.MESH


def mm(a, b):
    return jnp.dot(a, b, preferred_element_type=F32)


def route_masks(ids_block, expert_count, capacity):
    flat_ids = ids_block.reshape(-1)
    one_hot = (flat_ids[:, None] == jnp.arange(expert_count, dtype=jnp.int32)[None, :]).astype(
        jnp.int32
    )
    earlier = jnp.cumsum(one_hot, axis=0) - one_hot
    rank_slot = jnp.sum(earlier * one_hot, axis=1)
    route_slot = (flat_ids * capacity + rank_slot).reshape(-1, 2)
    position = jnp.arange(expert_count * capacity, dtype=jnp.int32)[:, None]
    return position == route_slot[None, :, 0], position == route_slot[None, :, 1]


def expert_step(recv, w_gate, w_up, w_down, width):
    rows_in = recv[:, :width]
    scaled = recv[:, width:]
    pre_gate = mm(rows_in, w_gate)
    pre_up = mm(rows_in, w_up)
    sigmoid_gate = jax.nn.sigmoid(pre_gate)
    activated = pre_gate * sigmoid_gate
    hidden = (activated * pre_up).astype(BF16)
    hidden_grad = mm(scaled, w_down)
    gate_sum = jnp.sum(hidden.astype(F32) * hidden_grad, axis=1)
    grad_pre_gate = (
        hidden_grad * pre_up * sigmoid_gate * (1.0 + pre_gate * (1.0 - sigmoid_gate))
    ).astype(BF16)
    grad_pre_up = (hidden_grad * activated).astype(BF16)
    input_grad = (
        lax.dot_general(grad_pre_gate, w_gate, CONTRACT_LAST, preferred_element_type=F32)
        + lax.dot_general(grad_pre_up, w_up, CONTRACT_LAST, preferred_element_type=F32)
    ).astype(BF16)
    grads = (
        lax.dot_general(rows_in, grad_pre_gate, CONTRACT_FIRST, preferred_element_type=F32),
        lax.dot_general(rows_in, grad_pre_up, CONTRACT_FIRST, preferred_element_type=F32),
        lax.dot_general(scaled, hidden, CONTRACT_FIRST, preferred_element_type=F32),
    )
    high = gate_sum.astype(BF16)
    low = (gate_sum - high.astype(F32)).astype(BF16)
    tail = jnp.concatenate(
        [high[:, None], low[:, None], jnp.zeros((recv.shape[0], PAD - 2), BF16)], axis=1
    )
    return jnp.concatenate([input_grad, tail], axis=1), grads


def exchange_kernel(p0_ref, p1_ref, w_ref, ret0_ref, ret1_ref, out_ref,
                    r0, r1, b0, b1, grad_ref, rounded, gathered, send_sem, recv_sem):
    n = lax.axis_size("expert")
    me = lax.axis_index("expert")
    n_row = lax.axis_size("dp")
    row = lax.axis_index("dp")
    chunk = p0_ref.shape[0] // n
    width = w_ref.shape[1]
    part = out_ref.shape[1]

    barrier = pltpu.get_barrier_semaphore()
    for k in range(1, n):
        peer = lax.rem(me + k, n)
        pl.semaphore_signal(barrier, inc=1, device_id=(row, peer), device_id_type=MESH)
    for k in range(1, n_row):
        peer = lax.rem(row + k, n_row)
        pl.semaphore_signal(barrier, inc=1, device_id=(peer, me), device_id_type=MESH)
    pl.semaphore_wait(barrier, n - 1 + n_row - 1)

    def send(src, dst, phase):
        mine = pl.ds(pl.multiple_of(me * chunk, chunk), chunk)
        local = pltpu.make_async_copy(src.at[mine], dst.at[mine], recv_sem.at[phase])
        local.start()
        for k in range(1, n):
            peer = lax.rem(me + k, n)
            rows = pl.ds(pl.multiple_of(peer * chunk, chunk), chunk)
            pltpu.make_async_remote_copy(
                src_ref=src.at[rows],
                dst_ref=dst.at[mine],
                send_sem=send_sem.at[phase],
                recv_sem=recv_sem.at[phase],
                device_id=(row, peer),
                device_id_type=MESH,
            ).start()

    def wait_recv(dst, phase):
        pltpu.make_async_copy(dst, dst, recv_sem.at[phase]).wait()

    def wait_send(src, phase):
        rest = pl.ds(0, (n - 1) * chunk)
        pltpu.make_async_copy(src.at[rest], src.at[rest], send_sem.at[phase]).wait()

    def compute(recv, back, first):
        rows_in = recv[:, :width]
        scaled = recv[:, width:]
        w_gate = w_ref[0]
        w_up = w_ref[1]
        w_down = w_ref[2]
        pre_gate = mm(rows_in, w_gate)
        pre_up = mm(rows_in, w_up)
        sigmoid_gate = jax.nn.sigmoid(pre_gate)
        activated = pre_gate * sigmoid_gate
        hidden = (activated * pre_up).astype(BF16)
        hidden_grad = mm(scaled, w_down)
        gate_sum = jnp.sum(hidden.astype(F32) * hidden_grad, axis=1, keepdims=True)
        grad_pre_gate = (
            hidden_grad * pre_up * sigmoid_gate * (1.0 + pre_gate * (1.0 - sigmoid_gate))
        ).astype(BF16)
        grad_pre_up = (hidden_grad * activated).astype(BF16)
        input_grad = (
            lax.dot_general(grad_pre_gate, w_gate, CONTRACT_LAST, preferred_element_type=F32)
            + lax.dot_general(grad_pre_up, w_up, CONTRACT_LAST, preferred_element_type=F32)
        ).astype(BF16)
        back[:, :width] = input_grad
        high = gate_sum.astype(BF16).astype(F32)
        low = gate_sum - high
        column = lax.broadcasted_iota(jnp.int32, (recv.shape[0], PAD), 1)
        tail = jnp.where(column == 0, high, jnp.where(column == 1, low, 0.0))
        back[:, width:] = tail.astype(BF16)
        grads = (
            lax.dot_general(rows_in, grad_pre_gate, CONTRACT_FIRST, preferred_element_type=F32),
            lax.dot_general(rows_in, grad_pre_up, CONTRACT_FIRST, preferred_element_type=F32),
            lax.dot_general(scaled, hidden, CONTRACT_FIRST, preferred_element_type=F32),
        )
        for index, value in enumerate(grads):
            if first:
                grad_ref[index] = value
            else:
                grad_ref[index] += value

    send(p0_ref, r0, 0)
    wait_recv(r0, 0)
    send(p1_ref, r1, 1)
    compute(r0, b0, True)
    send(b0, ret0_ref, 2)
    wait_recv(r1, 1)
    compute(r1, b1, False)
    send(b1, ret1_ref, 3)

    rounded[...] = grad_ref[...].astype(BF16)
    mine = pl.ds(pl.multiple_of(row * part, part), part)
    pltpu.make_async_copy(rounded.at[:, mine], gathered.at[row], recv_sem.at[4]).start()
    for k in range(1, n_row):
        peer = lax.rem(row + k, n_row)
        pltpu.make_async_remote_copy(
            src_ref=rounded.at[:, pl.ds(pl.multiple_of(peer * part, part), part)],
            dst_ref=gathered.at[row],
            send_sem=send_sem.at[4],
            recv_sem=recv_sem.at[4],
            device_id=(peer, me),
            device_id_type=MESH,
        ).start()
    pltpu.make_async_copy(gathered, gathered, recv_sem.at[4]).wait()
    total = gathered[0].astype(F32)
    for k in range(1, n_row):
        total = total + gathered[k].astype(F32)
    out_ref[...] = total.astype(BF16)

    wait_recv(ret0_ref, 2)
    wait_recv(ret1_ref, 3)
    wait_send(p0_ref, 0)
    wait_send(p1_ref, 1)
    wait_send(b0, 2)
    wait_send(b1, 3)
    rest = pl.ds(0, n_row - 1)
    pltpu.make_async_copy(gathered.at[rest], gathered.at[rest], send_sem.at[4]).wait()


def exchange(p0, p1, weights, n_row):
    slots, full = p0.shape
    width = weights.shape[1]
    part = width // n_row
    back = jax.ShapeDtypeStruct((slots, width + PAD), BF16)
    share = (weights.shape[0], part, weights.shape[2])
    vmem = pl.BlockSpec(memory_space=pltpu.VMEM)
    return pl.pallas_call(
        exchange_kernel,
        out_shape=(back, back, jax.ShapeDtypeStruct(share, BF16)),
        in_specs=[vmem] * 3,
        out_specs=(vmem, vmem, vmem),
        scratch_shapes=[
            pltpu.VMEM((slots, full), BF16),
            pltpu.VMEM((slots, full), BF16),
            pltpu.VMEM((slots, width + PAD), BF16),
            pltpu.VMEM((slots, width + PAD), BF16),
            pltpu.VMEM(weights.shape, F32),
            pltpu.VMEM(weights.shape, BF16),
            pltpu.VMEM((n_row,) + share, BF16),
            pltpu.SemaphoreType.DMA((5,)),
            pltpu.SemaphoreType.DMA((5,)),
        ],
        compiler_params=pltpu.CompilerParams(
            collective_id=0, has_side_effects=True, vmem_limit_bytes=60 * 1024 * 1024
        ),
    )(p0, p1, weights)


def on_device(tokens, cotangent, gates, expert_ids, expert_weights):
    n_expert = lax.axis_size("expert")
    expert_count = n_expert * expert_weights.shape[0]
    batch_rows = tokens.shape[0] // MICRO
    capacity = max(2, 4 * batch_rows // expert_count)
    width = tokens.shape[1]

    masks, gate_list, payloads = [], [], []
    for micro_index in range(MICRO):
        lower = micro_index * batch_rows
        upper = lower + batch_rows
        first, second = route_masks(expert_ids[lower:upper], expert_count, capacity)
        both = (first | second).astype(BF16)
        cot = cotangent[lower:upper].astype(F32)
        gate = gates[lower:upper].astype(F32)
        scaled_first = (gate[:, 0:1] * cot).astype(BF16)
        scaled_second = (gate[:, 1:2] * cot).astype(BF16)
        rows_in = mm(both, tokens[lower:upper]).astype(BF16)
        rows_scaled = (
            mm(first.astype(BF16), scaled_first) + mm(second.astype(BF16), scaled_second)
        ).astype(BF16)
        payloads.append(jnp.concatenate([rows_in, rows_scaled], axis=1))
        masks.append((first, second, both))
        gate_list.append(gate)

    ret0, ret1, weights_grad = exchange(
        payloads[0], payloads[1], expert_weights[0], lax.axis_size("dp")
    )

    token_parts, gate_parts = [], []
    for (first, second, both), gate, ret in zip(masks, gate_list, (ret0, ret1)):
        token_grad = lax.dot_general(
            both, ret[:, :width], CONTRACT_FIRST, preferred_element_type=F32
        ).astype(BF16)
        gate_sum = ret[:, width].astype(F32) + ret[:, width + 1].astype(F32)
        sum_first = jnp.sum(jnp.where(first, gate_sum[:, None], 0.0), axis=0)
        sum_second = jnp.sum(jnp.where(second, gate_sum[:, None], 0.0), axis=0)
        gate_grad = jnp.stack([sum_first / gate[:, 0], sum_second / gate[:, 1]], axis=1)
        token_parts.append(token_grad)
        gate_parts.append(gate_grad.astype(BF16))

    return (
        jnp.concatenate(token_parts, axis=0),
        jnp.concatenate(gate_parts, axis=0),
        weights_grad[None],
    )


def solution(mesh):
    placed = (
        P(("dp", "expert"), None),
        P(("dp", "expert"), None),
        P(("dp", "expert"), None),
        P(("dp", "expert"), None),
        P("expert", None, None, None),
    )
    return jax.shard_map(
        on_device,
        mesh=mesh,
        in_specs=placed,
        out_specs=(
            P(("dp", "expert"), None),
            P(("dp", "expert"), None),
            P("expert", None, "dp", None),
        ),
        check_vma=False,
    )
```

```python
import jax
import jax.numpy as jnp
from jax import lax
from jax.experimental import pallas as pl
from jax.experimental.pallas import tpu as pltpu
from jax.sharding import PartitionSpec as P

MICRO = 2
SPLITS = 2
PAD = 128

F32 = jnp.float32
BF16 = jnp.bfloat16

CONTRACT_LAST = (((1,), (1,)), ((), ()))
CONTRACT_FIRST = (((0,), (0,)), ((), ()))
MESH = pl.DeviceIdType.MESH


def mm(a, b):
    return jnp.dot(a, b, preferred_element_type=F32)


def route_masks(ids_block, expert_count, capacity):
    flat_ids = ids_block.reshape(-1)
    one_hot = (flat_ids[:, None] == jnp.arange(expert_count, dtype=jnp.int32)[None, :]).astype(
        jnp.int32
    )
    earlier = jnp.cumsum(one_hot, axis=0) - one_hot
    rank_slot = jnp.sum(earlier * one_hot, axis=1)
    route_slot = (flat_ids * capacity + rank_slot).reshape(-1, 2)
    position = jnp.arange(expert_count * capacity, dtype=jnp.int32)[:, None]
    return position == route_slot[None, :, 0], position == route_slot[None, :, 1]


def expert_step(recv, w_gate, w_up, w_down, width):
    rows_in = recv[:, :width]
    scaled = recv[:, width:]
    pre_gate = mm(rows_in, w_gate)
    pre_up = mm(rows_in, w_up)
    sigmoid_gate = jax.nn.sigmoid(pre_gate)
    activated = pre_gate * sigmoid_gate
    hidden = (activated * pre_up).astype(BF16)
    hidden_grad = mm(scaled, w_down)
    gate_sum = jnp.sum(hidden.astype(F32) * hidden_grad, axis=1)
    grad_pre_gate = (
        hidden_grad * pre_up * sigmoid_gate * (1.0 + pre_gate * (1.0 - sigmoid_gate))
    ).astype(BF16)
    grad_pre_up = (hidden_grad * activated).astype(BF16)
    input_grad = (
        lax.dot_general(grad_pre_gate, w_gate, CONTRACT_LAST, preferred_element_type=F32)
        + lax.dot_general(grad_pre_up, w_up, CONTRACT_LAST, preferred_element_type=F32)
    ).astype(BF16)
    grads = (
        lax.dot_general(rows_in, grad_pre_gate, CONTRACT_FIRST, preferred_element_type=F32),
        lax.dot_general(rows_in, grad_pre_up, CONTRACT_FIRST, preferred_element_type=F32),
        lax.dot_general(scaled, hidden, CONTRACT_FIRST, preferred_element_type=F32),
    )
    high = gate_sum.astype(BF16)
    low = (gate_sum - high.astype(F32)).astype(BF16)
    tail = jnp.concatenate(
        [high[:, None], low[:, None], jnp.zeros((recv.shape[0], PAD - 2), BF16)], axis=1
    )
    return jnp.concatenate([input_grad, tail], axis=1), grads


def exchange_kernel(p0_ref, p1_ref, w_ref, ret0_ref, ret1_ref, out_ref,
                    recv, back, grad_ref, rounded, gathered, send_sem, recv_sem):
    n = lax.axis_size("expert")
    me = lax.axis_index("expert")
    n_row = lax.axis_size("dp")
    row = lax.axis_index("dp")
    phases = recv.shape[0]
    splits = phases // MICRO
    capacity = p0_ref.shape[0] // n
    piece = capacity // splits
    width = w_ref.shape[1]
    part = out_ref.shape[1]
    payloads = (p0_ref, p1_ref)
    returns = (ret0_ref, ret1_ref)

    barrier = pltpu.get_barrier_semaphore()
    for k in range(1, n):
        peer = lax.rem(me + k, n)
        pl.semaphore_signal(barrier, inc=1, device_id=(row, peer), device_id_type=MESH)
    for k in range(1, n_row):
        peer = lax.rem(row + k, n_row)
        pl.semaphore_signal(barrier, inc=1, device_id=(peer, me), device_id_type=MESH)
    pl.semaphore_wait(barrier, n - 1 + n_row - 1)

    def slot_rows(expert, phase):
        start = expert * capacity + (phase % splits) * piece
        return pl.ds(pl.multiple_of(start, piece), piece)

    def held_rows(source):
        return pl.ds(pl.multiple_of(source * piece, piece), piece)

    def scatter(phase, src_rows, dst_rows, src, dst, sem):
        pltpu.make_async_copy(src.at[src_rows(me)], dst.at[dst_rows(me)], recv_sem.at[sem]).start()
        for k in range(1, n):
            peer = lax.rem(me + k, n)
            pltpu.make_async_remote_copy(
                src_ref=src.at[src_rows(peer)],
                dst_ref=dst.at[dst_rows(me)],
                send_sem=send_sem.at[sem],
                recv_sem=recv_sem.at[sem],
                device_id=(row, peer),
                device_id_type=MESH,
            ).start()

    def send_forward(phase):
        scatter(phase, lambda e: slot_rows(e, phase), held_rows,
                payloads[phase // splits], recv.at[phase], phase)

    def send_back(phase):
        scatter(phase, held_rows, lambda e: slot_rows(e, phase),
                back.at[phase], returns[phase // splits], phases + phase)

    def wait_all(buf, sem):
        pltpu.make_async_copy(buf, buf, recv_sem.at[sem]).wait()

    def wait_sent(buf, sem):
        rest = pl.ds(0, (n - 1) * piece)
        pltpu.make_async_copy(buf.at[rest], buf.at[rest], send_sem.at[sem]).wait()

    def scatter_grads():
        rounded[...] = grad_ref[...].astype(BF16)
        mine = pl.ds(pl.multiple_of(row * part, part), part)
        pltpu.make_async_copy(rounded.at[:, mine], gathered.at[row], recv_sem.at[2 * phases]).start()
        for k in range(1, n_row):
            peer = lax.rem(row + k, n_row)
            pltpu.make_async_remote_copy(
                src_ref=rounded.at[:, pl.ds(pl.multiple_of(peer * part, part), part)],
                dst_ref=gathered.at[row],
                send_sem=send_sem.at[2 * phases],
                recv_sem=recv_sem.at[2 * phases],
                device_id=(peer, me),
                device_id_type=MESH,
            ).start()

    def compute(phase):
        held = recv.at[phase]
        rows_in = held[:, :width]
        scaled = held[:, width:]
        w_gate = w_ref[0]
        w_up = w_ref[1]
        w_down = w_ref[2]
        pre_gate = mm(rows_in, w_gate)
        pre_up = mm(rows_in, w_up)
        sigmoid_gate = jax.nn.sigmoid(pre_gate)
        activated = pre_gate * sigmoid_gate
        hidden = (activated * pre_up).astype(BF16)
        hidden_grad = mm(scaled, w_down)
        gate_sum = jnp.sum(hidden.astype(F32) * hidden_grad, axis=1, keepdims=True)
        grad_pre_gate = (
            hidden_grad * pre_up * sigmoid_gate * (1.0 + pre_gate * (1.0 - sigmoid_gate))
        ).astype(BF16)
        grad_pre_up = (hidden_grad * activated).astype(BF16)
        grads = (
            lax.dot_general(rows_in, grad_pre_gate, CONTRACT_FIRST, preferred_element_type=F32),
            lax.dot_general(rows_in, grad_pre_up, CONTRACT_FIRST, preferred_element_type=F32),
            lax.dot_general(scaled, hidden, CONTRACT_FIRST, preferred_element_type=F32),
        )
        for index, value in enumerate(grads):
            if phase == 0:
                grad_ref[index] = value
            else:
                grad_ref[index] += value
        if phase == phases - 1:
            scatter_grads()
        input_grad = (
            lax.dot_general(grad_pre_gate, w_gate, CONTRACT_LAST, preferred_element_type=F32)
            + lax.dot_general(grad_pre_up, w_up, CONTRACT_LAST, preferred_element_type=F32)
        ).astype(BF16)
        out = back.at[phase]
        out[:, :width] = input_grad
        high = gate_sum.astype(BF16).astype(F32)
        low = gate_sum - high
        column = lax.broadcasted_iota(jnp.int32, (input_grad.shape[0], PAD), 1)
        tail = jnp.where(column == 0, high, jnp.where(column == 1, low, 0.0))
        out[:, width:] = tail.astype(BF16)

    send_forward(0)
    for phase in range(phases):
        wait_all(recv.at[phase], phase)
        if phase + 1 < phases:
            send_forward(phase + 1)
        compute(phase)
        send_back(phase)

    wait_all(gathered, 2 * phases)
    total = gathered[0].astype(F32)
    for k in range(1, n_row):
        total = total + gathered[k].astype(F32)
    out_ref[...] = total.astype(BF16)

    for phase in range(phases):
        wait_all(back.at[phase], phases + phase)
        wait_sent(recv.at[phase], phase)
        wait_sent(back.at[phase], phases + phase)
    rest = pl.ds(0, n_row - 1)
    pltpu.make_async_copy(gathered.at[rest], gathered.at[rest], send_sem.at[2 * phases]).wait()


def exchange(p0, p1, weights, n_row):
    slots, full = p0.shape
    width = weights.shape[1]
    part = width // n_row
    held = slots // SPLITS
    back = jax.ShapeDtypeStruct((slots, width + PAD), BF16)
    share = (weights.shape[0], part, weights.shape[2])
    phases = MICRO * SPLITS
    vmem = pl.BlockSpec(memory_space=pltpu.VMEM)
    return pl.pallas_call(
        exchange_kernel,
        out_shape=(back, back, jax.ShapeDtypeStruct(share, BF16)),
        in_specs=[vmem] * 3,
        out_specs=(vmem, vmem, vmem),
        scratch_shapes=[
            pltpu.VMEM((phases, held, full), BF16),
            pltpu.VMEM((phases, held, width + PAD), BF16),
            pltpu.VMEM(weights.shape, F32),
            pltpu.VMEM(weights.shape, BF16),
            pltpu.VMEM((n_row,) + share, BF16),
            pltpu.SemaphoreType.DMA((2 * phases + 1,)),
            pltpu.SemaphoreType.DMA((2 * phases + 1,)),
        ],
        compiler_params=pltpu.CompilerParams(
            collective_id=0, has_side_effects=True, vmem_limit_bytes=62 * 1024 * 1024
        ),
    )(p0, p1, weights)


def on_device(tokens, cotangent, gates, expert_ids, expert_weights):
    n_expert = lax.axis_size("expert")
    expert_count = n_expert * expert_weights.shape[0]
    batch_rows = tokens.shape[0] // MICRO
    capacity = max(2, 4 * batch_rows // expert_count)
    width = tokens.shape[1]

    masks, gate_list, payloads = [], [], []
    for micro_index in range(MICRO):
        lower = micro_index * batch_rows
        upper = lower + batch_rows
        first, second = route_masks(expert_ids[lower:upper], expert_count, capacity)
        both = (first | second).astype(BF16)
        cot = cotangent[lower:upper].astype(F32)
        gate = gates[lower:upper].astype(F32)
        scaled_first = (gate[:, 0:1] * cot).astype(BF16)
        scaled_second = (gate[:, 1:2] * cot).astype(BF16)
        rows_in = mm(both, tokens[lower:upper]).astype(BF16)
        rows_scaled = (
            mm(first.astype(BF16), scaled_first) + mm(second.astype(BF16), scaled_second)
        ).astype(BF16)
        payloads.append(jnp.concatenate([rows_in, rows_scaled], axis=1))
        masks.append((first, second, both))
        gate_list.append(gate)

    ret0, ret1, weights_grad = exchange(
        payloads[0], payloads[1], expert_weights[0], lax.axis_size("dp")
    )

    token_parts, gate_parts = [], []
    for (first, second, both), gate, ret in zip(masks, gate_list, (ret0, ret1)):
        token_grad = lax.dot_general(
            both, ret[:, :width], CONTRACT_FIRST, preferred_element_type=F32
        ).astype(BF16)
        gate_sum = ret[:, width].astype(F32) + ret[:, width + 1].astype(F32)
        sum_first = jnp.sum(jnp.where(first, gate_sum[:, None], 0.0), axis=0)
        sum_second = jnp.sum(jnp.where(second, gate_sum[:, None], 0.0), axis=0)
        gate_grad = jnp.stack([sum_first / gate[:, 0], sum_second / gate[:, 1]], axis=1)
        token_parts.append(token_grad)
        gate_parts.append(gate_grad.astype(BF16))

    return (
        jnp.concatenate(token_parts, axis=0),
        jnp.concatenate(gate_parts, axis=0),
        weights_grad[None],
    )


def solution(mesh):
    placed = (
        P(("dp", "expert"), None),
        P(("dp", "expert"), None),
        P(("dp", "expert"), None),
        P(("dp", "expert"), None),
        P("expert", None, None, None),
    )
    return jax.shard_map(
        on_device,
        mesh=mesh,
        in_specs=placed,
        out_specs=(
            P(("dp", "expert"), None),
            P(("dp", "expert"), None),
            P("expert", None, "dp", None),
        ),
        check_vma=False,
    )
```

```python
import jax
import jax.numpy as jnp
from jax import lax
from jax.experimental import pallas as pl
from jax.experimental.pallas import tpu as pltpu
from jax.sharding import PartitionSpec as P

MICRO = 2
SPLITS = 1
PAD = 128

F32 = jnp.float32
BF16 = jnp.bfloat16

CONTRACT_LAST = (((1,), (1,)), ((), ()))
CONTRACT_FIRST = (((0,), (0,)), ((), ()))
MESH = pl.DeviceIdType.MESH


def mm(a, b):
    return jnp.dot(a, b, preferred_element_type=F32)


def route_masks(ids_block, expert_count, capacity):
    flat_ids = ids_block.reshape(-1)
    one_hot = (flat_ids[:, None] == jnp.arange(expert_count, dtype=jnp.int32)[None, :]).astype(
        jnp.int32
    )
    earlier = jnp.cumsum(one_hot, axis=0) - one_hot
    rank_slot = jnp.sum(earlier * one_hot, axis=1)
    route_slot = (flat_ids * capacity + rank_slot).reshape(-1, 2)
    position = jnp.arange(expert_count * capacity, dtype=jnp.int32)[:, None]
    return position == route_slot[None, :, 0], position == route_slot[None, :, 1]


def expert_step(recv, w_gate, w_up, w_down, width):
    rows_in = recv[:, :width]
    scaled = recv[:, width:]
    pre_gate = mm(rows_in, w_gate)
    pre_up = mm(rows_in, w_up)
    sigmoid_gate = jax.nn.sigmoid(pre_gate)
    activated = pre_gate * sigmoid_gate
    hidden = (activated * pre_up).astype(BF16)
    hidden_grad = mm(scaled, w_down)
    gate_sum = jnp.sum(hidden.astype(F32) * hidden_grad, axis=1)
    grad_pre_gate = (
        hidden_grad * pre_up * sigmoid_gate * (1.0 + pre_gate * (1.0 - sigmoid_gate))
    ).astype(BF16)
    grad_pre_up = (hidden_grad * activated).astype(BF16)
    input_grad = (
        lax.dot_general(grad_pre_gate, w_gate, CONTRACT_LAST, preferred_element_type=F32)
        + lax.dot_general(grad_pre_up, w_up, CONTRACT_LAST, preferred_element_type=F32)
    ).astype(BF16)
    grads = (
        lax.dot_general(rows_in, grad_pre_gate, CONTRACT_FIRST, preferred_element_type=F32),
        lax.dot_general(rows_in, grad_pre_up, CONTRACT_FIRST, preferred_element_type=F32),
        lax.dot_general(scaled, hidden, CONTRACT_FIRST, preferred_element_type=F32),
    )
    high = gate_sum.astype(BF16)
    low = (gate_sum - high.astype(F32)).astype(BF16)
    tail = jnp.concatenate(
        [high[:, None], low[:, None], jnp.zeros((recv.shape[0], PAD - 2), BF16)], axis=1
    )
    return jnp.concatenate([input_grad, tail], axis=1), grads


def exchange_kernel(p0_ref, p1_ref, w_ref, ret0_ref, ret1_ref, out_ref,
                    recv, back, grad_ref, rounded, gathered, send_sem, recv_sem):
    n = lax.axis_size("expert")
    me = lax.axis_index("expert")
    n_row = lax.axis_size("dp")
    row = lax.axis_index("dp")
    phases = recv.shape[0]
    splits = phases // MICRO
    capacity = p0_ref.shape[0] // n
    piece = capacity // splits
    width = w_ref.shape[1]
    part = out_ref.shape[1]
    payloads = (p0_ref, p1_ref)
    returns = (ret0_ref, ret1_ref)

    barrier = pltpu.get_barrier_semaphore()
    for k in range(1, n):
        peer = lax.rem(me + k, n)
        pl.semaphore_signal(barrier, inc=1, device_id=(row, peer), device_id_type=MESH)
    for k in range(1, n_row):
        peer = lax.rem(row + k, n_row)
        pl.semaphore_signal(barrier, inc=1, device_id=(peer, me), device_id_type=MESH)
    pl.semaphore_wait(barrier, n - 1 + n_row - 1)

    def slot_rows(expert, phase):
        start = expert * capacity + (phase % splits) * piece
        return pl.ds(pl.multiple_of(start, piece), piece)

    def held_rows(source):
        return pl.ds(pl.multiple_of(source * piece, piece), piece)

    def scatter(phase, src_rows, dst_rows, src, dst, sem):
        pltpu.make_async_copy(src.at[src_rows(me)], dst.at[dst_rows(me)], recv_sem.at[sem]).start()
        for k in range(1, n):
            peer = lax.rem(me + k, n)
            pltpu.make_async_remote_copy(
                src_ref=src.at[src_rows(peer)],
                dst_ref=dst.at[dst_rows(me)],
                send_sem=send_sem.at[sem],
                recv_sem=recv_sem.at[sem],
                device_id=(row, peer),
                device_id_type=MESH,
            ).start()

    def send_forward(phase):
        scatter(phase, lambda e: slot_rows(e, phase), held_rows,
                payloads[phase // splits], recv.at[phase], phase)

    def send_back(phase):
        scatter(phase, held_rows, lambda e: slot_rows(e, phase),
                back.at[phase], returns[phase // splits], phases + phase)

    def wait_all(buf, sem):
        pltpu.make_async_copy(buf, buf, recv_sem.at[sem]).wait()

    def wait_sent(buf, sem):
        rest = pl.ds(0, (n - 1) * piece)
        pltpu.make_async_copy(buf.at[rest], buf.at[rest], send_sem.at[sem]).wait()

    def scatter_grads():
        rounded[...] = grad_ref[...].astype(BF16)
        mine = pl.ds(pl.multiple_of(row * part, part), part)
        pltpu.make_async_copy(rounded.at[:, mine], gathered.at[row], recv_sem.at[2 * phases]).start()
        for k in range(1, n_row):
            peer = lax.rem(row + k, n_row)
            pltpu.make_async_remote_copy(
                src_ref=rounded.at[:, pl.ds(pl.multiple_of(peer * part, part), part)],
                dst_ref=gathered.at[row],
                send_sem=send_sem.at[2 * phases],
                recv_sem=recv_sem.at[2 * phases],
                device_id=(peer, me),
                device_id_type=MESH,
            ).start()

    def compute(phase):
        held = recv.at[phase]
        rows_in = held[:, :width]
        scaled = held[:, width:]
        w_gate = w_ref[0]
        w_up = w_ref[1]
        w_down = w_ref[2]
        pre_gate = mm(rows_in, w_gate)
        pre_up = mm(rows_in, w_up)
        sigmoid_gate = jax.nn.sigmoid(pre_gate)
        activated = pre_gate * sigmoid_gate
        hidden = (activated * pre_up).astype(BF16)
        hidden_grad = mm(scaled, w_down)
        gate_sum = jnp.sum(hidden.astype(F32) * hidden_grad, axis=1, keepdims=True)
        grad_pre_gate = (
            hidden_grad * pre_up * sigmoid_gate * (1.0 + pre_gate * (1.0 - sigmoid_gate))
        ).astype(BF16)
        grad_pre_up = (hidden_grad * activated).astype(BF16)
        grads = (
            lax.dot_general(rows_in, grad_pre_gate, CONTRACT_FIRST, preferred_element_type=F32),
            lax.dot_general(rows_in, grad_pre_up, CONTRACT_FIRST, preferred_element_type=F32),
            lax.dot_general(scaled, hidden, CONTRACT_FIRST, preferred_element_type=F32),
        )
        for index, value in enumerate(grads):
            if phase == 0:
                grad_ref[index] = value
            else:
                grad_ref[index] += value
        if phase == phases - 1:
            scatter_grads()
        input_grad = (
            lax.dot_general(grad_pre_gate, w_gate, CONTRACT_LAST, preferred_element_type=F32)
            + lax.dot_general(grad_pre_up, w_up, CONTRACT_LAST, preferred_element_type=F32)
        ).astype(BF16)
        out = back.at[phase]
        out[:, :width] = input_grad
        high = gate_sum.astype(BF16).astype(F32)
        low = gate_sum - high
        column = lax.broadcasted_iota(jnp.int32, (input_grad.shape[0], PAD), 1)
        tail = jnp.where(column == 0, high, jnp.where(column == 1, low, 0.0))
        out[:, width:] = tail.astype(BF16)

    send_forward(0)
    for phase in range(phases):
        wait_all(recv.at[phase], phase)
        if phase + 1 < phases:
            send_forward(phase + 1)
        compute(phase)
        send_back(phase)

    wait_all(gathered, 2 * phases)
    total = gathered[0].astype(F32)
    for k in range(1, n_row):
        total = total + gathered[k].astype(F32)
    out_ref[...] = total.astype(BF16)

    for phase in range(phases):
        wait_all(back.at[phase], phases + phase)
        wait_sent(recv.at[phase], phase)
        wait_sent(back.at[phase], phases + phase)
    rest = pl.ds(0, n_row - 1)
    pltpu.make_async_copy(gathered.at[rest], gathered.at[rest], send_sem.at[2 * phases]).wait()


def exchange(p0, p1, weights, n_row):
    slots, full = p0.shape
    width = weights.shape[1]
    part = width // n_row
    held = slots // SPLITS
    back = jax.ShapeDtypeStruct((slots, width + PAD), BF16)
    share = (weights.shape[0], part, weights.shape[2])
    phases = MICRO * SPLITS
    vmem = pl.BlockSpec(memory_space=pltpu.VMEM)
    return pl.pallas_call(
        exchange_kernel,
        out_shape=(back, back, jax.ShapeDtypeStruct(share, BF16)),
        in_specs=[vmem] * 3,
        out_specs=(vmem, vmem, vmem),
        scratch_shapes=[
            pltpu.VMEM((phases, held, full), BF16),
            pltpu.VMEM((phases, held, width + PAD), BF16),
            pltpu.VMEM(weights.shape, F32),
            pltpu.VMEM(weights.shape, BF16),
            pltpu.VMEM((n_row,) + share, BF16),
            pltpu.SemaphoreType.DMA((2 * phases + 1,)),
            pltpu.SemaphoreType.DMA((2 * phases + 1,)),
        ],
        compiler_params=pltpu.CompilerParams(
            collective_id=0, has_side_effects=True, vmem_limit_bytes=62 * 1024 * 1024
        ),
    )(p0, p1, weights)


def on_device(tokens, cotangent, gates, expert_ids, expert_weights):
    n_expert = lax.axis_size("expert")
    expert_count = n_expert * expert_weights.shape[0]
    batch_rows = tokens.shape[0] // MICRO
    capacity = max(2, 4 * batch_rows // expert_count)
    width = tokens.shape[1]

    masks, gate_list, payloads = [], [], []
    for micro_index in range(MICRO):
        lower = micro_index * batch_rows
        upper = lower + batch_rows
        first, second = route_masks(expert_ids[lower:upper], expert_count, capacity)
        both = (first | second).astype(BF16)
        cot = cotangent[lower:upper].astype(F32)
        gate = gates[lower:upper].astype(F32)
        scaled_first = (gate[:, 0:1] * cot).astype(BF16)
        scaled_second = (gate[:, 1:2] * cot).astype(BF16)
        rows_in = mm(both, tokens[lower:upper]).astype(BF16)
        rows_scaled = (
            mm(first.astype(BF16), scaled_first) + mm(second.astype(BF16), scaled_second)
        ).astype(BF16)
        payloads.append(jnp.concatenate([rows_in, rows_scaled], axis=1))
        masks.append((first, second, both))
        gate_list.append(gate)

    ret0, ret1, weights_grad = exchange(
        payloads[0], payloads[1], expert_weights[0], lax.axis_size("dp")
    )

    token_parts, gate_parts = [], []
    for (first, second, both), gate, ret in zip(masks, gate_list, (ret0, ret1)):
        token_grad = lax.dot_general(
            both, ret[:, :width], CONTRACT_FIRST, preferred_element_type=F32
        ).astype(BF16)
        gate_sum = ret[:, width].astype(F32) + ret[:, width + 1].astype(F32)
        sum_first = jnp.sum(jnp.where(first, gate_sum[:, None], 0.0), axis=0)
        sum_second = jnp.sum(jnp.where(second, gate_sum[:, None], 0.0), axis=0)
        gate_grad = jnp.stack([sum_first / gate[:, 0], sum_second / gate[:, 1]], axis=1)
        token_parts.append(token_grad)
        gate_parts.append(gate_grad.astype(BF16))

    return (
        jnp.concatenate(token_parts, axis=0),
        jnp.concatenate(gate_parts, axis=0),
        weights_grad[None],
    )


def solution(mesh):
    placed = (
        P(("dp", "expert"), None),
        P(("dp", "expert"), None),
        P(("dp", "expert"), None),
        P(("dp", "expert"), None),
        P("expert", None, None, None),
    )
    return jax.shard_map(
        on_device,
        mesh=mesh,
        in_specs=placed,
        out_specs=(
            P(("dp", "expert"), None),
            P(("dp", "expert"), None),
            P("expert", None, "dp", None),
        ),
        check_vma=False,
    )
```

```python
import jax
import jax.numpy as jnp
from jax import lax
from jax.experimental import pallas as pl
from jax.experimental.pallas import tpu as pltpu
from jax.sharding import PartitionSpec as P

MICRO = 2
SPLITS = 1
SIDE = 4
PAD = 128

F32 = jnp.float32
BF16 = jnp.bfloat16

CONTRACT_LAST = (((1,), (1,)), ((), ()))
CONTRACT_FIRST = (((0,), (0,)), ((), ()))
MESH = pl.DeviceIdType.MESH


def mm(a, b):
    return jnp.dot(a, b, preferred_element_type=F32)


def route_masks(ids_block, expert_count, capacity):
    flat_ids = ids_block.reshape(-1)
    one_hot = (flat_ids[:, None] == jnp.arange(expert_count, dtype=jnp.int32)[None, :]).astype(
        jnp.int32
    )
    earlier = jnp.cumsum(one_hot, axis=0) - one_hot
    rank_slot = jnp.sum(earlier * one_hot, axis=1)
    route_slot = (flat_ids * capacity + rank_slot).reshape(-1, 2)
    position = jnp.arange(expert_count * capacity, dtype=jnp.int32)[:, None]
    return position == route_slot[None, :, 0], position == route_slot[None, :, 1]


def expert_step(recv, w_gate, w_up, w_down, width):
    rows_in = recv[:, :width]
    scaled = recv[:, width:]
    pre_gate = mm(rows_in, w_gate)
    pre_up = mm(rows_in, w_up)
    sigmoid_gate = jax.nn.sigmoid(pre_gate)
    activated = pre_gate * sigmoid_gate
    hidden = (activated * pre_up).astype(BF16)
    hidden_grad = mm(scaled, w_down)
    gate_sum = jnp.sum(hidden.astype(F32) * hidden_grad, axis=1)
    grad_pre_gate = (
        hidden_grad * pre_up * sigmoid_gate * (1.0 + pre_gate * (1.0 - sigmoid_gate))
    ).astype(BF16)
    grad_pre_up = (hidden_grad * activated).astype(BF16)
    input_grad = (
        lax.dot_general(grad_pre_gate, w_gate, CONTRACT_LAST, preferred_element_type=F32)
        + lax.dot_general(grad_pre_up, w_up, CONTRACT_LAST, preferred_element_type=F32)
    ).astype(BF16)
    grads = (
        lax.dot_general(rows_in, grad_pre_gate, CONTRACT_FIRST, preferred_element_type=F32),
        lax.dot_general(rows_in, grad_pre_up, CONTRACT_FIRST, preferred_element_type=F32),
        lax.dot_general(scaled, hidden, CONTRACT_FIRST, preferred_element_type=F32),
    )
    high = gate_sum.astype(BF16)
    low = (gate_sum - high.astype(F32)).astype(BF16)
    tail = jnp.concatenate(
        [high[:, None], low[:, None], jnp.zeros((recv.shape[0], PAD - 2), BF16)], axis=1
    )
    return jnp.concatenate([input_grad, tail], axis=1), grads


def exchange_kernel(p0_ref, p1_ref, w_ref, ret0_ref, ret1_ref, out_ref,
                    recv, back, grad_ref, round_a, round_b, first_a, first_b,
                    part_a, part_b, second_a, second_b, send_sem, recv_sem, rs_send, rs_recv):
    n = lax.axis_size("expert")
    me = lax.axis_index("expert")
    n_row = lax.axis_size("dp")
    row = lax.axis_index("dp")
    phases = recv.shape[0]
    splits = phases // MICRO
    capacity = p0_ref.shape[0] // n
    piece = capacity // splits
    width = w_ref.shape[1]
    part = out_ref.shape[1]
    payloads = (p0_ref, p1_ref)
    returns = (ret0_ref, ret1_ref)

    barrier = pltpu.get_barrier_semaphore()
    for k in range(1, n):
        peer = lax.rem(me + k, n)
        pl.semaphore_signal(barrier, inc=1, device_id=(row, peer), device_id_type=MESH)
    for k in range(1, n_row):
        peer = lax.rem(row + k, n_row)
        pl.semaphore_signal(barrier, inc=1, device_id=(peer, me), device_id_type=MESH)
    pl.semaphore_wait(barrier, n - 1 + n_row - 1)

    def slot_rows(expert, phase):
        start = expert * capacity + (phase % splits) * piece
        return pl.ds(pl.multiple_of(start, piece), piece)

    def held_rows(source):
        return pl.ds(pl.multiple_of(source * piece, piece), piece)

    def scatter(phase, src_rows, dst_rows, src, dst, sem):
        pltpu.make_async_copy(src.at[src_rows(me)], dst.at[dst_rows(me)], recv_sem.at[sem]).start()
        for k in range(1, n):
            peer = lax.rem(me + k, n)
            pltpu.make_async_remote_copy(
                src_ref=src.at[src_rows(peer)],
                dst_ref=dst.at[dst_rows(me)],
                send_sem=send_sem.at[sem],
                recv_sem=recv_sem.at[sem],
                device_id=(row, peer),
                device_id_type=MESH,
            ).start()

    def send_forward(phase):
        scatter(phase, lambda e: slot_rows(e, phase), held_rows,
                payloads[phase // splits], recv.at[phase], phase)

    def send_back(phase):
        scatter(phase, held_rows, lambda e: slot_rows(e, phase),
                back.at[phase], returns[phase // splits], phases + phase)

    def wait_all(buf, sem):
        pltpu.make_async_copy(buf, buf, recv_sem.at[sem]).wait()

    def wait_sent(buf, sem):
        rest = pl.ds(0, (n - 1) * piece)
        pltpu.make_async_copy(buf.at[rest], buf.at[rest], send_sem.at[sem]).wait()

    side = SIDE
    col_a, col_b = row % side, row // side
    half = out_ref.shape[2] // 2

    def x_peer(k):
        return col_b * side + lax.rem(col_a + k, side)

    def y_peer(k):
        return lax.rem(col_b + k, side) * side + col_a

    def spread(src, dst, index, peer_of, sem):
        pltpu.make_async_copy(src.at[index], dst.at[index], rs_recv.at[sem]).start()
        for k in range(1, side):
            pltpu.make_async_remote_copy(
                src_ref=src.at[lax.rem(index + k, side)],
                dst_ref=dst.at[index],
                send_sem=rs_send.at[sem],
                recv_sem=rs_recv.at[sem],
                device_id=(peer_of(k), me),
                device_id_type=MESH,
            ).start()

    def scatter_grads():
        for block in range(n_row):
            rounded = grad_ref[:, block * part:(block + 1) * part, :].astype(BF16)
            round_a[block % side, block // side] = rounded[:, :, :half]
            round_b[block // side, block % side] = rounded[:, :, half:]
        spread(round_a, first_a, col_a, x_peer, 0)
        spread(round_b, first_b, col_b, y_peer, 1)

    def reduce_grads():
        pltpu.make_async_copy(first_a, first_a, rs_recv.at[0]).wait()
        total = first_a[0].astype(F32)
        for k in range(1, side):
            total = total + first_a[k].astype(F32)
        part_a[...] = total
        spread(part_a, second_a, col_b, y_peer, 2)
        pltpu.make_async_copy(first_b, first_b, rs_recv.at[1]).wait()
        total = first_b[0].astype(F32)
        for k in range(1, side):
            total = total + first_b[k].astype(F32)
        part_b[...] = total
        spread(part_b, second_b, col_a, x_peer, 3)
        for second, columns, sem in ((second_a, slice(0, half), 2),
                                     (second_b, slice(half, 2 * half), 3)):
            pltpu.make_async_copy(second, second, rs_recv.at[sem]).wait()
            total = second[0]
            for k in range(1, side):
                total = total + second[k]
            out_ref[:, :, columns] = total.astype(BF16)

    def compute(phase):
        held = recv.at[phase]
        rows_in = held[:, :width]
        scaled = held[:, width:]
        w_gate = w_ref[0]
        w_up = w_ref[1]
        w_down = w_ref[2]
        pre_gate = mm(rows_in, w_gate)
        pre_up = mm(rows_in, w_up)
        sigmoid_gate = jax.nn.sigmoid(pre_gate)
        activated = pre_gate * sigmoid_gate
        hidden = (activated * pre_up).astype(BF16)
        hidden_grad = mm(scaled, w_down)
        gate_sum = jnp.sum(hidden.astype(F32) * hidden_grad, axis=1, keepdims=True)
        grad_pre_gate = (
            hidden_grad * pre_up * sigmoid_gate * (1.0 + pre_gate * (1.0 - sigmoid_gate))
        ).astype(BF16)
        grad_pre_up = (hidden_grad * activated).astype(BF16)
        grads = (
            lax.dot_general(rows_in, grad_pre_gate, CONTRACT_FIRST, preferred_element_type=F32),
            lax.dot_general(rows_in, grad_pre_up, CONTRACT_FIRST, preferred_element_type=F32),
            lax.dot_general(scaled, hidden, CONTRACT_FIRST, preferred_element_type=F32),
        )
        for index, value in enumerate(grads):
            if phase == 0:
                grad_ref[index] = value
            else:
                grad_ref[index] += value
        if phase == phases - 1:
            scatter_grads()
        input_grad = (
            lax.dot_general(grad_pre_gate, w_gate, CONTRACT_LAST, preferred_element_type=F32)
            + lax.dot_general(grad_pre_up, w_up, CONTRACT_LAST, preferred_element_type=F32)
        ).astype(BF16)
        out = back.at[phase]
        out[:, :width] = input_grad
        high = gate_sum.astype(BF16).astype(F32)
        low = gate_sum - high
        column = lax.broadcasted_iota(jnp.int32, (input_grad.shape[0], PAD), 1)
        tail = jnp.where(column == 0, high, jnp.where(column == 1, low, 0.0))
        out[:, width:] = tail.astype(BF16)

    send_forward(0)
    for phase in range(phases):
        wait_all(recv.at[phase], phase)
        if phase + 1 < phases:
            send_forward(phase + 1)
        compute(phase)
        send_back(phase)

    reduce_grads()

    for phase in range(phases):
        wait_all(back.at[phase], phases + phase)
        wait_sent(recv.at[phase], phase)
        wait_sent(back.at[phase], phases + phase)
    rest = pl.ds(0, side - 1)
    for sem, buf in enumerate((first_a, first_b, second_a, second_b)):
        pltpu.make_async_copy(buf.at[rest], buf.at[rest], rs_send.at[sem]).wait()


def exchange(p0, p1, weights, n_row):
    slots, full = p0.shape
    width = weights.shape[1]
    part = width // n_row
    held = slots // SPLITS
    back = jax.ShapeDtypeStruct((slots, width + PAD), BF16)
    share = (weights.shape[0], part, weights.shape[2])
    quarter = (weights.shape[0], part, weights.shape[2] // 2)
    phases = MICRO * SPLITS
    vmem = pl.BlockSpec(memory_space=pltpu.VMEM)
    return pl.pallas_call(
        exchange_kernel,
        out_shape=(back, back, jax.ShapeDtypeStruct(share, BF16)),
        in_specs=[vmem] * 3,
        out_specs=(vmem, vmem, vmem),
        scratch_shapes=[
            pltpu.VMEM((phases, held, full), BF16),
            pltpu.VMEM((phases, held, width + PAD), BF16),
            pltpu.VMEM(weights.shape, F32),
            pltpu.VMEM((SIDE, SIDE) + quarter, BF16),
            pltpu.VMEM((SIDE, SIDE) + quarter, BF16),
            pltpu.VMEM((SIDE, SIDE) + quarter, BF16),
            pltpu.VMEM((SIDE, SIDE) + quarter, BF16),
            pltpu.VMEM((SIDE,) + quarter, F32),
            pltpu.VMEM((SIDE,) + quarter, F32),
            pltpu.VMEM((SIDE,) + quarter, F32),
            pltpu.VMEM((SIDE,) + quarter, F32),
            pltpu.SemaphoreType.DMA((2 * phases,)),
            pltpu.SemaphoreType.DMA((2 * phases,)),
            pltpu.SemaphoreType.DMA((4,)),
            pltpu.SemaphoreType.DMA((4,)),
        ],
        compiler_params=pltpu.CompilerParams(
            collective_id=0, has_side_effects=True, vmem_limit_bytes=62 * 1024 * 1024
        ),
    )(p0, p1, weights)


def on_device(tokens, cotangent, gates, expert_ids, expert_weights):
    n_expert = lax.axis_size("expert")
    expert_count = n_expert * expert_weights.shape[0]
    batch_rows = tokens.shape[0] // MICRO
    capacity = max(2, 4 * batch_rows // expert_count)
    width = tokens.shape[1]

    masks, gate_list, payloads = [], [], []
    for micro_index in range(MICRO):
        lower = micro_index * batch_rows
        upper = lower + batch_rows
        first, second = route_masks(expert_ids[lower:upper], expert_count, capacity)
        both = (first | second).astype(BF16)
        cot = cotangent[lower:upper].astype(F32)
        gate = gates[lower:upper].astype(F32)
        scaled_first = (gate[:, 0:1] * cot).astype(BF16)
        scaled_second = (gate[:, 1:2] * cot).astype(BF16)
        rows_in = mm(both, tokens[lower:upper]).astype(BF16)
        rows_scaled = (
            mm(first.astype(BF16), scaled_first) + mm(second.astype(BF16), scaled_second)
        ).astype(BF16)
        payloads.append(jnp.concatenate([rows_in, rows_scaled], axis=1))
        masks.append((first, second, both))
        gate_list.append(gate)

    ret0, ret1, weights_grad = exchange(
        payloads[0], payloads[1], expert_weights[0], lax.axis_size("dp")
    )

    token_parts, gate_parts = [], []
    for (first, second, both), gate, ret in zip(masks, gate_list, (ret0, ret1)):
        token_grad = lax.dot_general(
            both, ret[:, :width], CONTRACT_FIRST, preferred_element_type=F32
        ).astype(BF16)
        gate_sum = ret[:, width].astype(F32) + ret[:, width + 1].astype(F32)
        sum_first = jnp.sum(jnp.where(first, gate_sum[:, None], 0.0), axis=0)
        sum_second = jnp.sum(jnp.where(second, gate_sum[:, None], 0.0), axis=0)
        gate_grad = jnp.stack([sum_first / gate[:, 0], sum_second / gate[:, 1]], axis=1)
        token_parts.append(token_grad)
        gate_parts.append(gate_grad.astype(BF16))

    return (
        jnp.concatenate(token_parts, axis=0),
        jnp.concatenate(gate_parts, axis=0),
        weights_grad[None],
    )


def solution(mesh):
    placed = (
        P(("dp", "expert"), None),
        P(("dp", "expert"), None),
        P(("dp", "expert"), None),
        P(("dp", "expert"), None),
        P("expert", None, None, None),
    )
    return jax.shard_map(
        on_device,
        mesh=mesh,
        in_specs=placed,
        out_specs=(
            P(("dp", "expert"), None),
            P(("dp", "expert"), None),
            P("expert", None, "dp", None),
        ),
        check_vma=False,
    )
```

```python
import jax
import jax.numpy as jnp
from jax import lax
from jax.experimental import pallas as pl
from jax.experimental.pallas import tpu as pltpu
from jax.sharding import PartitionSpec as P

MICRO = 2
SPLITS = 1
SIDE = 4
PAD = 128

F32 = jnp.float32
BF16 = jnp.bfloat16

CONTRACT_LAST = (((1,), (1,)), ((), ()))
CONTRACT_FIRST = (((0,), (0,)), ((), ()))
MESH = pl.DeviceIdType.MESH


def mm(a, b):
    return jnp.dot(a, b, preferred_element_type=F32)


def route_masks(ids_block, expert_count, capacity):
    flat_ids = ids_block.reshape(-1)
    one_hot = (flat_ids[:, None] == jnp.arange(expert_count, dtype=jnp.int32)[None, :]).astype(
        jnp.int32
    )
    earlier = jnp.cumsum(one_hot, axis=0) - one_hot
    rank_slot = jnp.sum(earlier * one_hot, axis=1)
    route_slot = (flat_ids * capacity + rank_slot).reshape(-1, 2)
    position = jnp.arange(expert_count * capacity, dtype=jnp.int32)[:, None]
    return position == route_slot[None, :, 0], position == route_slot[None, :, 1]


def expert_step(recv, w_gate, w_up, w_down, width):
    rows_in = recv[:, :width]
    scaled = recv[:, width:]
    pre_gate = mm(rows_in, w_gate)
    pre_up = mm(rows_in, w_up)
    sigmoid_gate = jax.nn.sigmoid(pre_gate)
    activated = pre_gate * sigmoid_gate
    hidden = (activated * pre_up).astype(BF16)
    hidden_grad = mm(scaled, w_down)
    gate_sum = jnp.sum(hidden.astype(F32) * hidden_grad, axis=1)
    grad_pre_gate = (
        hidden_grad * pre_up * sigmoid_gate * (1.0 + pre_gate * (1.0 - sigmoid_gate))
    ).astype(BF16)
    grad_pre_up = (hidden_grad * activated).astype(BF16)
    input_grad = (
        lax.dot_general(grad_pre_gate, w_gate, CONTRACT_LAST, preferred_element_type=F32)
        + lax.dot_general(grad_pre_up, w_up, CONTRACT_LAST, preferred_element_type=F32)
    ).astype(BF16)
    grads = (
        lax.dot_general(rows_in, grad_pre_gate, CONTRACT_FIRST, preferred_element_type=F32),
        lax.dot_general(rows_in, grad_pre_up, CONTRACT_FIRST, preferred_element_type=F32),
        lax.dot_general(scaled, hidden, CONTRACT_FIRST, preferred_element_type=F32),
    )
    high = gate_sum.astype(BF16)
    low = (gate_sum - high.astype(F32)).astype(BF16)
    tail = jnp.concatenate(
        [high[:, None], low[:, None], jnp.zeros((recv.shape[0], PAD - 2), BF16)], axis=1
    )
    return jnp.concatenate([input_grad, tail], axis=1), grads


def exchange_kernel(x0_ref, q0_ref, x1_ref, q1_ref, w_ref, ret0_ref, ret1_ref, out_ref,
                    recv, back, grad_ref, round_a, round_b, first_a, first_b,
                    part_a, part_b, second_a, second_b, send_sem, recv_sem, rs_send, rs_recv):
    n = lax.axis_size("expert")
    me = lax.axis_index("expert")
    n_row = lax.axis_size("dp")
    row = lax.axis_index("dp")
    phases = recv.shape[0]
    splits = phases // MICRO
    capacity = x0_ref.shape[0] // n
    piece = capacity // splits
    width = w_ref.shape[1]
    part = out_ref.shape[1]
    payloads = ((x0_ref, q0_ref), (x1_ref, q1_ref))
    returns = (ret0_ref, ret1_ref)

    barrier = pltpu.get_barrier_semaphore()
    for k in range(1, n):
        peer = lax.rem(me + k, n)
        pl.semaphore_signal(barrier, inc=1, device_id=(row, peer), device_id_type=MESH)
    for k in range(1, n_row):
        peer = lax.rem(row + k, n_row)
        pl.semaphore_signal(barrier, inc=1, device_id=(peer, me), device_id_type=MESH)
    pl.semaphore_wait(barrier, n - 1 + n_row - 1)

    def slot_rows(expert, phase):
        start = expert * capacity + (phase % splits) * piece
        return pl.ds(pl.multiple_of(start, piece), piece)

    def held_rows(source):
        return pl.ds(pl.multiple_of(source * piece, piece), piece)

    def scatter(phase, src_rows, dst_rows, src, dst, sem):
        pltpu.make_async_copy(src.at[src_rows(me)], dst.at[dst_rows(me)], recv_sem.at[sem]).start()
        for k in range(1, n):
            peer = lax.rem(me + k, n)
            pltpu.make_async_remote_copy(
                src_ref=src.at[src_rows(peer)],
                dst_ref=dst.at[dst_rows(me)],
                send_sem=send_sem.at[sem],
                recv_sem=recv_sem.at[sem],
                device_id=(row, peer),
                device_id_type=MESH,
            ).start()

    def send_forward(phase):
        for index, src in enumerate(payloads[phase // splits]):
            columns = pl.ds(index * width, width)
            scatter(phase, lambda e: slot_rows(e, phase), held_rows,
                    src, recv.at[phase, :, columns], phase)

    def send_back(phase):
        scatter(phase, held_rows, lambda e: slot_rows(e, phase),
                back.at[phase], returns[phase // splits], phases + phase)

    def wait_all(buf, sem):
        pltpu.make_async_copy(buf, buf, recv_sem.at[sem]).wait()

    def wait_sent(buf, sem):
        rest = pl.ds(0, (n - 1) * piece)
        pltpu.make_async_copy(buf.at[rest], buf.at[rest], send_sem.at[sem]).wait()

    side = SIDE
    col_a, col_b = row % side, row // side
    half = out_ref.shape[2] // 2

    def x_peer(k):
        return col_b * side + lax.rem(col_a + k, side)

    def y_peer(k):
        return lax.rem(col_b + k, side) * side + col_a

    def spread(src, dst, index, peer_of, sem):
        pltpu.make_async_copy(src.at[index], dst.at[index], rs_recv.at[sem]).start()
        for k in range(1, side):
            pltpu.make_async_remote_copy(
                src_ref=src.at[lax.rem(index + k, side)],
                dst_ref=dst.at[index],
                send_sem=rs_send.at[sem],
                recv_sem=rs_recv.at[sem],
                device_id=(peer_of(k), me),
                device_id_type=MESH,
            ).start()

    def scatter_grads():
        for block in range(n_row):
            rounded = grad_ref[:, block * part:(block + 1) * part, :].astype(BF16)
            round_a[block % side, block // side] = rounded[:, :, :half]
            round_b[block // side, block % side] = rounded[:, :, half:]
        spread(round_a, first_a, col_a, x_peer, 0)
        spread(round_b, first_b, col_b, y_peer, 1)

    def reduce_grads():
        pltpu.make_async_copy(first_a, first_a, rs_recv.at[0]).wait()
        total = first_a[0].astype(F32)
        for k in range(1, side):
            total = total + first_a[k].astype(F32)
        part_a[...] = total
        spread(part_a, second_a, col_b, y_peer, 2)
        pltpu.make_async_copy(first_b, first_b, rs_recv.at[1]).wait()
        total = first_b[0].astype(F32)
        for k in range(1, side):
            total = total + first_b[k].astype(F32)
        part_b[...] = total
        spread(part_b, second_b, col_a, x_peer, 3)
        for second, columns, sem in ((second_a, slice(0, half), 2),
                                     (second_b, slice(half, 2 * half), 3)):
            pltpu.make_async_copy(second, second, rs_recv.at[sem]).wait()
            total = second[0]
            for k in range(1, side):
                total = total + second[k]
            out_ref[:, :, columns] = total.astype(BF16)

    def compute(phase):
        held = recv.at[phase]
        rows_in = held[:, :width]
        scaled = held[:, width:]
        w_gate = w_ref[0]
        w_up = w_ref[1]
        w_down = w_ref[2]
        pre_gate = mm(rows_in, w_gate)
        pre_up = mm(rows_in, w_up)
        sigmoid_gate = jax.nn.sigmoid(pre_gate)
        activated = pre_gate * sigmoid_gate
        hidden = (activated * pre_up).astype(BF16)
        hidden_grad = mm(scaled, w_down)
        gate_sum = jnp.sum(hidden.astype(F32) * hidden_grad, axis=1, keepdims=True)
        grad_pre_gate = (
            hidden_grad * pre_up * sigmoid_gate * (1.0 + pre_gate * (1.0 - sigmoid_gate))
        ).astype(BF16)
        grad_pre_up = (hidden_grad * activated).astype(BF16)
        grads = (
            lax.dot_general(rows_in, grad_pre_gate, CONTRACT_FIRST, preferred_element_type=F32),
            lax.dot_general(rows_in, grad_pre_up, CONTRACT_FIRST, preferred_element_type=F32),
            lax.dot_general(scaled, hidden, CONTRACT_FIRST, preferred_element_type=F32),
        )
        for index, value in enumerate(grads):
            if phase == 0:
                grad_ref[index] = value
            else:
                grad_ref[index] += value
        if phase == phases - 1:
            scatter_grads()
        input_grad = (
            lax.dot_general(grad_pre_gate, w_gate, CONTRACT_LAST, preferred_element_type=F32)
            + lax.dot_general(grad_pre_up, w_up, CONTRACT_LAST, preferred_element_type=F32)
        ).astype(BF16)
        out = back.at[phase]
        out[:, :width] = input_grad
        high = gate_sum.astype(BF16).astype(F32)
        low = gate_sum - high
        column = lax.broadcasted_iota(jnp.int32, (input_grad.shape[0], PAD), 1)
        tail = jnp.where(column == 0, high, jnp.where(column == 1, low, 0.0))
        out[:, width:] = tail.astype(BF16)

    send_forward(0)
    for phase in range(phases):
        wait_all(recv.at[phase], phase)
        if phase + 1 < phases:
            send_forward(phase + 1)
        compute(phase)
        send_back(phase)

    reduce_grads()

    for phase in range(phases):
        wait_all(back.at[phase], phases + phase)
        wait_sent(recv.at[phase], phase)
        wait_sent(back.at[phase], phases + phase)
    rest = pl.ds(0, side - 1)
    for sem, buf in enumerate((first_a, first_b, second_a, second_b)):
        pltpu.make_async_copy(buf.at[rest], buf.at[rest], rs_send.at[sem]).wait()


def exchange(x0, q0, x1, q1, weights, n_row):
    slots, full = x0.shape[0], 2 * x0.shape[1]
    width = weights.shape[1]
    part = width // n_row
    held = slots // SPLITS
    back = jax.ShapeDtypeStruct((slots, width + PAD), BF16)
    share = (weights.shape[0], part, weights.shape[2])
    quarter = (weights.shape[0], part, weights.shape[2] // 2)
    phases = MICRO * SPLITS
    vmem = pl.BlockSpec(memory_space=pltpu.VMEM)
    return pl.pallas_call(
        exchange_kernel,
        out_shape=(back, back, jax.ShapeDtypeStruct(share, BF16)),
        in_specs=[vmem] * 5,
        out_specs=(vmem, vmem, vmem),
        scratch_shapes=[
            pltpu.VMEM((phases, held, full), BF16),
            pltpu.VMEM((phases, held, width + PAD), BF16),
            pltpu.VMEM(weights.shape, F32),
            pltpu.VMEM((SIDE, SIDE) + quarter, BF16),
            pltpu.VMEM((SIDE, SIDE) + quarter, BF16),
            pltpu.VMEM((SIDE, SIDE) + quarter, BF16),
            pltpu.VMEM((SIDE, SIDE) + quarter, BF16),
            pltpu.VMEM((SIDE,) + quarter, F32),
            pltpu.VMEM((SIDE,) + quarter, F32),
            pltpu.VMEM((SIDE,) + quarter, F32),
            pltpu.VMEM((SIDE,) + quarter, F32),
            pltpu.SemaphoreType.DMA((2 * phases,)),
            pltpu.SemaphoreType.DMA((2 * phases,)),
            pltpu.SemaphoreType.DMA((4,)),
            pltpu.SemaphoreType.DMA((4,)),
        ],
        compiler_params=pltpu.CompilerParams(
            collective_id=0, has_side_effects=True, vmem_limit_bytes=62 * 1024 * 1024
        ),
    )(x0, q0, x1, q1, weights)


def on_device(tokens, cotangent, gates, expert_ids, expert_weights):
    n_expert = lax.axis_size("expert")
    expert_count = n_expert * expert_weights.shape[0]
    batch_rows = tokens.shape[0] // MICRO
    capacity = max(2, 4 * batch_rows // expert_count)
    width = tokens.shape[1]

    masks, gate_list, payloads = [], [], []
    for micro_index in range(MICRO):
        lower = micro_index * batch_rows
        upper = lower + batch_rows
        first, second = route_masks(expert_ids[lower:upper], expert_count, capacity)
        both = (first | second).astype(BF16)
        cot = cotangent[lower:upper].astype(F32)
        gate = gates[lower:upper].astype(F32)
        scaled_first = (gate[:, 0:1] * cot).astype(BF16)
        scaled_second = (gate[:, 1:2] * cot).astype(BF16)
        rows_in = mm(both, tokens[lower:upper]).astype(BF16)
        rows_scaled = (
            mm(first.astype(BF16), scaled_first) + mm(second.astype(BF16), scaled_second)
        ).astype(BF16)
        payloads += [rows_in, rows_scaled]
        masks.append((first, second, both))
        gate_list.append(gate)

    ret0, ret1, weights_grad = exchange(*payloads, expert_weights[0], lax.axis_size("dp"))

    token_parts, gate_parts = [], []
    for (first, second, both), gate, ret in zip(masks, gate_list, (ret0, ret1)):
        token_grad = lax.dot_general(
            both, ret[:, :width], CONTRACT_FIRST, preferred_element_type=F32
        ).astype(BF16)
        gate_sum = ret[:, width].astype(F32) + ret[:, width + 1].astype(F32)
        sum_first = jnp.sum(jnp.where(first, gate_sum[:, None], 0.0), axis=0)
        sum_second = jnp.sum(jnp.where(second, gate_sum[:, None], 0.0), axis=0)
        gate_grad = jnp.stack([sum_first / gate[:, 0], sum_second / gate[:, 1]], axis=1)
        token_parts.append(token_grad)
        gate_parts.append(gate_grad.astype(BF16))

    return (
        jnp.concatenate(token_parts, axis=0),
        jnp.concatenate(gate_parts, axis=0),
        weights_grad[None],
    )


def solution(mesh):
    placed = (
        P(("dp", "expert"), None),
        P(("dp", "expert"), None),
        P(("dp", "expert"), None),
        P(("dp", "expert"), None),
        P("expert", None, None, None),
    )
    return jax.shard_map(
        on_device,
        mesh=mesh,
        in_specs=placed,
        out_specs=(
            P(("dp", "expert"), None),
            P(("dp", "expert"), None),
            P("expert", None, "dp", None),
        ),
        check_vma=False,
    )
```

```python
import jax
import jax.numpy as jnp
from jax import lax
from jax.experimental import pallas as pl
from jax.experimental.pallas import tpu as pltpu
from jax.sharding import PartitionSpec as P

MICRO = 2
SPLITS = 1
SIDE = 4
PAD = 128

F32 = jnp.float32
BF16 = jnp.bfloat16

CONTRACT_LAST = (((1,), (1,)), ((), ()))
CONTRACT_FIRST = (((0,), (0,)), ((), ()))
MESH = pl.DeviceIdType.MESH


def mm(a, b):
    return jnp.dot(a, b, preferred_element_type=F32)


def route_masks(ids_block, expert_count, capacity):
    flat_ids = ids_block.reshape(-1)
    one_hot = (flat_ids[:, None] == jnp.arange(expert_count, dtype=jnp.int32)[None, :]).astype(
        jnp.int32
    )
    earlier = jnp.cumsum(one_hot, axis=0) - one_hot
    rank_slot = jnp.sum(earlier * one_hot, axis=1)
    route_slot = (flat_ids * capacity + rank_slot).reshape(-1, 2)
    position = jnp.arange(expert_count * capacity, dtype=jnp.int32)[:, None]
    return position == route_slot[None, :, 0], position == route_slot[None, :, 1]


def expert_step(recv, w_gate, w_up, w_down, width):
    rows_in = recv[:, :width]
    scaled = recv[:, width:]
    pre_gate = mm(rows_in, w_gate)
    pre_up = mm(rows_in, w_up)
    sigmoid_gate = jax.nn.sigmoid(pre_gate)
    activated = pre_gate * sigmoid_gate
    hidden = (activated * pre_up).astype(BF16)
    hidden_grad = mm(scaled, w_down)
    gate_sum = jnp.sum(hidden.astype(F32) * hidden_grad, axis=1)
    grad_pre_gate = (
        hidden_grad * pre_up * sigmoid_gate * (1.0 + pre_gate * (1.0 - sigmoid_gate))
    ).astype(BF16)
    grad_pre_up = (hidden_grad * activated).astype(BF16)
    input_grad = (
        lax.dot_general(grad_pre_gate, w_gate, CONTRACT_LAST, preferred_element_type=F32)
        + lax.dot_general(grad_pre_up, w_up, CONTRACT_LAST, preferred_element_type=F32)
    ).astype(BF16)
    grads = (
        lax.dot_general(rows_in, grad_pre_gate, CONTRACT_FIRST, preferred_element_type=F32),
        lax.dot_general(rows_in, grad_pre_up, CONTRACT_FIRST, preferred_element_type=F32),
        lax.dot_general(scaled, hidden, CONTRACT_FIRST, preferred_element_type=F32),
    )
    high = gate_sum.astype(BF16)
    low = (gate_sum - high.astype(F32)).astype(BF16)
    tail = jnp.concatenate(
        [high[:, None], low[:, None], jnp.zeros((recv.shape[0], PAD - 2), BF16)], axis=1
    )
    return jnp.concatenate([input_grad, tail], axis=1), grads


def exchange_kernel(p0_ref, both1_ref, first1_ref, second1_ref, x1_ref, qa1_ref, qb1_ref,
                    both0_ref, first0_ref, second0_ref, w_ref,
                    ret1_ref, out_ref, tg0_ref, gs0_ref,
                    p1, ret0, recv, back, grad_ref, round_a, round_b, first_a, first_b,
                    part_a, part_b, second_a, second_b, send_sem, recv_sem, rs_send, rs_recv):
    n = lax.axis_size("expert")
    me = lax.axis_index("expert")
    n_row = lax.axis_size("dp")
    row = lax.axis_index("dp")
    phases = recv.shape[0]
    splits = phases // MICRO
    capacity = p0_ref.shape[0] // n
    piece = capacity // splits
    width = w_ref.shape[1]
    part = out_ref.shape[1]
    payloads = (p0_ref, p1)
    returns = (ret0, ret1_ref)

    barrier = pltpu.get_barrier_semaphore()
    for k in range(1, n):
        peer = lax.rem(me + k, n)
        pl.semaphore_signal(barrier, inc=1, device_id=(row, peer), device_id_type=MESH)
    for k in range(1, n_row):
        peer = lax.rem(row + k, n_row)
        pl.semaphore_signal(barrier, inc=1, device_id=(peer, me), device_id_type=MESH)
    pl.semaphore_wait(barrier, n - 1 + n_row - 1)

    def slot_rows(expert, phase):
        start = expert * capacity + (phase % splits) * piece
        return pl.ds(pl.multiple_of(start, piece), piece)

    def held_rows(source):
        return pl.ds(pl.multiple_of(source * piece, piece), piece)

    def scatter(phase, src_rows, dst_rows, src, dst, sem):
        pltpu.make_async_copy(src.at[src_rows(me)], dst.at[dst_rows(me)], recv_sem.at[sem]).start()
        for k in range(1, n):
            peer = lax.rem(me + k, n)
            pltpu.make_async_remote_copy(
                src_ref=src.at[src_rows(peer)],
                dst_ref=dst.at[dst_rows(me)],
                send_sem=send_sem.at[sem],
                recv_sem=recv_sem.at[sem],
                device_id=(row, peer),
                device_id_type=MESH,
            ).start()

    def send_forward(phase):
        scatter(phase, lambda e: slot_rows(e, phase), held_rows,
                payloads[phase // splits], recv.at[phase], phase)

    def send_back(phase):
        scatter(phase, held_rows, lambda e: slot_rows(e, phase),
                back.at[phase], returns[phase // splits], phases + phase)

    def wait_all(buf, sem):
        pltpu.make_async_copy(buf, buf, recv_sem.at[sem]).wait()

    def wait_sent(buf, sem):
        rest = pl.ds(0, (n - 1) * piece)
        pltpu.make_async_copy(buf.at[rest], buf.at[rest], send_sem.at[sem]).wait()

    side = SIDE
    col_a, col_b = row % side, row // side
    half = out_ref.shape[2] // 2

    def x_peer(k):
        return col_b * side + lax.rem(col_a + k, side)

    def y_peer(k):
        return lax.rem(col_b + k, side) * side + col_a

    def spread(src, dst, index, peer_of, sem):
        pltpu.make_async_copy(src.at[index], dst.at[index], rs_recv.at[sem]).start()
        for k in range(1, side):
            pltpu.make_async_remote_copy(
                src_ref=src.at[lax.rem(index + k, side)],
                dst_ref=dst.at[index],
                send_sem=rs_send.at[sem],
                recv_sem=rs_recv.at[sem],
                device_id=(peer_of(k), me),
                device_id_type=MESH,
            ).start()

    def scatter_grads():
        for block in range(n_row):
            rounded = grad_ref[:, block * part:(block + 1) * part, :].astype(BF16)
            round_a[block % side, block // side] = rounded[:, :, :half]
            round_b[block // side, block % side] = rounded[:, :, half:]
        spread(round_a, first_a, col_a, x_peer, 0)
        spread(round_b, first_b, col_b, y_peer, 1)

    def reduce_grads():
        pltpu.make_async_copy(first_a, first_a, rs_recv.at[0]).wait()
        total = first_a[0].astype(F32)
        for k in range(1, side):
            total = total + first_a[k].astype(F32)
        part_a[...] = total
        spread(part_a, second_a, col_b, y_peer, 2)
        pltpu.make_async_copy(first_b, first_b, rs_recv.at[1]).wait()
        total = first_b[0].astype(F32)
        for k in range(1, side):
            total = total + first_b[k].astype(F32)
        part_b[...] = total
        spread(part_b, second_b, col_a, x_peer, 3)
        for second, columns, sem in ((second_a, slice(0, half), 2),
                                     (second_b, slice(half, 2 * half), 3)):
            pltpu.make_async_copy(second, second, rs_recv.at[sem]).wait()
            total = second[0]
            for k in range(1, side):
                total = total + second[k]
            out_ref[:, :, columns] = total.astype(BF16)

    def compute(phase):
        held = recv.at[phase]
        rows_in = held[:, :width]
        scaled = held[:, width:]
        w_gate = w_ref[0]
        w_up = w_ref[1]
        w_down = w_ref[2]
        pre_gate = mm(rows_in, w_gate)
        pre_up = mm(rows_in, w_up)
        sigmoid_gate = jax.nn.sigmoid(pre_gate)
        activated = pre_gate * sigmoid_gate
        hidden = (activated * pre_up).astype(BF16)
        hidden_grad = mm(scaled, w_down)
        gate_sum = jnp.sum(hidden.astype(F32) * hidden_grad, axis=1, keepdims=True)
        grad_pre_gate = (
            hidden_grad * pre_up * sigmoid_gate * (1.0 + pre_gate * (1.0 - sigmoid_gate))
        ).astype(BF16)
        grad_pre_up = (hidden_grad * activated).astype(BF16)
        grads = (
            lax.dot_general(rows_in, grad_pre_gate, CONTRACT_FIRST, preferred_element_type=F32),
            lax.dot_general(rows_in, grad_pre_up, CONTRACT_FIRST, preferred_element_type=F32),
            lax.dot_general(scaled, hidden, CONTRACT_FIRST, preferred_element_type=F32),
        )
        for index, value in enumerate(grads):
            if phase == 0:
                grad_ref[index] = value
            else:
                grad_ref[index] += value
        if phase == phases - 1:
            scatter_grads()
        input_grad = (
            lax.dot_general(grad_pre_gate, w_gate, CONTRACT_LAST, preferred_element_type=F32)
            + lax.dot_general(grad_pre_up, w_up, CONTRACT_LAST, preferred_element_type=F32)
        ).astype(BF16)
        out = back.at[phase]
        out[:, :width] = input_grad
        high = gate_sum.astype(BF16).astype(F32)
        low = gate_sum - high
        column = lax.broadcasted_iota(jnp.int32, (input_grad.shape[0], PAD), 1)
        tail = jnp.where(column == 0, high, jnp.where(column == 1, low, 0.0))
        out[:, width:] = tail.astype(BF16)

    send_forward(0)
    p1[:, :width] = mm(both1_ref[...], x1_ref[...]).astype(BF16)
    p1[:, width:] = (
        mm(first1_ref[...], qa1_ref[...]) + mm(second1_ref[...], qb1_ref[...])
    ).astype(BF16)
    for phase in range(phases):
        wait_all(recv.at[phase], phase)
        if phase + 1 < phases:
            send_forward(phase + 1)
        compute(phase)
        send_back(phase)

    wait_all(back.at[0], phases)
    held = ret0[...]
    tg0_ref[...] = lax.dot_general(
        both0_ref[...], held[:, :width], CONTRACT_FIRST, preferred_element_type=F32
    ).astype(BF16)
    gate_sum = held[:, width:width + 1].astype(F32) + held[:, width + 1:width + 2].astype(F32)
    for index, mask in enumerate((first0_ref, second0_ref)):
        chosen = mask[...].astype(F32) > 0.5
        gs0_ref[index:index + 1, :] = jnp.sum(
            jnp.where(chosen, gate_sum, 0.0), axis=0, keepdims=True
        )
    reduce_grads()

    for phase in range(phases):
        if phase > 0:
            wait_all(back.at[phase], phases + phase)
        wait_sent(recv.at[phase], phase)
        wait_sent(back.at[phase], phases + phase)
    rest = pl.ds(0, side - 1)
    for sem, buf in enumerate((first_a, first_b, second_a, second_b)):
        pltpu.make_async_copy(buf.at[rest], buf.at[rest], rs_send.at[sem]).wait()


def exchange(p0, packing, unpacking, weights, n_row):
    slots, full = p0.shape
    batch_rows = packing[3].shape[0]
    width = weights.shape[1]
    part = width // n_row
    held = slots // SPLITS
    back = jax.ShapeDtypeStruct((slots, width + PAD), BF16)
    share = (weights.shape[0], part, weights.shape[2])
    quarter = (weights.shape[0], part, weights.shape[2] // 2)
    phases = MICRO * SPLITS
    vmem = pl.BlockSpec(memory_space=pltpu.VMEM)
    return pl.pallas_call(
        exchange_kernel,
        out_shape=(
            back,
            jax.ShapeDtypeStruct(share, BF16),
            jax.ShapeDtypeStruct((batch_rows, width), BF16),
            jax.ShapeDtypeStruct((2, batch_rows), F32),
        ),
        in_specs=[vmem] * 11,
        out_specs=(vmem, vmem, vmem, vmem),
        scratch_shapes=[
            pltpu.VMEM((slots, full), BF16),
            pltpu.VMEM((slots, width + PAD), BF16),
            pltpu.VMEM((phases, held, full), BF16),
            pltpu.VMEM((phases, held, width + PAD), BF16),
            pltpu.VMEM(weights.shape, F32),
            pltpu.VMEM((SIDE, SIDE) + quarter, BF16),
            pltpu.VMEM((SIDE, SIDE) + quarter, BF16),
            pltpu.VMEM((SIDE, SIDE) + quarter, BF16),
            pltpu.VMEM((SIDE, SIDE) + quarter, BF16),
            pltpu.VMEM((SIDE,) + quarter, F32),
            pltpu.VMEM((SIDE,) + quarter, F32),
            pltpu.VMEM((SIDE,) + quarter, F32),
            pltpu.VMEM((SIDE,) + quarter, F32),
            pltpu.SemaphoreType.DMA((2 * phases,)),
            pltpu.SemaphoreType.DMA((2 * phases,)),
            pltpu.SemaphoreType.DMA((4,)),
            pltpu.SemaphoreType.DMA((4,)),
        ],
        compiler_params=pltpu.CompilerParams(
            collective_id=0, has_side_effects=True, vmem_limit_bytes=62 * 1024 * 1024
        ),
    )(p0, *packing, *unpacking, weights)


def on_device(tokens, cotangent, gates, expert_ids, expert_weights):
    n_expert = lax.axis_size("expert")
    expert_count = n_expert * expert_weights.shape[0]
    batch_rows = tokens.shape[0] // MICRO
    capacity = max(2, 4 * batch_rows // expert_count)
    width = tokens.shape[1]

    masks, gate_list, parts = [], [], []
    for micro_index in range(MICRO):
        lower = micro_index * batch_rows
        upper = lower + batch_rows
        first, second = route_masks(expert_ids[lower:upper], expert_count, capacity)
        both = (first | second).astype(BF16)
        cot = cotangent[lower:upper].astype(F32)
        gate = gates[lower:upper].astype(F32)
        scaled_first = (gate[:, 0:1] * cot).astype(BF16)
        scaled_second = (gate[:, 1:2] * cot).astype(BF16)
        masks.append((first, second, both))
        gate_list.append(gate)
        parts.append((tokens[lower:upper], scaled_first, scaled_second))

    first, second, both = masks[0]
    rows_in, scaled_first, scaled_second = parts[0]
    rows_in = mm(both, rows_in).astype(BF16)
    rows_scaled = (
        mm(first.astype(BF16), scaled_first) + mm(second.astype(BF16), scaled_second)
    ).astype(BF16)
    p0 = jnp.concatenate([rows_in, rows_scaled], axis=1)
    first, second, both = masks[1]
    packing = (both, first.astype(BF16), second.astype(BF16)) + parts[1]
    first, second, both = masks[0]
    unpacking = (both, first.astype(BF16), second.astype(BF16))

    ret1, weights_grad, token_first, gate_sums = exchange(
        p0, packing, unpacking, expert_weights[0], lax.axis_size("dp")
    )

    gate = gate_list[0]
    gate_first = jnp.stack([gate_sums[0] / gate[:, 0], gate_sums[1] / gate[:, 1]], axis=1)
    token_parts, gate_parts = [token_first], [gate_first.astype(BF16)]
    (first, second, both), gate = masks[1], gate_list[1]
    token_grad = lax.dot_general(
        both, ret1[:, :width], CONTRACT_FIRST, preferred_element_type=F32
    ).astype(BF16)
    gate_sum = ret1[:, width].astype(F32) + ret1[:, width + 1].astype(F32)
    sum_first = jnp.sum(jnp.where(first, gate_sum[:, None], 0.0), axis=0)
    sum_second = jnp.sum(jnp.where(second, gate_sum[:, None], 0.0), axis=0)
    gate_grad = jnp.stack([sum_first / gate[:, 0], sum_second / gate[:, 1]], axis=1)
    token_parts.append(token_grad)
    gate_parts.append(gate_grad.astype(BF16))

    return (
        jnp.concatenate(token_parts, axis=0),
        jnp.concatenate(gate_parts, axis=0),
        weights_grad[None],
    )


def solution(mesh):
    placed = (
        P(("dp", "expert"), None),
        P(("dp", "expert"), None),
        P(("dp", "expert"), None),
        P(("dp", "expert"), None),
        P("expert", None, None, None),
    )
    return jax.shard_map(
        on_device,
        mesh=mesh,
        in_specs=placed,
        out_specs=(
            P(("dp", "expert"), None),
            P(("dp", "expert"), None),
            P("expert", None, "dp", None),
        ),
        check_vma=False,
    )
```

```python
import jax
import jax.numpy as jnp
from jax import lax
from jax.experimental import pallas as pl
from jax.experimental.pallas import tpu as pltpu
from jax.sharding import PartitionSpec as P

MICRO = 2
SPLITS = 1
SIDE = 4
PAD = 128

F32 = jnp.float32
BF16 = jnp.bfloat16

CONTRACT_LAST = (((1,), (1,)), ((), ()))
CONTRACT_FIRST = (((0,), (0,)), ((), ()))
MESH = pl.DeviceIdType.MESH


def mm(a, b):
    return jnp.dot(a, b, preferred_element_type=F32)


def route_masks(ids_block, expert_count, capacity):
    flat_ids = ids_block.reshape(-1)
    one_hot = (flat_ids[:, None] == jnp.arange(expert_count, dtype=jnp.int32)[None, :]).astype(
        jnp.int32
    )
    earlier = jnp.cumsum(one_hot, axis=0) - one_hot
    rank_slot = jnp.sum(earlier * one_hot, axis=1)
    route_slot = (flat_ids * capacity + rank_slot).reshape(-1, 2)
    position = jnp.arange(expert_count * capacity, dtype=jnp.int32)[:, None]
    return position == route_slot[None, :, 0], position == route_slot[None, :, 1]


def expert_step(recv, w_gate, w_up, w_down, width):
    rows_in = recv[:, :width]
    scaled = recv[:, width:]
    pre_gate = mm(rows_in, w_gate)
    pre_up = mm(rows_in, w_up)
    sigmoid_gate = jax.nn.sigmoid(pre_gate)
    activated = pre_gate * sigmoid_gate
    hidden = (activated * pre_up).astype(BF16)
    hidden_grad = mm(scaled, w_down)
    gate_sum = jnp.sum(hidden.astype(F32) * hidden_grad, axis=1)
    grad_pre_gate = (
        hidden_grad * pre_up * sigmoid_gate * (1.0 + pre_gate * (1.0 - sigmoid_gate))
    ).astype(BF16)
    grad_pre_up = (hidden_grad * activated).astype(BF16)
    input_grad = (
        lax.dot_general(grad_pre_gate, w_gate, CONTRACT_LAST, preferred_element_type=F32)
        + lax.dot_general(grad_pre_up, w_up, CONTRACT_LAST, preferred_element_type=F32)
    ).astype(BF16)
    grads = (
        lax.dot_general(rows_in, grad_pre_gate, CONTRACT_FIRST, preferred_element_type=F32),
        lax.dot_general(rows_in, grad_pre_up, CONTRACT_FIRST, preferred_element_type=F32),
        lax.dot_general(scaled, hidden, CONTRACT_FIRST, preferred_element_type=F32),
    )
    high = gate_sum.astype(BF16)
    low = (gate_sum - high.astype(F32)).astype(BF16)
    tail = jnp.concatenate(
        [high[:, None], low[:, None], jnp.zeros((recv.shape[0], PAD - 2), BF16)], axis=1
    )
    return jnp.concatenate([input_grad, tail], axis=1), grads


def exchange_kernel(slot_ref, x_ref, qa_ref, qb_ref, w_ref, out_ref, tg_ref, gs_ref,
                    p0, p1, ret0, ret1, recv, back, grad_ref, round_a, round_b, first_a, first_b,
                    part_a, part_b, second_a, second_b, send_sem, recv_sem, rs_send, rs_recv):
    n = lax.axis_size("expert")
    me = lax.axis_index("expert")
    n_row = lax.axis_size("dp")
    row = lax.axis_index("dp")
    phases = recv.shape[0]
    splits = phases // MICRO
    capacity = p0.shape[0] // n
    batch_rows = x_ref.shape[0] // MICRO
    piece = capacity // splits
    width = w_ref.shape[1]
    part = out_ref.shape[1]
    payloads = (p0, p1)
    returns = (ret0, ret1)

    def selections(micro):
        position = lax.broadcasted_iota(jnp.int32, (p0.shape[0], batch_rows), 0)
        first = position == slot_ref[micro, 0:1, :]
        second = position == slot_ref[micro, 1:2, :]
        return first, second

    def pack(micro):
        first, second = selections(micro)
        first_b = jnp.where(first, 1.0, 0.0).astype(BF16)
        second_b = jnp.where(second, 1.0, 0.0).astype(BF16)
        both_b = jnp.where(first | second, 1.0, 0.0).astype(BF16)
        rows = pl.ds(micro * batch_rows, batch_rows)
        dst = payloads[micro]
        dst[:, :width] = mm(both_b, x_ref[rows, :]).astype(BF16)
        dst[:, width:] = (mm(first_b, qa_ref[rows, :]) + mm(second_b, qb_ref[rows, :])).astype(BF16)

    def unpack(micro):
        first, second = selections(micro)
        both_b = jnp.where(first | second, 1.0, 0.0).astype(BF16)
        held = returns[micro][...]
        rows = pl.ds(micro * batch_rows, batch_rows)
        tg_ref[rows, :] = lax.dot_general(
            both_b, held[:, :width], CONTRACT_FIRST, preferred_element_type=F32
        ).astype(BF16)
        gate_sum = held[:, width:width + 1].astype(F32) + held[:, width + 1:width + 2].astype(F32)
        for index, chosen in enumerate((first, second)):
            at = 2 * micro + index
            gs_ref[at:at + 1, :] = jnp.sum(jnp.where(chosen, gate_sum, 0.0), axis=0, keepdims=True)

    barrier = pltpu.get_barrier_semaphore()
    for k in range(1, n):
        peer = lax.rem(me + k, n)
        pl.semaphore_signal(barrier, inc=1, device_id=(row, peer), device_id_type=MESH)
    for k in range(1, n_row):
        peer = lax.rem(row + k, n_row)
        pl.semaphore_signal(barrier, inc=1, device_id=(peer, me), device_id_type=MESH)
    pack(0)
    pl.semaphore_wait(barrier, n - 1 + n_row - 1)

    def slot_rows(expert, phase):
        start = expert * capacity + (phase % splits) * piece
        return pl.ds(pl.multiple_of(start, piece), piece)

    def held_rows(source):
        return pl.ds(pl.multiple_of(source * piece, piece), piece)

    def scatter(phase, src_rows, dst_rows, src, dst, sem):
        pltpu.make_async_copy(src.at[src_rows(me)], dst.at[dst_rows(me)], recv_sem.at[sem]).start()
        for k in range(1, n):
            peer = lax.rem(me + k, n)
            pltpu.make_async_remote_copy(
                src_ref=src.at[src_rows(peer)],
                dst_ref=dst.at[dst_rows(me)],
                send_sem=send_sem.at[sem],
                recv_sem=recv_sem.at[sem],
                device_id=(row, peer),
                device_id_type=MESH,
            ).start()

    def send_forward(phase):
        scatter(phase, lambda e: slot_rows(e, phase), held_rows,
                payloads[phase // splits], recv.at[phase], phase)

    def send_back(phase):
        scatter(phase, held_rows, lambda e: slot_rows(e, phase),
                back.at[phase], returns[phase // splits], phases + phase)

    def wait_all(buf, sem):
        pltpu.make_async_copy(buf, buf, recv_sem.at[sem]).wait()

    def wait_sent(buf, sem):
        rest = pl.ds(0, (n - 1) * piece)
        pltpu.make_async_copy(buf.at[rest], buf.at[rest], send_sem.at[sem]).wait()

    side = SIDE
    col_a, col_b = row % side, row // side
    half = out_ref.shape[2] // 2

    def x_peer(k):
        return col_b * side + lax.rem(col_a + k, side)

    def y_peer(k):
        return lax.rem(col_b + k, side) * side + col_a

    def spread(src, dst, index, peer_of, sem):
        pltpu.make_async_copy(src.at[index], dst.at[index], rs_recv.at[sem]).start()
        for k in range(1, side):
            pltpu.make_async_remote_copy(
                src_ref=src.at[lax.rem(index + k, side)],
                dst_ref=dst.at[index],
                send_sem=rs_send.at[sem],
                recv_sem=rs_recv.at[sem],
                device_id=(peer_of(k), me),
                device_id_type=MESH,
            ).start()

    def scatter_grads():
        for block in range(n_row):
            rounded = grad_ref[:, block * part:(block + 1) * part, :].astype(BF16)
            round_a[block % side, block // side] = rounded[:, :, :half]
            round_b[block // side, block % side] = rounded[:, :, half:]
        spread(round_a, first_a, col_a, x_peer, 0)
        spread(round_b, first_b, col_b, y_peer, 1)

    def reduce_grads():
        pltpu.make_async_copy(first_a, first_a, rs_recv.at[0]).wait()
        total = first_a[0].astype(F32)
        for k in range(1, side):
            total = total + first_a[k].astype(F32)
        part_a[...] = total
        spread(part_a, second_a, col_b, y_peer, 2)
        pltpu.make_async_copy(first_b, first_b, rs_recv.at[1]).wait()
        total = first_b[0].astype(F32)
        for k in range(1, side):
            total = total + first_b[k].astype(F32)
        part_b[...] = total
        spread(part_b, second_b, col_a, x_peer, 3)
        for second, columns, sem in ((second_a, slice(0, half), 2),
                                     (second_b, slice(half, 2 * half), 3)):
            pltpu.make_async_copy(second, second, rs_recv.at[sem]).wait()
            total = second[0]
            for k in range(1, side):
                total = total + second[k]
            out_ref[:, :, columns] = total.astype(BF16)

    def compute(phase):
        held = recv.at[phase]
        rows_in = held[:, :width]
        scaled = held[:, width:]
        w_gate = w_ref[0]
        w_up = w_ref[1]
        w_down = w_ref[2]
        pre_gate = mm(rows_in, w_gate)
        pre_up = mm(rows_in, w_up)
        sigmoid_gate = jax.nn.sigmoid(pre_gate)
        activated = pre_gate * sigmoid_gate
        hidden = (activated * pre_up).astype(BF16)
        hidden_grad = mm(scaled, w_down)
        gate_sum = jnp.sum(hidden.astype(F32) * hidden_grad, axis=1, keepdims=True)
        grad_pre_gate = (
            hidden_grad * pre_up * sigmoid_gate * (1.0 + pre_gate * (1.0 - sigmoid_gate))
        ).astype(BF16)
        grad_pre_up = (hidden_grad * activated).astype(BF16)
        grads = (
            lax.dot_general(rows_in, grad_pre_gate, CONTRACT_FIRST, preferred_element_type=F32),
            lax.dot_general(rows_in, grad_pre_up, CONTRACT_FIRST, preferred_element_type=F32),
            lax.dot_general(scaled, hidden, CONTRACT_FIRST, preferred_element_type=F32),
        )
        for index, value in enumerate(grads):
            if phase == 0:
                grad_ref[index] = value
            else:
                grad_ref[index] += value
        if phase == phases - 1:
            scatter_grads()
        input_grad = (
            lax.dot_general(grad_pre_gate, w_gate, CONTRACT_LAST, preferred_element_type=F32)
            + lax.dot_general(grad_pre_up, w_up, CONTRACT_LAST, preferred_element_type=F32)
        ).astype(BF16)
        out = back.at[phase]
        out[:, :width] = input_grad
        high = gate_sum.astype(BF16).astype(F32)
        low = gate_sum - high
        column = lax.broadcasted_iota(jnp.int32, (input_grad.shape[0], PAD), 1)
        tail = jnp.where(column == 0, high, jnp.where(column == 1, low, 0.0))
        out[:, width:] = tail.astype(BF16)

    send_forward(0)
    pack(1)
    for phase in range(phases):
        wait_all(recv.at[phase], phase)
        if phase + 1 < phases:
            send_forward(phase + 1)
        compute(phase)
        send_back(phase)

    wait_all(back.at[0], phases)
    unpack(0)
    reduce_grads()

    for phase in range(phases):
        if phase > 0:
            wait_all(back.at[phase], phases + phase)
            unpack(phase)
        wait_sent(recv.at[phase], phase)
        wait_sent(back.at[phase], phases + phase)
    rest = pl.ds(0, side - 1)
    for sem, buf in enumerate((first_a, first_b, second_a, second_b)):
        pltpu.make_async_copy(buf.at[rest], buf.at[rest], rs_send.at[sem]).wait()


def exchange(slots, tokens, scaled_first, scaled_second, weights, n_row, capacity):
    n_expert = lax.axis_size("expert")
    rows = n_expert * capacity
    width = weights.shape[1]
    full = 2 * width
    part = width // n_row
    back = (rows, width + PAD)
    share = (weights.shape[0], part, weights.shape[2])
    quarter = (weights.shape[0], part, weights.shape[2] // 2)
    phases = MICRO
    vmem = pl.BlockSpec(memory_space=pltpu.VMEM)
    return pl.pallas_call(
        exchange_kernel,
        out_shape=(
            jax.ShapeDtypeStruct(share, BF16),
            jax.ShapeDtypeStruct(tokens.shape, BF16),
            jax.ShapeDtypeStruct((2 * MICRO, tokens.shape[0] // MICRO), F32),
        ),
        in_specs=[vmem] * 5,
        out_specs=(vmem, vmem, vmem),
        scratch_shapes=[
            pltpu.VMEM((rows, full), BF16),
            pltpu.VMEM((rows, full), BF16),
            pltpu.VMEM(back, BF16),
            pltpu.VMEM(back, BF16),
            pltpu.VMEM((phases, rows, full), BF16),
            pltpu.VMEM((phases,) + back, BF16),
            pltpu.VMEM(weights.shape, F32),
            pltpu.VMEM((SIDE, SIDE) + quarter, BF16),
            pltpu.VMEM((SIDE, SIDE) + quarter, BF16),
            pltpu.VMEM((SIDE, SIDE) + quarter, BF16),
            pltpu.VMEM((SIDE, SIDE) + quarter, BF16),
            pltpu.VMEM((SIDE,) + quarter, F32),
            pltpu.VMEM((SIDE,) + quarter, F32),
            pltpu.VMEM((SIDE,) + quarter, F32),
            pltpu.VMEM((SIDE,) + quarter, F32),
            pltpu.SemaphoreType.DMA((2 * phases,)),
            pltpu.SemaphoreType.DMA((2 * phases,)),
            pltpu.SemaphoreType.DMA((4,)),
            pltpu.SemaphoreType.DMA((4,)),
        ],
        compiler_params=pltpu.CompilerParams(
            collective_id=0, has_side_effects=True, vmem_limit_bytes=62 * 1024 * 1024
        ),
    )(slots, tokens, scaled_first, scaled_second, weights)


def route_slot_rows(ids_block, expert_count, capacity):
    flat_ids = ids_block.reshape(-1)
    one_hot = (flat_ids[:, None] == jnp.arange(expert_count, dtype=jnp.int32)[None, :]).astype(
        jnp.int32
    )
    earlier = jnp.cumsum(one_hot, axis=0) - one_hot
    rank_slot = jnp.sum(earlier * one_hot, axis=1)
    return (flat_ids * capacity + rank_slot).reshape(-1, 2).T


def on_device(tokens, cotangent, gates, expert_ids, expert_weights):
    n_expert = lax.axis_size("expert")
    expert_count = n_expert * expert_weights.shape[0]
    batch_rows = tokens.shape[0] // MICRO
    capacity = max(2, 4 * batch_rows // expert_count)
    slots = jnp.stack(
        [
            route_slot_rows(expert_ids[m * batch_rows:(m + 1) * batch_rows], expert_count, capacity)
            for m in range(MICRO)
        ]
    )
    cot = cotangent.astype(F32)
    gate = gates.astype(F32)
    scaled_first = (gate[:, 0:1] * cot).astype(BF16)
    scaled_second = (gate[:, 1:2] * cot).astype(BF16)
    weights_grad, token_grad, gate_sums = exchange(
        slots, tokens, scaled_first, scaled_second, expert_weights[0],
        lax.axis_size("dp"), capacity,
    )
    sums = gate_sums.reshape(MICRO, 2, batch_rows).transpose(0, 2, 1).reshape(-1, 2)
    return token_grad, (sums / gate).astype(BF16), weights_grad[None]


def solution(mesh):
    placed = (
        P(("dp", "expert"), None),
        P(("dp", "expert"), None),
        P(("dp", "expert"), None),
        P(("dp", "expert"), None),
        P("expert", None, None, None),
    )
    return jax.shard_map(
        on_device,
        mesh=mesh,
        in_specs=placed,
        out_specs=(
            P(("dp", "expert"), None),
            P(("dp", "expert"), None),
            P("expert", None, "dp", None),
        ),
        check_vma=False,
    )
```

```python
import jax
import jax.numpy as jnp
from jax import lax
from jax.experimental import pallas as pl
from jax.experimental.pallas import tpu as pltpu
from jax.sharding import PartitionSpec as P

MICRO = 2
SPLITS = 1
SIDE = 4
PAD = 128

F32 = jnp.float32
BF16 = jnp.bfloat16

CONTRACT_LAST = (((1,), (1,)), ((), ()))
CONTRACT_FIRST = (((0,), (0,)), ((), ()))
MESH = pl.DeviceIdType.MESH


def mm(a, b):
    return jnp.dot(a, b, preferred_element_type=F32)


def route_masks(ids_block, expert_count, capacity):
    flat_ids = ids_block.reshape(-1)
    one_hot = (flat_ids[:, None] == jnp.arange(expert_count, dtype=jnp.int32)[None, :]).astype(
        jnp.int32
    )
    earlier = jnp.cumsum(one_hot, axis=0) - one_hot
    rank_slot = jnp.sum(earlier * one_hot, axis=1)
    route_slot = (flat_ids * capacity + rank_slot).reshape(-1, 2)
    position = jnp.arange(expert_count * capacity, dtype=jnp.int32)[:, None]
    return position == route_slot[None, :, 0], position == route_slot[None, :, 1]


def expert_step(recv, w_gate, w_up, w_down, width):
    rows_in = recv[:, :width]
    scaled = recv[:, width:]
    pre_gate = mm(rows_in, w_gate)
    pre_up = mm(rows_in, w_up)
    sigmoid_gate = jax.nn.sigmoid(pre_gate)
    activated = pre_gate * sigmoid_gate
    hidden = (activated * pre_up).astype(BF16)
    hidden_grad = mm(scaled, w_down)
    gate_sum = jnp.sum(hidden.astype(F32) * hidden_grad, axis=1)
    grad_pre_gate = (
        hidden_grad * pre_up * sigmoid_gate * (1.0 + pre_gate * (1.0 - sigmoid_gate))
    ).astype(BF16)
    grad_pre_up = (hidden_grad * activated).astype(BF16)
    input_grad = (
        lax.dot_general(grad_pre_gate, w_gate, CONTRACT_LAST, preferred_element_type=F32)
        + lax.dot_general(grad_pre_up, w_up, CONTRACT_LAST, preferred_element_type=F32)
    ).astype(BF16)
    grads = (
        lax.dot_general(rows_in, grad_pre_gate, CONTRACT_FIRST, preferred_element_type=F32),
        lax.dot_general(rows_in, grad_pre_up, CONTRACT_FIRST, preferred_element_type=F32),
        lax.dot_general(scaled, hidden, CONTRACT_FIRST, preferred_element_type=F32),
    )
    high = gate_sum.astype(BF16)
    low = (gate_sum - high.astype(F32)).astype(BF16)
    tail = jnp.concatenate(
        [high[:, None], low[:, None], jnp.zeros((recv.shape[0], PAD - 2), BF16)], axis=1
    )
    return jnp.concatenate([input_grad, tail], axis=1), grads


def exchange_kernel(slot_ref, x_ref, cot_ref, gate_ref, w_ref, out_ref, tg_ref, gs_ref,
                    p0, p1, ret0, ret1, recv, back, grad_ref, round_a, round_b, first_a, first_b,
                    part_a, part_b, second_a, second_b, send_sem, recv_sem, rs_send, rs_recv):
    n = lax.axis_size("expert")
    me = lax.axis_index("expert")
    n_row = lax.axis_size("dp")
    row = lax.axis_index("dp")
    phases = recv.shape[0]
    splits = phases // MICRO
    capacity = p0.shape[0] // n
    batch_rows = x_ref.shape[0] // MICRO
    piece = capacity // splits
    width = w_ref.shape[1]
    part = out_ref.shape[1]
    payloads = (p0, p1)
    returns = (ret0, ret1)

    def selections(micro):
        position = lax.broadcasted_iota(jnp.int32, (p0.shape[0], batch_rows), 0)
        first = position == slot_ref[micro, 0:1, :]
        second = position == slot_ref[micro, 1:2, :]
        return first, second

    def pack(micro):
        first, second = selections(micro)
        first_b = jnp.where(first, 1.0, 0.0).astype(BF16)
        second_b = jnp.where(second, 1.0, 0.0).astype(BF16)
        both_b = jnp.where(first | second, 1.0, 0.0).astype(BF16)
        rows = pl.ds(micro * batch_rows, batch_rows)
        dst = payloads[micro]
        dst[:, :width] = mm(both_b, x_ref[rows, :]).astype(BF16)
        cot = cot_ref[rows, :].astype(F32)
        gate = gate_ref[rows, :].astype(F32)
        scaled_first = (gate[:, 0:1] * cot).astype(BF16)
        scaled_second = (gate[:, 1:2] * cot).astype(BF16)
        dst[:, width:] = (mm(first_b, scaled_first) + mm(second_b, scaled_second)).astype(BF16)

    def unpack(micro):
        first, second = selections(micro)
        both_b = jnp.where(first | second, 1.0, 0.0).astype(BF16)
        held = returns[micro][...]
        rows = pl.ds(micro * batch_rows, batch_rows)
        tg_ref[rows, :] = lax.dot_general(
            both_b, held[:, :width], CONTRACT_FIRST, preferred_element_type=F32
        ).astype(BF16)
        gate_sum = held[:, width:width + 1].astype(F32) + held[:, width + 1:width + 2].astype(F32)
        for index, chosen in enumerate((first, second)):
            at = 2 * micro + index
            gs_ref[at:at + 1, :] = jnp.sum(jnp.where(chosen, gate_sum, 0.0), axis=0, keepdims=True)

    barrier = pltpu.get_barrier_semaphore()
    for k in range(1, n):
        peer = lax.rem(me + k, n)
        pl.semaphore_signal(barrier, inc=1, device_id=(row, peer), device_id_type=MESH)
    for k in range(1, n_row):
        peer = lax.rem(row + k, n_row)
        pl.semaphore_signal(barrier, inc=1, device_id=(peer, me), device_id_type=MESH)
    pack(0)
    pl.semaphore_wait(barrier, n - 1 + n_row - 1)

    def slot_rows(expert, phase):
        start = expert * capacity + (phase % splits) * piece
        return pl.ds(pl.multiple_of(start, piece), piece)

    def held_rows(source):
        return pl.ds(pl.multiple_of(source * piece, piece), piece)

    def scatter(phase, src_rows, dst_rows, src, dst, sem):
        pltpu.make_async_copy(src.at[src_rows(me)], dst.at[dst_rows(me)], recv_sem.at[sem]).start()
        for k in range(1, n):
            peer = lax.rem(me + k, n)
            pltpu.make_async_remote_copy(
                src_ref=src.at[src_rows(peer)],
                dst_ref=dst.at[dst_rows(me)],
                send_sem=send_sem.at[sem],
                recv_sem=recv_sem.at[sem],
                device_id=(row, peer),
                device_id_type=MESH,
            ).start()

    def send_forward(phase):
        scatter(phase, lambda e: slot_rows(e, phase), held_rows,
                payloads[phase // splits], recv.at[phase], phase)

    def send_back(phase):
        scatter(phase, held_rows, lambda e: slot_rows(e, phase),
                back.at[phase], returns[phase // splits], phases + phase)

    def wait_all(buf, sem):
        pltpu.make_async_copy(buf, buf, recv_sem.at[sem]).wait()

    def wait_sent(buf, sem):
        rest = pl.ds(0, (n - 1) * piece)
        pltpu.make_async_copy(buf.at[rest], buf.at[rest], send_sem.at[sem]).wait()

    side = SIDE
    col_a, col_b = row % side, row // side
    half = out_ref.shape[2] // 2

    def x_peer(k):
        return col_b * side + lax.rem(col_a + k, side)

    def y_peer(k):
        return lax.rem(col_b + k, side) * side + col_a

    def spread(src, dst, index, peer_of, sem):
        pltpu.make_async_copy(src.at[index], dst.at[index], rs_recv.at[sem]).start()
        for k in range(1, side):
            pltpu.make_async_remote_copy(
                src_ref=src.at[lax.rem(index + k, side)],
                dst_ref=dst.at[index],
                send_sem=rs_send.at[sem],
                recv_sem=rs_recv.at[sem],
                device_id=(peer_of(k), me),
                device_id_type=MESH,
            ).start()

    def scatter_grads():
        for block in range(n_row):
            rounded = grad_ref[:, block * part:(block + 1) * part, :].astype(BF16)
            round_a[block % side, block // side] = rounded[:, :, :half]
            round_b[block // side, block % side] = rounded[:, :, half:]
        spread(round_a, first_a, col_a, x_peer, 0)
        spread(round_b, first_b, col_b, y_peer, 1)

    def reduce_grads():
        pltpu.make_async_copy(first_a, first_a, rs_recv.at[0]).wait()
        total = first_a[0].astype(F32)
        for k in range(1, side):
            total = total + first_a[k].astype(F32)
        part_a[...] = total
        spread(part_a, second_a, col_b, y_peer, 2)
        pltpu.make_async_copy(first_b, first_b, rs_recv.at[1]).wait()
        total = first_b[0].astype(F32)
        for k in range(1, side):
            total = total + first_b[k].astype(F32)
        part_b[...] = total
        spread(part_b, second_b, col_a, x_peer, 3)
        for second, columns, sem in ((second_a, slice(0, half), 2),
                                     (second_b, slice(half, 2 * half), 3)):
            pltpu.make_async_copy(second, second, rs_recv.at[sem]).wait()
            total = second[0]
            for k in range(1, side):
                total = total + second[k]
            out_ref[:, :, columns] = total.astype(BF16)

    def compute(phase):
        held = recv.at[phase]
        rows_in = held[:, :width]
        scaled = held[:, width:]
        w_gate = w_ref[0]
        w_up = w_ref[1]
        w_down = w_ref[2]
        pre_gate = mm(rows_in, w_gate)
        pre_up = mm(rows_in, w_up)
        sigmoid_gate = jax.nn.sigmoid(pre_gate)
        activated = pre_gate * sigmoid_gate
        hidden = (activated * pre_up).astype(BF16)
        hidden_grad = mm(scaled, w_down)
        gate_sum = jnp.sum(hidden.astype(F32) * hidden_grad, axis=1, keepdims=True)
        grad_pre_gate = (
            hidden_grad * pre_up * sigmoid_gate * (1.0 + pre_gate * (1.0 - sigmoid_gate))
        ).astype(BF16)
        grad_pre_up = (hidden_grad * activated).astype(BF16)
        grads = (
            lax.dot_general(rows_in, grad_pre_gate, CONTRACT_FIRST, preferred_element_type=F32),
            lax.dot_general(rows_in, grad_pre_up, CONTRACT_FIRST, preferred_element_type=F32),
            lax.dot_general(scaled, hidden, CONTRACT_FIRST, preferred_element_type=F32),
        )
        for index, value in enumerate(grads):
            if phase == 0:
                grad_ref[index] = value
            else:
                grad_ref[index] += value
        if phase == phases - 1:
            scatter_grads()
        input_grad = (
            lax.dot_general(grad_pre_gate, w_gate, CONTRACT_LAST, preferred_element_type=F32)
            + lax.dot_general(grad_pre_up, w_up, CONTRACT_LAST, preferred_element_type=F32)
        ).astype(BF16)
        out = back.at[phase]
        out[:, :width] = input_grad
        high = gate_sum.astype(BF16).astype(F32)
        low = gate_sum - high
        column = lax.broadcasted_iota(jnp.int32, (input_grad.shape[0], PAD), 1)
        tail = jnp.where(column == 0, high, jnp.where(column == 1, low, 0.0))
        out[:, width:] = tail.astype(BF16)

    send_forward(0)
    pack(1)
    for phase in range(phases):
        wait_all(recv.at[phase], phase)
        if phase + 1 < phases:
            send_forward(phase + 1)
        compute(phase)
        send_back(phase)

    wait_all(back.at[0], phases)
    unpack(0)
    reduce_grads()

    for phase in range(phases):
        if phase > 0:
            wait_all(back.at[phase], phases + phase)
            unpack(phase)
        wait_sent(recv.at[phase], phase)
        wait_sent(back.at[phase], phases + phase)
    rest = pl.ds(0, side - 1)
    for sem, buf in enumerate((first_a, first_b, second_a, second_b)):
        pltpu.make_async_copy(buf.at[rest], buf.at[rest], rs_send.at[sem]).wait()


def exchange(slots, tokens, cotangent, gates, weights, n_row, capacity):
    n_expert = lax.axis_size("expert")
    rows = n_expert * capacity
    width = weights.shape[1]
    full = 2 * width
    part = width // n_row
    back = (rows, width + PAD)
    share = (weights.shape[0], part, weights.shape[2])
    quarter = (weights.shape[0], part, weights.shape[2] // 2)
    phases = MICRO
    vmem = pl.BlockSpec(memory_space=pltpu.VMEM)
    return pl.pallas_call(
        exchange_kernel,
        out_shape=(
            jax.ShapeDtypeStruct(share, BF16),
            jax.ShapeDtypeStruct(tokens.shape, BF16),
            jax.ShapeDtypeStruct((2 * MICRO, tokens.shape[0] // MICRO), F32),
        ),
        in_specs=[vmem] * 5,
        out_specs=(vmem, vmem, vmem),
        scratch_shapes=[
            pltpu.VMEM((rows, full), BF16),
            pltpu.VMEM((rows, full), BF16),
            pltpu.VMEM(back, BF16),
            pltpu.VMEM(back, BF16),
            pltpu.VMEM((phases, rows, full), BF16),
            pltpu.VMEM((phases,) + back, BF16),
            pltpu.VMEM(weights.shape, F32),
            pltpu.VMEM((SIDE, SIDE) + quarter, BF16),
            pltpu.VMEM((SIDE, SIDE) + quarter, BF16),
            pltpu.VMEM((SIDE, SIDE) + quarter, BF16),
            pltpu.VMEM((SIDE, SIDE) + quarter, BF16),
            pltpu.VMEM((SIDE,) + quarter, F32),
            pltpu.VMEM((SIDE,) + quarter, F32),
            pltpu.VMEM((SIDE,) + quarter, F32),
            pltpu.VMEM((SIDE,) + quarter, F32),
            pltpu.SemaphoreType.DMA((2 * phases,)),
            pltpu.SemaphoreType.DMA((2 * phases,)),
            pltpu.SemaphoreType.DMA((4,)),
            pltpu.SemaphoreType.DMA((4,)),
        ],
        compiler_params=pltpu.CompilerParams(
            collective_id=0, has_side_effects=True, vmem_limit_bytes=62 * 1024 * 1024
        ),
    )(slots, tokens, cotangent, gates, weights)


def route_slot_rows(ids_block, expert_count, capacity):
    flat_ids = ids_block.reshape(-1)
    one_hot = (flat_ids[:, None] == jnp.arange(expert_count, dtype=jnp.int32)[None, :]).astype(
        jnp.int32
    )
    earlier = jnp.cumsum(one_hot, axis=0) - one_hot
    rank_slot = jnp.sum(earlier * one_hot, axis=1)
    return (flat_ids * capacity + rank_slot).reshape(-1, 2).T


def on_device(tokens, cotangent, gates, expert_ids, expert_weights):
    n_expert = lax.axis_size("expert")
    expert_count = n_expert * expert_weights.shape[0]
    batch_rows = tokens.shape[0] // MICRO
    capacity = max(2, 4 * batch_rows // expert_count)
    slots = jnp.stack(
        [
            route_slot_rows(expert_ids[m * batch_rows:(m + 1) * batch_rows], expert_count, capacity)
            for m in range(MICRO)
        ]
    )
    gate = gates.astype(F32)
    weights_grad, token_grad, gate_sums = exchange(
        slots, tokens, cotangent, gates, expert_weights[0],
        lax.axis_size("dp"), capacity,
    )
    sums = gate_sums.reshape(MICRO, 2, batch_rows).transpose(0, 2, 1).reshape(-1, 2)
    return token_grad, (sums / gate).astype(BF16), weights_grad[None]


def solution(mesh):
    placed = (
        P(("dp", "expert"), None),
        P(("dp", "expert"), None),
        P(("dp", "expert"), None),
        P(("dp", "expert"), None),
        P("expert", None, None, None),
    )
    return jax.shard_map(
        on_device,
        mesh=mesh,
        in_specs=placed,
        out_specs=(
            P(("dp", "expert"), None),
            P(("dp", "expert"), None),
            P("expert", None, "dp", None),
        ),
        check_vma=False,
    )
```

```python
import jax
import jax.numpy as jnp
from jax import lax
from jax.experimental import pallas as pl
from jax.experimental.pallas import tpu as pltpu
from jax.sharding import PartitionSpec as P

MICRO = 2
SPLITS = 1
SIDE = 4
PAD = 128

F32 = jnp.float32
BF16 = jnp.bfloat16

CONTRACT_LAST = (((1,), (1,)), ((), ()))
CONTRACT_FIRST = (((0,), (0,)), ((), ()))
MESH = pl.DeviceIdType.MESH


def mm(a, b):
    return jnp.dot(a, b, preferred_element_type=F32)


def route_masks(ids_block, expert_count, capacity):
    flat_ids = ids_block.reshape(-1)
    one_hot = (flat_ids[:, None] == jnp.arange(expert_count, dtype=jnp.int32)[None, :]).astype(
        jnp.int32
    )
    earlier = jnp.cumsum(one_hot, axis=0) - one_hot
    rank_slot = jnp.sum(earlier * one_hot, axis=1)
    route_slot = (flat_ids * capacity + rank_slot).reshape(-1, 2)
    position = jnp.arange(expert_count * capacity, dtype=jnp.int32)[:, None]
    return position == route_slot[None, :, 0], position == route_slot[None, :, 1]


def expert_step(recv, w_gate, w_up, w_down, width):
    rows_in = recv[:, :width]
    scaled = recv[:, width:]
    pre_gate = mm(rows_in, w_gate)
    pre_up = mm(rows_in, w_up)
    sigmoid_gate = jax.nn.sigmoid(pre_gate)
    activated = pre_gate * sigmoid_gate
    hidden = (activated * pre_up).astype(BF16)
    hidden_grad = mm(scaled, w_down)
    gate_sum = jnp.sum(hidden.astype(F32) * hidden_grad, axis=1)
    grad_pre_gate = (
        hidden_grad * pre_up * sigmoid_gate * (1.0 + pre_gate * (1.0 - sigmoid_gate))
    ).astype(BF16)
    grad_pre_up = (hidden_grad * activated).astype(BF16)
    input_grad = (
        lax.dot_general(grad_pre_gate, w_gate, CONTRACT_LAST, preferred_element_type=F32)
        + lax.dot_general(grad_pre_up, w_up, CONTRACT_LAST, preferred_element_type=F32)
    ).astype(BF16)
    grads = (
        lax.dot_general(rows_in, grad_pre_gate, CONTRACT_FIRST, preferred_element_type=F32),
        lax.dot_general(rows_in, grad_pre_up, CONTRACT_FIRST, preferred_element_type=F32),
        lax.dot_general(scaled, hidden, CONTRACT_FIRST, preferred_element_type=F32),
    )
    high = gate_sum.astype(BF16)
    low = (gate_sum - high.astype(F32)).astype(BF16)
    tail = jnp.concatenate(
        [high[:, None], low[:, None], jnp.zeros((recv.shape[0], PAD - 2), BF16)], axis=1
    )
    return jnp.concatenate([input_grad, tail], axis=1), grads


def exchange_kernel(ids_ref, x_ref, cot_ref, gate_ref, w_ref, out_ref, tg_ref, gs_ref,
                    p0, p1, ret0, ret1, recv, back, grad_ref, round_a, round_b, first_a, first_b,
                    part_a, part_b, second_a, second_b, send_sem, recv_sem, rs_send, rs_recv):
    n = lax.axis_size("expert")
    me = lax.axis_index("expert")
    n_row = lax.axis_size("dp")
    row = lax.axis_index("dp")
    phases = recv.shape[0]
    splits = phases // MICRO
    capacity = p0.shape[0] // n
    batch_rows = x_ref.shape[0] // MICRO
    n_experts = n * (p0.shape[0] // n // capacity)
    piece = capacity // splits
    width = w_ref.shape[1]
    part = out_ref.shape[1]
    payloads = (p0, p1)
    returns = (ret0, ret1)

    def selections(micro):
        rows = pl.ds(micro * batch_rows, batch_rows)
        ids = ids_ref[rows, :]
        expert = lax.broadcasted_iota(jnp.int32, (batch_rows, n_experts), 1)
        hot = [jnp.where(expert == ids[:, k:k + 1], 1.0, 0.0) for k in range(2)]
        token = lax.broadcasted_iota(jnp.int32, (batch_rows, batch_rows), 0)
        other = lax.broadcasted_iota(jnp.int32, (batch_rows, batch_rows), 1)
        earlier = jnp.where(token > other, 1.0, 0.0).astype(BF16)
        counts = mm(earlier, (hot[0] + hot[1]).astype(BF16))
        position = lax.broadcasted_iota(jnp.int32, (batch_rows, p0.shape[0]), 1)
        chosen = []
        for k in range(2):
            rank = jnp.sum(counts * hot[k], axis=1, keepdims=True).astype(jnp.int32)
            chosen.append(position == ids[:, k:k + 1] * capacity + rank)
        return chosen[0], chosen[1]

    def pack(micro):
        first, second = selections(micro)
        first_b = jnp.where(first, 1.0, 0.0).astype(BF16)
        second_b = jnp.where(second, 1.0, 0.0).astype(BF16)
        both_b = jnp.where(first | second, 1.0, 0.0).astype(BF16)
        rows = pl.ds(micro * batch_rows, batch_rows)
        dst = payloads[micro]
        cot = cot_ref[rows, :].astype(F32)
        gate = gate_ref[rows, :].astype(F32)
        scaled_first = (gate[:, 0:1] * cot).astype(BF16)
        scaled_second = (gate[:, 1:2] * cot).astype(BF16)
        dst[:, :width] = lax.dot_general(
            both_b, x_ref[rows, :], CONTRACT_FIRST, preferred_element_type=F32
        ).astype(BF16)
        dst[:, width:] = (
            lax.dot_general(first_b, scaled_first, CONTRACT_FIRST, preferred_element_type=F32)
            + lax.dot_general(second_b, scaled_second, CONTRACT_FIRST, preferred_element_type=F32)
        ).astype(BF16)

    def unpack(micro):
        first, second = selections(micro)
        both_b = jnp.where(first | second, 1.0, 0.0).astype(BF16)
        held = returns[micro][...]
        rows = pl.ds(micro * batch_rows, batch_rows)
        tg_ref[rows, :] = mm(both_b, held[:, :width]).astype(BF16)
        for index, chosen in enumerate((first, second)):
            picked = mm(jnp.where(chosen, 1.0, 0.0).astype(BF16), held[:, width:])
            gs_ref[rows, index:index + 1] = picked[:, 0:1] + picked[:, 1:2]

    barrier = pltpu.get_barrier_semaphore()
    for k in range(1, n):
        peer = lax.rem(me + k, n)
        pl.semaphore_signal(barrier, inc=1, device_id=(row, peer), device_id_type=MESH)
    for k in range(1, n_row):
        peer = lax.rem(row + k, n_row)
        pl.semaphore_signal(barrier, inc=1, device_id=(peer, me), device_id_type=MESH)
    pack(0)
    pl.semaphore_wait(barrier, n - 1 + n_row - 1)

    def slot_rows(expert, phase):
        start = expert * capacity + (phase % splits) * piece
        return pl.ds(pl.multiple_of(start, piece), piece)

    def held_rows(source):
        return pl.ds(pl.multiple_of(source * piece, piece), piece)

    def scatter(phase, src_rows, dst_rows, src, dst, sem):
        pltpu.make_async_copy(src.at[src_rows(me)], dst.at[dst_rows(me)], recv_sem.at[sem]).start()
        for k in range(1, n):
            peer = lax.rem(me + k, n)
            pltpu.make_async_remote_copy(
                src_ref=src.at[src_rows(peer)],
                dst_ref=dst.at[dst_rows(me)],
                send_sem=send_sem.at[sem],
                recv_sem=recv_sem.at[sem],
                device_id=(row, peer),
                device_id_type=MESH,
            ).start()

    def send_forward(phase):
        scatter(phase, lambda e: slot_rows(e, phase), held_rows,
                payloads[phase // splits], recv.at[phase], phase)

    def send_back(phase):
        scatter(phase, held_rows, lambda e: slot_rows(e, phase),
                back.at[phase], returns[phase // splits], phases + phase)

    def wait_all(buf, sem):
        pltpu.make_async_copy(buf, buf, recv_sem.at[sem]).wait()

    def wait_sent(buf, sem):
        rest = pl.ds(0, (n - 1) * piece)
        pltpu.make_async_copy(buf.at[rest], buf.at[rest], send_sem.at[sem]).wait()

    side = SIDE
    col_a, col_b = row % side, row // side
    half = out_ref.shape[2] // 2

    def x_peer(k):
        return col_b * side + lax.rem(col_a + k, side)

    def y_peer(k):
        return lax.rem(col_b + k, side) * side + col_a

    def spread(src, dst, index, peer_of, sem):
        pltpu.make_async_copy(src.at[index], dst.at[index], rs_recv.at[sem]).start()
        for k in range(1, side):
            pltpu.make_async_remote_copy(
                src_ref=src.at[lax.rem(index + k, side)],
                dst_ref=dst.at[index],
                send_sem=rs_send.at[sem],
                recv_sem=rs_recv.at[sem],
                device_id=(peer_of(k), me),
                device_id_type=MESH,
            ).start()

    def scatter_grads():
        for block in range(n_row):
            rounded = grad_ref[:, block * part:(block + 1) * part, :].astype(BF16)
            round_a[block % side, block // side] = rounded[:, :, :half]
            round_b[block // side, block % side] = rounded[:, :, half:]
        spread(round_a, first_a, col_a, x_peer, 0)
        spread(round_b, first_b, col_b, y_peer, 1)

    def reduce_grads():
        pltpu.make_async_copy(first_a, first_a, rs_recv.at[0]).wait()
        total = first_a[0].astype(F32)
        for k in range(1, side):
            total = total + first_a[k].astype(F32)
        part_a[...] = total
        spread(part_a, second_a, col_b, y_peer, 2)
        pltpu.make_async_copy(first_b, first_b, rs_recv.at[1]).wait()
        total = first_b[0].astype(F32)
        for k in range(1, side):
            total = total + first_b[k].astype(F32)
        part_b[...] = total
        spread(part_b, second_b, col_a, x_peer, 3)
        for second, columns, sem in ((second_a, slice(0, half), 2),
                                     (second_b, slice(half, 2 * half), 3)):
            pltpu.make_async_copy(second, second, rs_recv.at[sem]).wait()
            total = second[0]
            for k in range(1, side):
                total = total + second[k]
            out_ref[:, :, columns] = total.astype(BF16)

    def compute(phase):
        held = recv.at[phase]
        rows_in = held[:, :width]
        scaled = held[:, width:]
        w_gate = w_ref[0]
        w_up = w_ref[1]
        w_down = w_ref[2]
        pre_gate = mm(rows_in, w_gate)
        pre_up = mm(rows_in, w_up)
        sigmoid_gate = jax.nn.sigmoid(pre_gate)
        activated = pre_gate * sigmoid_gate
        hidden = (activated * pre_up).astype(BF16)
        hidden_grad = mm(scaled, w_down)
        gate_sum = jnp.sum(hidden.astype(F32) * hidden_grad, axis=1, keepdims=True)
        grad_pre_gate = (
            hidden_grad * pre_up * sigmoid_gate * (1.0 + pre_gate * (1.0 - sigmoid_gate))
        ).astype(BF16)
        grad_pre_up = (hidden_grad * activated).astype(BF16)
        grads = (
            lax.dot_general(rows_in, grad_pre_gate, CONTRACT_FIRST, preferred_element_type=F32),
            lax.dot_general(rows_in, grad_pre_up, CONTRACT_FIRST, preferred_element_type=F32),
            lax.dot_general(scaled, hidden, CONTRACT_FIRST, preferred_element_type=F32),
        )
        for index, value in enumerate(grads):
            if phase == 0:
                grad_ref[index] = value
            else:
                grad_ref[index] += value
        if phase == phases - 1:
            scatter_grads()
        input_grad = (
            lax.dot_general(grad_pre_gate, w_gate, CONTRACT_LAST, preferred_element_type=F32)
            + lax.dot_general(grad_pre_up, w_up, CONTRACT_LAST, preferred_element_type=F32)
        ).astype(BF16)
        out = back.at[phase]
        out[:, :width] = input_grad
        high = gate_sum.astype(BF16).astype(F32)
        low = gate_sum - high
        column = lax.broadcasted_iota(jnp.int32, (input_grad.shape[0], PAD), 1)
        tail = jnp.where(column == 0, high, jnp.where(column == 1, low, 0.0))
        out[:, width:] = tail.astype(BF16)

    send_forward(0)
    pack(1)
    for phase in range(phases):
        wait_all(recv.at[phase], phase)
        if phase + 1 < phases:
            send_forward(phase + 1)
        compute(phase)
        send_back(phase)

    wait_all(back.at[0], phases)
    unpack(0)
    reduce_grads()

    for phase in range(phases):
        if phase > 0:
            wait_all(back.at[phase], phases + phase)
            unpack(phase)
        wait_sent(recv.at[phase], phase)
        wait_sent(back.at[phase], phases + phase)
    rest = pl.ds(0, side - 1)
    for sem, buf in enumerate((first_a, first_b, second_a, second_b)):
        pltpu.make_async_copy(buf.at[rest], buf.at[rest], rs_send.at[sem]).wait()


def exchange(slots, tokens, cotangent, gates, weights, n_row, capacity):
    n_expert = lax.axis_size("expert")
    rows = n_expert * capacity
    width = weights.shape[1]
    full = 2 * width
    part = width // n_row
    back = (rows, width + PAD)
    share = (weights.shape[0], part, weights.shape[2])
    quarter = (weights.shape[0], part, weights.shape[2] // 2)
    phases = MICRO
    vmem = pl.BlockSpec(memory_space=pltpu.VMEM)
    return pl.pallas_call(
        exchange_kernel,
        out_shape=(
            jax.ShapeDtypeStruct(share, BF16),
            jax.ShapeDtypeStruct(tokens.shape, BF16),
            jax.ShapeDtypeStruct((tokens.shape[0], 2), F32),
        ),
        in_specs=[vmem] * 5,
        out_specs=(vmem, vmem, vmem),
        scratch_shapes=[
            pltpu.VMEM((rows, full), BF16),
            pltpu.VMEM((rows, full), BF16),
            pltpu.VMEM(back, BF16),
            pltpu.VMEM(back, BF16),
            pltpu.VMEM((phases, rows, full), BF16),
            pltpu.VMEM((phases,) + back, BF16),
            pltpu.VMEM(weights.shape, F32),
            pltpu.VMEM((SIDE, SIDE) + quarter, BF16),
            pltpu.VMEM((SIDE, SIDE) + quarter, BF16),
            pltpu.VMEM((SIDE, SIDE) + quarter, BF16),
            pltpu.VMEM((SIDE, SIDE) + quarter, BF16),
            pltpu.VMEM((SIDE,) + quarter, F32),
            pltpu.VMEM((SIDE,) + quarter, F32),
            pltpu.VMEM((SIDE,) + quarter, F32),
            pltpu.VMEM((SIDE,) + quarter, F32),
            pltpu.SemaphoreType.DMA((2 * phases,)),
            pltpu.SemaphoreType.DMA((2 * phases,)),
            pltpu.SemaphoreType.DMA((4,)),
            pltpu.SemaphoreType.DMA((4,)),
        ],
        compiler_params=pltpu.CompilerParams(
            collective_id=0, has_side_effects=True, vmem_limit_bytes=62 * 1024 * 1024
        ),
    )(slots, tokens, cotangent, gates, weights)


def route_slot_rows(ids_block, expert_count, capacity):
    flat_ids = ids_block.reshape(-1)
    one_hot = (flat_ids[:, None] == jnp.arange(expert_count, dtype=jnp.int32)[None, :]).astype(
        jnp.int32
    )
    earlier = jnp.cumsum(one_hot, axis=0) - one_hot
    rank_slot = jnp.sum(earlier * one_hot, axis=1)
    return (flat_ids * capacity + rank_slot).reshape(-1, 2).T


def on_device(tokens, cotangent, gates, expert_ids, expert_weights):
    n_expert = lax.axis_size("expert")
    expert_count = n_expert * expert_weights.shape[0]
    batch_rows = tokens.shape[0] // MICRO
    capacity = max(2, 4 * batch_rows // expert_count)
    gate = gates.astype(F32)
    weights_grad, token_grad, gate_sums = exchange(
        expert_ids, tokens, cotangent, gates, expert_weights[0],
        lax.axis_size("dp"), capacity,
    )
    return token_grad, (gate_sums / gate).astype(BF16), weights_grad[None]


def solution(mesh):
    placed = (
        P(("dp", "expert"), None),
        P(("dp", "expert"), None),
        P(("dp", "expert"), None),
        P(("dp", "expert"), None),
        P("expert", None, None, None),
    )
    return jax.shard_map(
        on_device,
        mesh=mesh,
        in_specs=placed,
        out_specs=(
            P(("dp", "expert"), None),
            P(("dp", "expert"), None),
            P("expert", None, "dp", None),
        ),
        check_vma=False,
    )
```

```python
import jax
import jax.numpy as jnp
from jax import lax
from jax.experimental import pallas as pl
from jax.experimental.pallas import tpu as pltpu
from jax.sharding import PartitionSpec as P

MICRO = 2
SPLITS = 1
SIDE = 4
PAD = 128

F32 = jnp.float32
BF16 = jnp.bfloat16

CONTRACT_LAST = (((1,), (1,)), ((), ()))
CONTRACT_FIRST = (((0,), (0,)), ((), ()))
MESH = pl.DeviceIdType.MESH


def mm(a, b):
    return jnp.dot(a, b, preferred_element_type=F32)


def route_masks(ids_block, expert_count, capacity):
    flat_ids = ids_block.reshape(-1)
    one_hot = (flat_ids[:, None] == jnp.arange(expert_count, dtype=jnp.int32)[None, :]).astype(
        jnp.int32
    )
    earlier = jnp.cumsum(one_hot, axis=0) - one_hot
    rank_slot = jnp.sum(earlier * one_hot, axis=1)
    route_slot = (flat_ids * capacity + rank_slot).reshape(-1, 2)
    position = jnp.arange(expert_count * capacity, dtype=jnp.int32)[:, None]
    return position == route_slot[None, :, 0], position == route_slot[None, :, 1]


def expert_step(recv, w_gate, w_up, w_down, width):
    rows_in = recv[:, :width]
    scaled = recv[:, width:]
    pre_gate = mm(rows_in, w_gate)
    pre_up = mm(rows_in, w_up)
    sigmoid_gate = jax.nn.sigmoid(pre_gate)
    activated = pre_gate * sigmoid_gate
    hidden = (activated * pre_up).astype(BF16)
    hidden_grad = mm(scaled, w_down)
    gate_sum = jnp.sum(hidden.astype(F32) * hidden_grad, axis=1)
    grad_pre_gate = (
        hidden_grad * pre_up * sigmoid_gate * (1.0 + pre_gate * (1.0 - sigmoid_gate))
    ).astype(BF16)
    grad_pre_up = (hidden_grad * activated).astype(BF16)
    input_grad = (
        lax.dot_general(grad_pre_gate, w_gate, CONTRACT_LAST, preferred_element_type=F32)
        + lax.dot_general(grad_pre_up, w_up, CONTRACT_LAST, preferred_element_type=F32)
    ).astype(BF16)
    grads = (
        lax.dot_general(rows_in, grad_pre_gate, CONTRACT_FIRST, preferred_element_type=F32),
        lax.dot_general(rows_in, grad_pre_up, CONTRACT_FIRST, preferred_element_type=F32),
        lax.dot_general(scaled, hidden, CONTRACT_FIRST, preferred_element_type=F32),
    )
    high = gate_sum.astype(BF16)
    low = (gate_sum - high.astype(F32)).astype(BF16)
    tail = jnp.concatenate(
        [high[:, None], low[:, None], jnp.zeros((recv.shape[0], PAD - 2), BF16)], axis=1
    )
    return jnp.concatenate([input_grad, tail], axis=1), grads


def exchange_kernel(ids_ref, x_ref, cot_ref, gate_ref, w_ref, out_ref, tg_ref, gs_ref,
                    p0, p1, ret0, ret1, recv, back, grad_ref, round_a, round_b, first_a, first_b,
                    part_a, part_b, second_a, second_b, send_sem, recv_sem, rs_send, rs_recv):
    n = lax.axis_size("expert")
    me = lax.axis_index("expert")
    n_row = lax.axis_size("dp")
    row = lax.axis_index("dp")
    phases = recv.shape[0]
    splits = phases // MICRO
    capacity = p0.shape[0] // n
    batch_rows = x_ref.shape[0] // MICRO
    n_experts = n * (p0.shape[0] // n // capacity)
    piece = capacity // splits
    width = w_ref.shape[1]
    part = out_ref.shape[1]
    payloads = (p0, p1)
    returns = (ret0, ret1)

    def selections(micro):
        rows = pl.ds(micro * batch_rows, batch_rows)
        ids = ids_ref[:, rows]
        expert = lax.broadcasted_iota(jnp.int32, (n_experts, batch_rows), 0)
        hot = [jnp.where(expert == ids[k:k + 1, :], 1.0, 0.0) for k in range(2)]
        before = lax.broadcasted_iota(jnp.int32, (batch_rows, batch_rows), 0)
        after = lax.broadcasted_iota(jnp.int32, (batch_rows, batch_rows), 1)
        earlier = jnp.where(before < after, 1.0, 0.0).astype(BF16)
        counts = mm((hot[0] + hot[1]).astype(BF16), earlier)
        position = lax.broadcasted_iota(jnp.int32, (p0.shape[0], batch_rows), 0)
        chosen = []
        for k in range(2):
            rank = jnp.sum(counts * hot[k], axis=0, keepdims=True).astype(jnp.int32)
            chosen.append(position == ids[k:k + 1, :] * capacity + rank)
        return chosen[0], chosen[1]

    def pack(micro):
        first, second = selections(micro)
        rows = pl.ds(micro * batch_rows, batch_rows)
        gate = gate_ref[:, rows].astype(F32)
        both_b = jnp.where(first | second, 1.0, 0.0).astype(BF16)
        gated = jnp.where(first, gate[0:1, :], jnp.where(second, gate[1:2, :], 0.0)).astype(BF16)
        dst = payloads[micro]
        dst[:, :width] = mm(both_b, x_ref[rows, :]).astype(BF16)
        dst[:, width:] = mm(gated, cot_ref[rows, :]).astype(BF16)

    def unpack(micro):
        first, second = selections(micro)
        both_b = jnp.where(first | second, 1.0, 0.0).astype(BF16)
        held = returns[micro][...]
        rows = pl.ds(micro * batch_rows, batch_rows)
        tg_ref[rows, :] = lax.dot_general(
            both_b, held[:, :width], CONTRACT_FIRST, preferred_element_type=F32
        ).astype(BF16)
        gate_sum = held[:, width:width + 1].astype(F32) + held[:, width + 1:width + 2].astype(F32)
        for index, chosen in enumerate((first, second)):
            gs_ref[index:index + 1, rows] = jnp.sum(
                jnp.where(chosen, gate_sum, 0.0), axis=0, keepdims=True
            )

    barrier = pltpu.get_barrier_semaphore()
    for k in range(1, n):
        peer = lax.rem(me + k, n)
        pl.semaphore_signal(barrier, inc=1, device_id=(row, peer), device_id_type=MESH)
    for k in range(1, n_row):
        peer = lax.rem(row + k, n_row)
        pl.semaphore_signal(barrier, inc=1, device_id=(peer, me), device_id_type=MESH)
    pack(0)
    pl.semaphore_wait(barrier, n - 1 + n_row - 1)

    def slot_rows(expert, phase):
        start = expert * capacity + (phase % splits) * piece
        return pl.ds(pl.multiple_of(start, piece), piece)

    def held_rows(source):
        return pl.ds(pl.multiple_of(source * piece, piece), piece)

    def scatter(phase, src_rows, dst_rows, src, dst, sem):
        pltpu.make_async_copy(src.at[src_rows(me)], dst.at[dst_rows(me)], recv_sem.at[sem]).start()
        for k in range(1, n):
            peer = lax.rem(me + k, n)
            pltpu.make_async_remote_copy(
                src_ref=src.at[src_rows(peer)],
                dst_ref=dst.at[dst_rows(me)],
                send_sem=send_sem.at[sem],
                recv_sem=recv_sem.at[sem],
                device_id=(row, peer),
                device_id_type=MESH,
            ).start()

    def send_forward(phase):
        scatter(phase, lambda e: slot_rows(e, phase), held_rows,
                payloads[phase // splits], recv.at[phase], phase)

    def send_back(phase):
        scatter(phase, held_rows, lambda e: slot_rows(e, phase),
                back.at[phase], returns[phase // splits], phases + phase)

    def wait_all(buf, sem):
        pltpu.make_async_copy(buf, buf, recv_sem.at[sem]).wait()

    def wait_sent(buf, sem):
        rest = pl.ds(0, (n - 1) * piece)
        pltpu.make_async_copy(buf.at[rest], buf.at[rest], send_sem.at[sem]).wait()

    side = SIDE
    col_a, col_b = row % side, row // side
    half = out_ref.shape[2] // 2

    def x_peer(k):
        return col_b * side + lax.rem(col_a + k, side)

    def y_peer(k):
        return lax.rem(col_b + k, side) * side + col_a

    def spread(src, dst, index, peer_of, sem):
        pltpu.make_async_copy(src.at[index], dst.at[index], rs_recv.at[sem]).start()
        for k in range(1, side):
            pltpu.make_async_remote_copy(
                src_ref=src.at[lax.rem(index + k, side)],
                dst_ref=dst.at[index],
                send_sem=rs_send.at[sem],
                recv_sem=rs_recv.at[sem],
                device_id=(peer_of(k), me),
                device_id_type=MESH,
            ).start()

    def scatter_grads():
        for block in range(n_row):
            rounded = grad_ref[:, block * part:(block + 1) * part, :].astype(BF16)
            round_a[block % side, block // side] = rounded[:, :, :half]
            round_b[block // side, block % side] = rounded[:, :, half:]
        spread(round_a, first_a, col_a, x_peer, 0)
        spread(round_b, first_b, col_b, y_peer, 1)

    def reduce_grads():
        pltpu.make_async_copy(first_a, first_a, rs_recv.at[0]).wait()
        total = first_a[0].astype(F32)
        for k in range(1, side):
            total = total + first_a[k].astype(F32)
        part_a[...] = total
        spread(part_a, second_a, col_b, y_peer, 2)
        pltpu.make_async_copy(first_b, first_b, rs_recv.at[1]).wait()
        total = first_b[0].astype(F32)
        for k in range(1, side):
            total = total + first_b[k].astype(F32)
        part_b[...] = total
        spread(part_b, second_b, col_a, x_peer, 3)
        for second, columns, sem in ((second_a, slice(0, half), 2),
                                     (second_b, slice(half, 2 * half), 3)):
            pltpu.make_async_copy(second, second, rs_recv.at[sem]).wait()
            total = second[0]
            for k in range(1, side):
                total = total + second[k]
            out_ref[:, :, columns] = total.astype(BF16)

    def compute(phase):
        held = recv.at[phase]
        rows_in = held[:, :width]
        scaled = held[:, width:]
        w_gate = w_ref[0]
        w_up = w_ref[1]
        w_down = w_ref[2]
        pre_gate = mm(rows_in, w_gate)
        pre_up = mm(rows_in, w_up)
        sigmoid_gate = jax.nn.sigmoid(pre_gate)
        activated = pre_gate * sigmoid_gate
        hidden = (activated * pre_up).astype(BF16)
        hidden_grad = mm(scaled, w_down)
        gate_sum = jnp.sum(hidden.astype(F32) * hidden_grad, axis=1, keepdims=True)
        grad_pre_gate = (
            hidden_grad * pre_up * sigmoid_gate * (1.0 + pre_gate * (1.0 - sigmoid_gate))
        ).astype(BF16)
        grad_pre_up = (hidden_grad * activated).astype(BF16)
        grads = (
            lax.dot_general(rows_in, grad_pre_gate, CONTRACT_FIRST, preferred_element_type=F32),
            lax.dot_general(rows_in, grad_pre_up, CONTRACT_FIRST, preferred_element_type=F32),
            lax.dot_general(scaled, hidden, CONTRACT_FIRST, preferred_element_type=F32),
        )
        for index, value in enumerate(grads):
            if phase == 0:
                grad_ref[index] = value
            else:
                grad_ref[index] += value
        if phase == phases - 1:
            scatter_grads()
        input_grad = (
            lax.dot_general(grad_pre_gate, w_gate, CONTRACT_LAST, preferred_element_type=F32)
            + lax.dot_general(grad_pre_up, w_up, CONTRACT_LAST, preferred_element_type=F32)
        ).astype(BF16)
        out = back.at[phase]
        out[:, :width] = input_grad
        high = gate_sum.astype(BF16).astype(F32)
        low = gate_sum - high
        column = lax.broadcasted_iota(jnp.int32, (input_grad.shape[0], PAD), 1)
        tail = jnp.where(column == 0, high, jnp.where(column == 1, low, 0.0))
        out[:, width:] = tail.astype(BF16)

    send_forward(0)
    pack(1)
    for phase in range(phases):
        wait_all(recv.at[phase], phase)
        if phase + 1 < phases:
            send_forward(phase + 1)
        compute(phase)
        send_back(phase)

    wait_all(back.at[0], phases)
    unpack(0)
    reduce_grads()

    for phase in range(phases):
        if phase > 0:
            wait_all(back.at[phase], phases + phase)
            unpack(phase)
        wait_sent(recv.at[phase], phase)
        wait_sent(back.at[phase], phases + phase)
    rest = pl.ds(0, side - 1)
    for sem, buf in enumerate((first_a, first_b, second_a, second_b)):
        pltpu.make_async_copy(buf.at[rest], buf.at[rest], rs_send.at[sem]).wait()


def exchange(slots, tokens, cotangent, gates, weights, n_row, capacity):
    n_expert = lax.axis_size("expert")
    rows = n_expert * capacity
    width = weights.shape[1]
    full = 2 * width
    part = width // n_row
    back = (rows, width + PAD)
    share = (weights.shape[0], part, weights.shape[2])
    quarter = (weights.shape[0], part, weights.shape[2] // 2)
    phases = MICRO
    vmem = pl.BlockSpec(memory_space=pltpu.VMEM)
    return pl.pallas_call(
        exchange_kernel,
        out_shape=(
            jax.ShapeDtypeStruct(share, BF16),
            jax.ShapeDtypeStruct(tokens.shape, BF16),
            jax.ShapeDtypeStruct((2, tokens.shape[0]), F32),
        ),
        in_specs=[vmem] * 5,
        out_specs=(vmem, vmem, vmem),
        scratch_shapes=[
            pltpu.VMEM((rows, full), BF16),
            pltpu.VMEM((rows, full), BF16),
            pltpu.VMEM(back, BF16),
            pltpu.VMEM(back, BF16),
            pltpu.VMEM((phases, rows, full), BF16),
            pltpu.VMEM((phases,) + back, BF16),
            pltpu.VMEM(weights.shape, F32),
            pltpu.VMEM((SIDE, SIDE) + quarter, BF16),
            pltpu.VMEM((SIDE, SIDE) + quarter, BF16),
            pltpu.VMEM((SIDE, SIDE) + quarter, BF16),
            pltpu.VMEM((SIDE, SIDE) + quarter, BF16),
            pltpu.VMEM((SIDE,) + quarter, F32),
            pltpu.VMEM((SIDE,) + quarter, F32),
            pltpu.VMEM((SIDE,) + quarter, F32),
            pltpu.VMEM((SIDE,) + quarter, F32),
            pltpu.SemaphoreType.DMA((2 * phases,)),
            pltpu.SemaphoreType.DMA((2 * phases,)),
            pltpu.SemaphoreType.DMA((4,)),
            pltpu.SemaphoreType.DMA((4,)),
        ],
        compiler_params=pltpu.CompilerParams(
            collective_id=0, has_side_effects=True, vmem_limit_bytes=62 * 1024 * 1024
        ),
    )(slots, tokens, cotangent, gates, weights)


def route_slot_rows(ids_block, expert_count, capacity):
    flat_ids = ids_block.reshape(-1)
    one_hot = (flat_ids[:, None] == jnp.arange(expert_count, dtype=jnp.int32)[None, :]).astype(
        jnp.int32
    )
    earlier = jnp.cumsum(one_hot, axis=0) - one_hot
    rank_slot = jnp.sum(earlier * one_hot, axis=1)
    return (flat_ids * capacity + rank_slot).reshape(-1, 2).T


def on_device(tokens, cotangent, gates, expert_ids, expert_weights):
    n_expert = lax.axis_size("expert")
    expert_count = n_expert * expert_weights.shape[0]
    batch_rows = tokens.shape[0] // MICRO
    capacity = max(2, 4 * batch_rows // expert_count)
    gate = gates.T.astype(F32)
    weights_grad, token_grad, gate_sums = exchange(
        expert_ids.T, tokens, cotangent, gates.T, expert_weights[0],
        lax.axis_size("dp"), capacity,
    )
    return token_grad, (gate_sums / gate).astype(BF16).T, weights_grad[None]


def solution(mesh):
    placed = (
        P(("dp", "expert"), None),
        P(("dp", "expert"), None),
        P(("dp", "expert"), None),
        P(("dp", "expert"), None),
        P("expert", None, None, None),
    )
    return jax.shard_map(
        on_device,
        mesh=mesh,
        in_specs=placed,
        out_specs=(
            P(("dp", "expert"), None),
            P(("dp", "expert"), None),
            P("expert", None, "dp", None),
        ),
        check_vma=False,
    )
```

```python
import jax
import jax.numpy as jnp
from jax import lax
from jax.experimental import pallas as pl
from jax.experimental.pallas import tpu as pltpu
from jax.sharding import PartitionSpec as P

MICRO = 2
SPLITS = 1
SIDE = 4
PAD = 128

F32 = jnp.float32
BF16 = jnp.bfloat16

CONTRACT_LAST = (((1,), (1,)), ((), ()))
CONTRACT_FIRST = (((0,), (0,)), ((), ()))
MESH = pl.DeviceIdType.MESH


def mm(a, b):
    return jnp.dot(a, b, preferred_element_type=F32)


def route_masks(ids_block, expert_count, capacity):
    flat_ids = ids_block.reshape(-1)
    one_hot = (flat_ids[:, None] == jnp.arange(expert_count, dtype=jnp.int32)[None, :]).astype(
        jnp.int32
    )
    earlier = jnp.cumsum(one_hot, axis=0) - one_hot
    rank_slot = jnp.sum(earlier * one_hot, axis=1)
    route_slot = (flat_ids * capacity + rank_slot).reshape(-1, 2)
    position = jnp.arange(expert_count * capacity, dtype=jnp.int32)[:, None]
    return position == route_slot[None, :, 0], position == route_slot[None, :, 1]


def expert_step(recv, w_gate, w_up, w_down, width):
    rows_in = recv[:, :width]
    scaled = recv[:, width:]
    pre_gate = mm(rows_in, w_gate)
    pre_up = mm(rows_in, w_up)
    sigmoid_gate = jax.nn.sigmoid(pre_gate)
    activated = pre_gate * sigmoid_gate
    hidden = (activated * pre_up).astype(BF16)
    hidden_grad = mm(scaled, w_down)
    gate_sum = jnp.sum(hidden.astype(F32) * hidden_grad, axis=1)
    grad_pre_gate = (
        hidden_grad * pre_up * sigmoid_gate * (1.0 + pre_gate * (1.0 - sigmoid_gate))
    ).astype(BF16)
    grad_pre_up = (hidden_grad * activated).astype(BF16)
    input_grad = (
        lax.dot_general(grad_pre_gate, w_gate, CONTRACT_LAST, preferred_element_type=F32)
        + lax.dot_general(grad_pre_up, w_up, CONTRACT_LAST, preferred_element_type=F32)
    ).astype(BF16)
    grads = (
        lax.dot_general(rows_in, grad_pre_gate, CONTRACT_FIRST, preferred_element_type=F32),
        lax.dot_general(rows_in, grad_pre_up, CONTRACT_FIRST, preferred_element_type=F32),
        lax.dot_general(scaled, hidden, CONTRACT_FIRST, preferred_element_type=F32),
    )
    high = gate_sum.astype(BF16)
    low = (gate_sum - high.astype(F32)).astype(BF16)
    tail = jnp.concatenate(
        [high[:, None], low[:, None], jnp.zeros((recv.shape[0], PAD - 2), BF16)], axis=1
    )
    return jnp.concatenate([input_grad, tail], axis=1), grads


def exchange_kernel(ids_ref, x_ref, cot_ref, gate_ref, w_ref, out_ref, tg_ref, gg_ref,
                    gs_ref, p0, p1, ret0, ret1, recv, back, grad_ref, round_a, round_b, first_a, first_b,
                    part_a, part_b, second_a, second_b, send_sem, recv_sem, rs_send, rs_recv):
    n = lax.axis_size("expert")
    me = lax.axis_index("expert")
    n_row = lax.axis_size("dp")
    row = lax.axis_index("dp")
    phases = recv.shape[0]
    splits = phases // MICRO
    capacity = p0.shape[0] // n
    batch_rows = x_ref.shape[0] // MICRO
    n_experts = n * (p0.shape[0] // n // capacity)
    piece = capacity // splits
    width = w_ref.shape[1]
    part = out_ref.shape[1]
    payloads = (p0, p1)
    returns = (ret0, ret1)

    def selections(micro):
        rows = pl.ds(micro * batch_rows, batch_rows)
        ids = ids_ref[:, rows]
        expert = lax.broadcasted_iota(jnp.int32, (n_experts, batch_rows), 0)
        hot = [jnp.where(expert == ids[k:k + 1, :], 1.0, 0.0) for k in range(2)]
        before = lax.broadcasted_iota(jnp.int32, (batch_rows, batch_rows), 0)
        after = lax.broadcasted_iota(jnp.int32, (batch_rows, batch_rows), 1)
        earlier = jnp.where(before < after, 1.0, 0.0).astype(BF16)
        counts = mm((hot[0] + hot[1]).astype(BF16), earlier)
        position = lax.broadcasted_iota(jnp.int32, (p0.shape[0], batch_rows), 0)
        chosen = []
        for k in range(2):
            rank = jnp.sum(counts * hot[k], axis=0, keepdims=True).astype(jnp.int32)
            chosen.append(position == ids[k:k + 1, :] * capacity + rank)
        return chosen[0], chosen[1]

    def pack(micro):
        first, second = selections(micro)
        rows = pl.ds(micro * batch_rows, batch_rows)
        gate = gate_ref[:, rows].astype(F32)
        both_b = jnp.where(first | second, 1.0, 0.0).astype(BF16)
        gated = jnp.where(first, gate[0:1, :], jnp.where(second, gate[1:2, :], 0.0)).astype(BF16)
        dst = payloads[micro]
        dst[:, :width] = mm(both_b, x_ref[rows, :]).astype(BF16)
        dst[:, width:] = mm(gated, cot_ref[rows, :]).astype(BF16)

    def unpack(micro):
        first, second = selections(micro)
        both_b = jnp.where(first | second, 1.0, 0.0).astype(BF16)
        held = returns[micro][...]
        rows = pl.ds(micro * batch_rows, batch_rows)
        tg_ref[rows, :] = lax.dot_general(
            both_b, held[:, :width], CONTRACT_FIRST, preferred_element_type=F32
        ).astype(BF16)
        gate_sum = held[:, width:width + 1].astype(F32) + held[:, width + 1:width + 2].astype(F32)
        for index, chosen in enumerate((first, second)):
            gs_ref[index:index + 1, rows] = jnp.sum(
                jnp.where(chosen, gate_sum, 0.0), axis=0, keepdims=True
            )

    barrier = pltpu.get_barrier_semaphore()
    for k in range(1, n):
        peer = lax.rem(me + k, n)
        pl.semaphore_signal(barrier, inc=1, device_id=(row, peer), device_id_type=MESH)
    for k in range(1, n_row):
        peer = lax.rem(row + k, n_row)
        pl.semaphore_signal(barrier, inc=1, device_id=(peer, me), device_id_type=MESH)
    pack(0)
    pl.semaphore_wait(barrier, n - 1 + n_row - 1)

    def slot_rows(expert, phase):
        start = expert * capacity + (phase % splits) * piece
        return pl.ds(pl.multiple_of(start, piece), piece)

    def held_rows(source):
        return pl.ds(pl.multiple_of(source * piece, piece), piece)

    def scatter(phase, src_rows, dst_rows, src, dst, sem):
        pltpu.make_async_copy(src.at[src_rows(me)], dst.at[dst_rows(me)], recv_sem.at[sem]).start()
        for k in range(1, n):
            peer = lax.rem(me + k, n)
            pltpu.make_async_remote_copy(
                src_ref=src.at[src_rows(peer)],
                dst_ref=dst.at[dst_rows(me)],
                send_sem=send_sem.at[sem],
                recv_sem=recv_sem.at[sem],
                device_id=(row, peer),
                device_id_type=MESH,
            ).start()

    def send_forward(phase):
        scatter(phase, lambda e: slot_rows(e, phase), held_rows,
                payloads[phase // splits], recv.at[phase], phase)

    def send_back(phase):
        scatter(phase, held_rows, lambda e: slot_rows(e, phase),
                back.at[phase], returns[phase // splits], phases + phase)

    def wait_all(buf, sem):
        pltpu.make_async_copy(buf, buf, recv_sem.at[sem]).wait()

    def wait_sent(buf, sem):
        rest = pl.ds(0, (n - 1) * piece)
        pltpu.make_async_copy(buf.at[rest], buf.at[rest], send_sem.at[sem]).wait()

    side = SIDE
    col_a, col_b = row % side, row // side
    half = out_ref.shape[2] // 2

    def x_peer(k):
        return col_b * side + lax.rem(col_a + k, side)

    def y_peer(k):
        return lax.rem(col_b + k, side) * side + col_a

    def spread(src, dst, index, peer_of, sem):
        pltpu.make_async_copy(src.at[index], dst.at[index], rs_recv.at[sem]).start()
        for k in range(1, side):
            pltpu.make_async_remote_copy(
                src_ref=src.at[lax.rem(index + k, side)],
                dst_ref=dst.at[index],
                send_sem=rs_send.at[sem],
                recv_sem=rs_recv.at[sem],
                device_id=(peer_of(k), me),
                device_id_type=MESH,
            ).start()

    def scatter_grads():
        for block in range(n_row):
            rounded = grad_ref[:, block * part:(block + 1) * part, :].astype(BF16)
            round_a[block % side, block // side] = rounded[:, :, :half]
            round_b[block // side, block % side] = rounded[:, :, half:]
        spread(round_a, first_a, col_a, x_peer, 0)
        spread(round_b, first_b, col_b, y_peer, 1)

    def reduce_grads():
        pltpu.make_async_copy(first_a, first_a, rs_recv.at[0]).wait()
        total = first_a[0].astype(F32)
        for k in range(1, side):
            total = total + first_a[k].astype(F32)
        part_a[...] = total
        spread(part_a, second_a, col_b, y_peer, 2)
        pltpu.make_async_copy(first_b, first_b, rs_recv.at[1]).wait()
        total = first_b[0].astype(F32)
        for k in range(1, side):
            total = total + first_b[k].astype(F32)
        part_b[...] = total
        spread(part_b, second_b, col_a, x_peer, 3)
        for second, columns, sem in ((second_a, slice(0, half), 2),
                                     (second_b, slice(half, 2 * half), 3)):
            pltpu.make_async_copy(second, second, rs_recv.at[sem]).wait()
            total = second[0]
            for k in range(1, side):
                total = total + second[k]
            out_ref[:, :, columns] = total.astype(BF16)

    def compute(phase):
        held = recv.at[phase]
        rows_in = held[:, :width]
        scaled = held[:, width:]
        w_gate = w_ref[0]
        w_up = w_ref[1]
        w_down = w_ref[2]
        pre_gate = mm(rows_in, w_gate)
        pre_up = mm(rows_in, w_up)
        sigmoid_gate = jax.nn.sigmoid(pre_gate)
        activated = pre_gate * sigmoid_gate
        hidden = (activated * pre_up).astype(BF16)
        hidden_grad = mm(scaled, w_down)
        gate_sum = jnp.sum(hidden.astype(F32) * hidden_grad, axis=1, keepdims=True)
        grad_pre_gate = (
            hidden_grad * pre_up * sigmoid_gate * (1.0 + pre_gate * (1.0 - sigmoid_gate))
        ).astype(BF16)
        grad_pre_up = (hidden_grad * activated).astype(BF16)
        grads = (
            lax.dot_general(rows_in, grad_pre_gate, CONTRACT_FIRST, preferred_element_type=F32),
            lax.dot_general(rows_in, grad_pre_up, CONTRACT_FIRST, preferred_element_type=F32),
            lax.dot_general(scaled, hidden, CONTRACT_FIRST, preferred_element_type=F32),
        )
        for index, value in enumerate(grads):
            if phase == 0:
                grad_ref[index] = value
            else:
                grad_ref[index] += value
        if phase == phases - 1:
            scatter_grads()
        input_grad = (
            lax.dot_general(grad_pre_gate, w_gate, CONTRACT_LAST, preferred_element_type=F32)
            + lax.dot_general(grad_pre_up, w_up, CONTRACT_LAST, preferred_element_type=F32)
        ).astype(BF16)
        out = back.at[phase]
        out[:, :width] = input_grad
        high = gate_sum.astype(BF16).astype(F32)
        low = gate_sum - high
        column = lax.broadcasted_iota(jnp.int32, (input_grad.shape[0], PAD), 1)
        tail = jnp.where(column == 0, high, jnp.where(column == 1, low, 0.0))
        out[:, width:] = tail.astype(BF16)

    send_forward(0)
    pack(1)
    for phase in range(phases):
        wait_all(recv.at[phase], phase)
        if phase + 1 < phases:
            send_forward(phase + 1)
        compute(phase)
        send_back(phase)

    wait_all(back.at[0], phases)
    unpack(0)
    reduce_grads()

    for phase in range(phases):
        if phase > 0:
            wait_all(back.at[phase], phases + phase)
            unpack(phase)
        wait_sent(recv.at[phase], phase)
        wait_sent(back.at[phase], phases + phase)
    gg_ref[...] = (gs_ref[...] / gate_ref[...].astype(F32)).astype(BF16)
    rest = pl.ds(0, side - 1)
    for sem, buf in enumerate((first_a, first_b, second_a, second_b)):
        pltpu.make_async_copy(buf.at[rest], buf.at[rest], rs_send.at[sem]).wait()


def exchange(slots, tokens, cotangent, gates, weights, n_row, capacity):
    n_expert = lax.axis_size("expert")
    rows = n_expert * capacity
    width = weights.shape[1]
    full = 2 * width
    part = width // n_row
    back = (rows, width + PAD)
    share = (weights.shape[0], part, weights.shape[2])
    quarter = (weights.shape[0], part, weights.shape[2] // 2)
    phases = MICRO
    vmem = pl.BlockSpec(memory_space=pltpu.VMEM)
    return pl.pallas_call(
        exchange_kernel,
        out_shape=(
            jax.ShapeDtypeStruct(share, BF16),
            jax.ShapeDtypeStruct(tokens.shape, BF16),
            jax.ShapeDtypeStruct((2, tokens.shape[0]), BF16),
        ),
        in_specs=[vmem] * 5,
        out_specs=(vmem, vmem, vmem),
        scratch_shapes=[
            pltpu.VMEM((2, tokens.shape[0]), F32),
            pltpu.VMEM((rows, full), BF16),
            pltpu.VMEM((rows, full), BF16),
            pltpu.VMEM(back, BF16),
            pltpu.VMEM(back, BF16),
            pltpu.VMEM((phases, rows, full), BF16),
            pltpu.VMEM((phases,) + back, BF16),
            pltpu.VMEM(weights.shape, F32),
            pltpu.VMEM((SIDE, SIDE) + quarter, BF16),
            pltpu.VMEM((SIDE, SIDE) + quarter, BF16),
            pltpu.VMEM((SIDE, SIDE) + quarter, BF16),
            pltpu.VMEM((SIDE, SIDE) + quarter, BF16),
            pltpu.VMEM((SIDE,) + quarter, F32),
            pltpu.VMEM((SIDE,) + quarter, F32),
            pltpu.VMEM((SIDE,) + quarter, F32),
            pltpu.VMEM((SIDE,) + quarter, F32),
            pltpu.SemaphoreType.DMA((2 * phases,)),
            pltpu.SemaphoreType.DMA((2 * phases,)),
            pltpu.SemaphoreType.DMA((4,)),
            pltpu.SemaphoreType.DMA((4,)),
        ],
        compiler_params=pltpu.CompilerParams(
            collective_id=0, has_side_effects=True, vmem_limit_bytes=62 * 1024 * 1024
        ),
    )(slots, tokens, cotangent, gates, weights)


def route_slot_rows(ids_block, expert_count, capacity):
    flat_ids = ids_block.reshape(-1)
    one_hot = (flat_ids[:, None] == jnp.arange(expert_count, dtype=jnp.int32)[None, :]).astype(
        jnp.int32
    )
    earlier = jnp.cumsum(one_hot, axis=0) - one_hot
    rank_slot = jnp.sum(earlier * one_hot, axis=1)
    return (flat_ids * capacity + rank_slot).reshape(-1, 2).T


def on_device(tokens, cotangent, gates, expert_ids, expert_weights):
    n_expert = lax.axis_size("expert")
    expert_count = n_expert * expert_weights.shape[0]
    batch_rows = tokens.shape[0] // MICRO
    capacity = max(2, 4 * batch_rows // expert_count)
    weights_grad, token_grad, gate_grad = exchange(
        expert_ids.T, tokens, cotangent, gates.T, expert_weights[0],
        lax.axis_size("dp"), capacity,
    )
    return token_grad, gate_grad.T, weights_grad[None]


def solution(mesh):
    placed = (
        P(("dp", "expert"), None),
        P(("dp", "expert"), None),
        P(("dp", "expert"), None),
        P(("dp", "expert"), None),
        P("expert", None, None, None),
    )
    return jax.shard_map(
        on_device,
        mesh=mesh,
        in_specs=placed,
        out_specs=(
            P(("dp", "expert"), None),
            P(("dp", "expert"), None),
            P("expert", None, "dp", None),
        ),
        check_vma=False,
    )
```

```python
import jax
import jax.numpy as jnp
from jax import lax
from jax.experimental import pallas as pl
from jax.experimental.pallas import tpu as pltpu
from jax.sharding import PartitionSpec as P

MICRO = 2
SPLITS = 1
SIDE = 4
PAD = 128

F32 = jnp.float32
BF16 = jnp.bfloat16

CONTRACT_LAST = (((1,), (1,)), ((), ()))
CONTRACT_FIRST = (((0,), (0,)), ((), ()))
MESH = pl.DeviceIdType.MESH


def mm(a, b):
    return jnp.dot(a, b, preferred_element_type=F32)


def route_masks(ids_block, expert_count, capacity):
    flat_ids = ids_block.reshape(-1)
    one_hot = (flat_ids[:, None] == jnp.arange(expert_count, dtype=jnp.int32)[None, :]).astype(
        jnp.int32
    )
    earlier = jnp.cumsum(one_hot, axis=0) - one_hot
    rank_slot = jnp.sum(earlier * one_hot, axis=1)
    route_slot = (flat_ids * capacity + rank_slot).reshape(-1, 2)
    position = jnp.arange(expert_count * capacity, dtype=jnp.int32)[:, None]
    return position == route_slot[None, :, 0], position == route_slot[None, :, 1]


def expert_step(recv, w_gate, w_up, w_down, width):
    rows_in = recv[:, :width]
    scaled = recv[:, width:]
    pre_gate = mm(rows_in, w_gate)
    pre_up = mm(rows_in, w_up)
    sigmoid_gate = jax.nn.sigmoid(pre_gate)
    activated = pre_gate * sigmoid_gate
    hidden = (activated * pre_up).astype(BF16)
    hidden_grad = mm(scaled, w_down)
    gate_sum = jnp.sum(hidden.astype(F32) * hidden_grad, axis=1)
    grad_pre_gate = (
        hidden_grad * pre_up * sigmoid_gate * (1.0 + pre_gate * (1.0 - sigmoid_gate))
    ).astype(BF16)
    grad_pre_up = (hidden_grad * activated).astype(BF16)
    input_grad = (
        lax.dot_general(grad_pre_gate, w_gate, CONTRACT_LAST, preferred_element_type=F32)
        + lax.dot_general(grad_pre_up, w_up, CONTRACT_LAST, preferred_element_type=F32)
    ).astype(BF16)
    grads = (
        lax.dot_general(rows_in, grad_pre_gate, CONTRACT_FIRST, preferred_element_type=F32),
        lax.dot_general(rows_in, grad_pre_up, CONTRACT_FIRST, preferred_element_type=F32),
        lax.dot_general(scaled, hidden, CONTRACT_FIRST, preferred_element_type=F32),
    )
    high = gate_sum.astype(BF16)
    low = (gate_sum - high.astype(F32)).astype(BF16)
    tail = jnp.concatenate(
        [high[:, None], low[:, None], jnp.zeros((recv.shape[0], PAD - 2), BF16)], axis=1
    )
    return jnp.concatenate([input_grad, tail], axis=1), grads


def exchange_kernel(ids_ref, x_ref, cot_ref, gate_ref, w_ref, out_ref, tg_ref, gs_ref,
                    p0, p1, ret0, ret1, recv, back, grad_ref, round_a, round_b, first_a, first_b,
                    part_a, part_b, second_a, second_b, send_sem, recv_sem, rs_send, rs_recv):
    n = lax.axis_size("expert")
    me = lax.axis_index("expert")
    n_row = lax.axis_size("dp")
    row = lax.axis_index("dp")
    phases = recv.shape[0]
    splits = phases // MICRO
    capacity = p0.shape[0] // n
    batch_rows = x_ref.shape[0] // MICRO
    n_experts = n * (p0.shape[0] // n // capacity)
    piece = capacity // splits
    width = w_ref.shape[1]
    part = out_ref.shape[1]
    payloads = (p0, p1)
    returns = (ret0, ret1)

    def selections(micro):
        rows = pl.ds(micro * batch_rows, batch_rows)
        ids = ids_ref[:, rows]
        expert = lax.broadcasted_iota(jnp.int32, (n_experts, batch_rows), 0)
        hot = [jnp.where(expert == ids[k:k + 1, :], 1.0, 0.0) for k in range(2)]
        before = lax.broadcasted_iota(jnp.int32, (batch_rows, batch_rows), 0)
        after = lax.broadcasted_iota(jnp.int32, (batch_rows, batch_rows), 1)
        earlier = jnp.where(before < after, 1.0, 0.0).astype(BF16)
        counts = mm((hot[0] + hot[1]).astype(BF16), earlier)
        position = lax.broadcasted_iota(jnp.int32, (p0.shape[0], batch_rows), 0)
        chosen = []
        for k in range(2):
            rank = jnp.sum(counts * hot[k], axis=0, keepdims=True).astype(jnp.int32)
            chosen.append(position == ids[k:k + 1, :] * capacity + rank)
        return chosen[0], chosen[1]

    def pack(micro):
        first, second = selections(micro)
        rows = pl.ds(micro * batch_rows, batch_rows)
        gate = gate_ref[:, rows].astype(F32)
        both_b = jnp.where(first | second, 1.0, 0.0).astype(BF16)
        gated = jnp.where(first, gate[0:1, :], jnp.where(second, gate[1:2, :], 0.0)).astype(BF16)
        dst = payloads[micro]
        dst[:, :width] = mm(both_b, x_ref[rows, :]).astype(BF16)
        dst[:, width:] = mm(gated, cot_ref[rows, :]).astype(BF16)

    def unpack(micro):
        first, second = selections(micro)
        both_b = jnp.where(first | second, 1.0, 0.0).astype(BF16)
        held = returns[micro][...]
        rows = pl.ds(micro * batch_rows, batch_rows)
        tg_ref[rows, :] = lax.dot_general(
            both_b, held[:, :width], CONTRACT_FIRST, preferred_element_type=F32
        ).astype(BF16)
        gate_sum = held[:, width:width + 1].astype(F32) + held[:, width + 1:width + 2].astype(F32)
        for index, chosen in enumerate((first, second)):
            gs_ref[index:index + 1, rows] = jnp.sum(
                jnp.where(chosen, gate_sum, 0.0), axis=0, keepdims=True
            )

    barrier = pltpu.get_barrier_semaphore()
    for k in range(1, n):
        peer = lax.rem(me + k, n)
        pl.semaphore_signal(barrier, inc=1, device_id=(row, peer), device_id_type=MESH)
    for k in range(1, n_row):
        peer = lax.rem(row + k, n_row)
        pl.semaphore_signal(barrier, inc=1, device_id=(peer, me), device_id_type=MESH)
    pack(0)
    pl.semaphore_wait(barrier, n - 1 + n_row - 1)

    def slot_rows(expert, phase):
        start = expert * capacity + (phase % splits) * piece
        return pl.ds(pl.multiple_of(start, piece), piece)

    def held_rows(source):
        return pl.ds(pl.multiple_of(source * piece, piece), piece)

    def scatter(phase, src_rows, dst_rows, src, dst, sem):
        pltpu.make_async_copy(src.at[src_rows(me)], dst.at[dst_rows(me)], recv_sem.at[sem]).start()
        for k in sorted(range(1, n), key=lambda k: -min(k, n - k)):
            peer = lax.rem(me + k, n)
            pltpu.make_async_remote_copy(
                src_ref=src.at[src_rows(peer)],
                dst_ref=dst.at[dst_rows(me)],
                send_sem=send_sem.at[sem],
                recv_sem=recv_sem.at[sem],
                device_id=(row, peer),
                device_id_type=MESH,
            ).start()

    def send_forward(phase):
        scatter(phase, lambda e: slot_rows(e, phase), held_rows,
                payloads[phase // splits], recv.at[phase], phase)

    def send_back(phase):
        scatter(phase, held_rows, lambda e: slot_rows(e, phase),
                back.at[phase], returns[phase // splits], phases + phase)

    def wait_all(buf, sem):
        pltpu.make_async_copy(buf, buf, recv_sem.at[sem]).wait()

    def wait_sent(buf, sem):
        rest = pl.ds(0, (n - 1) * piece)
        pltpu.make_async_copy(buf.at[rest], buf.at[rest], send_sem.at[sem]).wait()

    side = SIDE
    col_a, col_b = row % side, row // side
    half = out_ref.shape[2] // 2

    def x_peer(k):
        return col_b * side + lax.rem(col_a + k, side)

    def y_peer(k):
        return lax.rem(col_b + k, side) * side + col_a

    def spread(src, dst, index, peer_of, sem):
        pltpu.make_async_copy(src.at[index], dst.at[index], rs_recv.at[sem]).start()
        for k in range(1, side):
            pltpu.make_async_remote_copy(
                src_ref=src.at[lax.rem(index + k, side)],
                dst_ref=dst.at[index],
                send_sem=rs_send.at[sem],
                recv_sem=rs_recv.at[sem],
                device_id=(peer_of(k), me),
                device_id_type=MESH,
            ).start()

    def scatter_grads():
        for block in range(n_row):
            rounded = grad_ref[:, block * part:(block + 1) * part, :].astype(BF16)
            round_a[block % side, block // side] = rounded[:, :, :half]
            round_b[block // side, block % side] = rounded[:, :, half:]
        spread(round_a, first_a, col_a, x_peer, 0)
        spread(round_b, first_b, col_b, y_peer, 1)

    def reduce_grads():
        pltpu.make_async_copy(first_a, first_a, rs_recv.at[0]).wait()
        total = first_a[0].astype(F32)
        for k in range(1, side):
            total = total + first_a[k].astype(F32)
        part_a[...] = total
        spread(part_a, second_a, col_b, y_peer, 2)
        pltpu.make_async_copy(first_b, first_b, rs_recv.at[1]).wait()
        total = first_b[0].astype(F32)
        for k in range(1, side):
            total = total + first_b[k].astype(F32)
        part_b[...] = total
        spread(part_b, second_b, col_a, x_peer, 3)
        for second, columns, sem in ((second_a, slice(0, half), 2),
                                     (second_b, slice(half, 2 * half), 3)):
            pltpu.make_async_copy(second, second, rs_recv.at[sem]).wait()
            total = second[0]
            for k in range(1, side):
                total = total + second[k]
            out_ref[:, :, columns] = total.astype(BF16)

    def compute(phase):
        held = recv.at[phase]
        rows_in = held[:, :width]
        scaled = held[:, width:]
        w_gate = w_ref[0]
        w_up = w_ref[1]
        w_down = w_ref[2]
        pre_gate = mm(rows_in, w_gate)
        pre_up = mm(rows_in, w_up)
        sigmoid_gate = jax.nn.sigmoid(pre_gate)
        activated = pre_gate * sigmoid_gate
        hidden = (activated * pre_up).astype(BF16)
        hidden_grad = mm(scaled, w_down)
        gate_sum = jnp.sum(hidden.astype(F32) * hidden_grad, axis=1, keepdims=True)
        grad_pre_gate = (
            hidden_grad * pre_up * sigmoid_gate * (1.0 + pre_gate * (1.0 - sigmoid_gate))
        ).astype(BF16)
        grad_pre_up = (hidden_grad * activated).astype(BF16)
        grads = (
            lax.dot_general(rows_in, grad_pre_gate, CONTRACT_FIRST, preferred_element_type=F32),
            lax.dot_general(rows_in, grad_pre_up, CONTRACT_FIRST, preferred_element_type=F32),
            lax.dot_general(scaled, hidden, CONTRACT_FIRST, preferred_element_type=F32),
        )
        for index, value in enumerate(grads):
            if phase == 0:
                grad_ref[index] = value
            else:
                grad_ref[index] += value
        if phase == phases - 1:
            scatter_grads()
        input_grad = (
            lax.dot_general(grad_pre_gate, w_gate, CONTRACT_LAST, preferred_element_type=F32)
            + lax.dot_general(grad_pre_up, w_up, CONTRACT_LAST, preferred_element_type=F32)
        ).astype(BF16)
        out = back.at[phase]
        out[:, :width] = input_grad
        high = gate_sum.astype(BF16).astype(F32)
        low = gate_sum - high
        column = lax.broadcasted_iota(jnp.int32, (input_grad.shape[0], PAD), 1)
        tail = jnp.where(column == 0, high, jnp.where(column == 1, low, 0.0))
        out[:, width:] = tail.astype(BF16)

    send_forward(0)
    pack(1)
    for phase in range(phases):
        wait_all(recv.at[phase], phase)
        if phase + 1 < phases:
            send_forward(phase + 1)
        compute(phase)
        send_back(phase)

    wait_all(back.at[0], phases)
    unpack(0)
    reduce_grads()

    for phase in range(phases):
        if phase > 0:
            wait_all(back.at[phase], phases + phase)
            unpack(phase)
        wait_sent(recv.at[phase], phase)
        wait_sent(back.at[phase], phases + phase)
    rest = pl.ds(0, side - 1)
    for sem, buf in enumerate((first_a, first_b, second_a, second_b)):
        pltpu.make_async_copy(buf.at[rest], buf.at[rest], rs_send.at[sem]).wait()


def exchange(slots, tokens, cotangent, gates, weights, n_row, capacity):
    n_expert = lax.axis_size("expert")
    rows = n_expert * capacity
    width = weights.shape[1]
    full = 2 * width
    part = width // n_row
    back = (rows, width + PAD)
    share = (weights.shape[0], part, weights.shape[2])
    quarter = (weights.shape[0], part, weights.shape[2] // 2)
    phases = MICRO
    vmem = pl.BlockSpec(memory_space=pltpu.VMEM)
    return pl.pallas_call(
        exchange_kernel,
        out_shape=(
            jax.ShapeDtypeStruct(share, BF16),
            jax.ShapeDtypeStruct(tokens.shape, BF16),
            jax.ShapeDtypeStruct((2, tokens.shape[0]), F32),
        ),
        in_specs=[vmem] * 5,
        out_specs=(vmem, vmem, vmem),
        scratch_shapes=[
            pltpu.VMEM((rows, full), BF16),
            pltpu.VMEM((rows, full), BF16),
            pltpu.VMEM(back, BF16),
            pltpu.VMEM(back, BF16),
            pltpu.VMEM((phases, rows, full), BF16),
            pltpu.VMEM((phases,) + back, BF16),
            pltpu.VMEM(weights.shape, F32),
            pltpu.VMEM((SIDE, SIDE) + quarter, BF16),
            pltpu.VMEM((SIDE, SIDE) + quarter, BF16),
            pltpu.VMEM((SIDE, SIDE) + quarter, BF16),
            pltpu.VMEM((SIDE, SIDE) + quarter, BF16),
            pltpu.VMEM((SIDE,) + quarter, F32),
            pltpu.VMEM((SIDE,) + quarter, F32),
            pltpu.VMEM((SIDE,) + quarter, F32),
            pltpu.VMEM((SIDE,) + quarter, F32),
            pltpu.SemaphoreType.DMA((2 * phases,)),
            pltpu.SemaphoreType.DMA((2 * phases,)),
            pltpu.SemaphoreType.DMA((4,)),
            pltpu.SemaphoreType.DMA((4,)),
        ],
        compiler_params=pltpu.CompilerParams(
            collective_id=0, has_side_effects=True, vmem_limit_bytes=62 * 1024 * 1024
        ),
    )(slots, tokens, cotangent, gates, weights)


def route_slot_rows(ids_block, expert_count, capacity):
    flat_ids = ids_block.reshape(-1)
    one_hot = (flat_ids[:, None] == jnp.arange(expert_count, dtype=jnp.int32)[None, :]).astype(
        jnp.int32
    )
    earlier = jnp.cumsum(one_hot, axis=0) - one_hot
    rank_slot = jnp.sum(earlier * one_hot, axis=1)
    return (flat_ids * capacity + rank_slot).reshape(-1, 2).T


def on_device(tokens, cotangent, gates, expert_ids, expert_weights):
    n_expert = lax.axis_size("expert")
    expert_count = n_expert * expert_weights.shape[0]
    batch_rows = tokens.shape[0] // MICRO
    capacity = max(2, 4 * batch_rows // expert_count)
    gate = gates.T.astype(F32)
    weights_grad, token_grad, gate_sums = exchange(
        expert_ids.T, tokens, cotangent, gates.T, expert_weights[0],
        lax.axis_size("dp"), capacity,
    )
    return token_grad, (gate_sums / gate).astype(BF16).T, weights_grad[None]


def solution(mesh):
    placed = (
        P(("dp", "expert"), None),
        P(("dp", "expert"), None),
        P(("dp", "expert"), None),
        P(("dp", "expert"), None),
        P("expert", None, None, None),
    )
    return jax.shard_map(
        on_device,
        mesh=mesh,
        in_specs=placed,
        out_specs=(
            P(("dp", "expert"), None),
            P(("dp", "expert"), None),
            P("expert", None, "dp", None),
        ),
        check_vma=False,
    )
```

```python
import jax
import jax.numpy as jnp
from jax import lax
from jax.experimental import pallas as pl
from jax.experimental.pallas import tpu as pltpu
from jax.sharding import PartitionSpec as P

MICRO = 2
SPLITS = 1
SIDE = 4
PAD = 128

F32 = jnp.float32
BF16 = jnp.bfloat16

CONTRACT_LAST = (((1,), (1,)), ((), ()))
CONTRACT_FIRST = (((0,), (0,)), ((), ()))
MESH = pl.DeviceIdType.MESH


def mm(a, b):
    return jnp.dot(a, b, preferred_element_type=F32)


def route_masks(ids_block, expert_count, capacity):
    flat_ids = ids_block.reshape(-1)
    one_hot = (flat_ids[:, None] == jnp.arange(expert_count, dtype=jnp.int32)[None, :]).astype(
        jnp.int32
    )
    earlier = jnp.cumsum(one_hot, axis=0) - one_hot
    rank_slot = jnp.sum(earlier * one_hot, axis=1)
    route_slot = (flat_ids * capacity + rank_slot).reshape(-1, 2)
    position = jnp.arange(expert_count * capacity, dtype=jnp.int32)[:, None]
    return position == route_slot[None, :, 0], position == route_slot[None, :, 1]


def expert_step(recv, w_gate, w_up, w_down, width):
    rows_in = recv[:, :width]
    scaled = recv[:, width:]
    pre_gate = mm(rows_in, w_gate)
    pre_up = mm(rows_in, w_up)
    sigmoid_gate = jax.nn.sigmoid(pre_gate)
    activated = pre_gate * sigmoid_gate
    hidden = (activated * pre_up).astype(BF16)
    hidden_grad = mm(scaled, w_down)
    gate_sum = jnp.sum(hidden.astype(F32) * hidden_grad, axis=1)
    grad_pre_gate = (
        hidden_grad * pre_up * sigmoid_gate * (1.0 + pre_gate * (1.0 - sigmoid_gate))
    ).astype(BF16)
    grad_pre_up = (hidden_grad * activated).astype(BF16)
    input_grad = (
        lax.dot_general(grad_pre_gate, w_gate, CONTRACT_LAST, preferred_element_type=F32)
        + lax.dot_general(grad_pre_up, w_up, CONTRACT_LAST, preferred_element_type=F32)
    ).astype(BF16)
    grads = (
        lax.dot_general(rows_in, grad_pre_gate, CONTRACT_FIRST, preferred_element_type=F32),
        lax.dot_general(rows_in, grad_pre_up, CONTRACT_FIRST, preferred_element_type=F32),
        lax.dot_general(scaled, hidden, CONTRACT_FIRST, preferred_element_type=F32),
    )
    high = gate_sum.astype(BF16)
    low = (gate_sum - high.astype(F32)).astype(BF16)
    tail = jnp.concatenate(
        [high[:, None], low[:, None], jnp.zeros((recv.shape[0], PAD - 2), BF16)], axis=1
    )
    return jnp.concatenate([input_grad, tail], axis=1), grads


def exchange_kernel(ids_ref, x_ref, cot_ref, gate_ref, w_ref, out_hbm, tg_hbm, gs_ref,
                    out_ref, tg_ref, out_sem, p0, p1, ret0, ret1, recv, back, grad_ref, round_a, round_b, first_a, first_b,
                    part_a, part_b, second_a, second_b, send_sem, recv_sem, rs_send, rs_recv):
    n = lax.axis_size("expert")
    me = lax.axis_index("expert")
    n_row = lax.axis_size("dp")
    row = lax.axis_index("dp")
    phases = recv.shape[0]
    splits = phases // MICRO
    capacity = p0.shape[0] // n
    batch_rows = x_ref.shape[0] // MICRO
    n_experts = n * (p0.shape[0] // n // capacity)
    piece = capacity // splits
    width = w_ref.shape[1]
    part = out_ref.shape[1]
    payloads = (p0, p1)
    returns = (ret0, ret1)

    def selections(micro):
        rows = pl.ds(micro * batch_rows, batch_rows)
        ids = ids_ref[:, rows]
        expert = lax.broadcasted_iota(jnp.int32, (n_experts, batch_rows), 0)
        hot = [jnp.where(expert == ids[k:k + 1, :], 1.0, 0.0) for k in range(2)]
        before = lax.broadcasted_iota(jnp.int32, (batch_rows, batch_rows), 0)
        after = lax.broadcasted_iota(jnp.int32, (batch_rows, batch_rows), 1)
        earlier = jnp.where(before < after, 1.0, 0.0).astype(BF16)
        counts = mm((hot[0] + hot[1]).astype(BF16), earlier)
        position = lax.broadcasted_iota(jnp.int32, (p0.shape[0], batch_rows), 0)
        chosen = []
        for k in range(2):
            rank = jnp.sum(counts * hot[k], axis=0, keepdims=True).astype(jnp.int32)
            chosen.append(position == ids[k:k + 1, :] * capacity + rank)
        return chosen[0], chosen[1]

    def pack(micro):
        first, second = selections(micro)
        rows = pl.ds(micro * batch_rows, batch_rows)
        gate = gate_ref[:, rows].astype(F32)
        both_b = jnp.where(first | second, 1.0, 0.0).astype(BF16)
        gated = jnp.where(first, gate[0:1, :], jnp.where(second, gate[1:2, :], 0.0)).astype(BF16)
        dst = payloads[micro]
        dst[:, :width] = mm(both_b, x_ref[rows, :]).astype(BF16)
        dst[:, width:] = mm(gated, cot_ref[rows, :]).astype(BF16)

    def unpack(micro):
        first, second = selections(micro)
        both_b = jnp.where(first | second, 1.0, 0.0).astype(BF16)
        held = returns[micro][...]
        rows = pl.ds(micro * batch_rows, batch_rows)
        tg_ref[rows, :] = lax.dot_general(
            both_b, held[:, :width], CONTRACT_FIRST, preferred_element_type=F32
        ).astype(BF16)
        gate_sum = held[:, width:width + 1].astype(F32) + held[:, width + 1:width + 2].astype(F32)
        for index, chosen in enumerate((first, second)):
            gs_ref[index:index + 1, rows] = jnp.sum(
                jnp.where(chosen, gate_sum, 0.0), axis=0, keepdims=True
            )

    barrier = pltpu.get_barrier_semaphore()
    for k in range(1, n):
        peer = lax.rem(me + k, n)
        pl.semaphore_signal(barrier, inc=1, device_id=(row, peer), device_id_type=MESH)
    for k in range(1, n_row):
        peer = lax.rem(row + k, n_row)
        pl.semaphore_signal(barrier, inc=1, device_id=(peer, me), device_id_type=MESH)
    pack(0)
    pl.semaphore_wait(barrier, n - 1 + n_row - 1)

    def slot_rows(expert, phase):
        start = expert * capacity + (phase % splits) * piece
        return pl.ds(pl.multiple_of(start, piece), piece)

    def held_rows(source):
        return pl.ds(pl.multiple_of(source * piece, piece), piece)

    def scatter(phase, src_rows, dst_rows, src, dst, sem):
        pltpu.make_async_copy(src.at[src_rows(me)], dst.at[dst_rows(me)], recv_sem.at[sem]).start()
        for k in range(1, n):
            peer = lax.rem(me + k, n)
            pltpu.make_async_remote_copy(
                src_ref=src.at[src_rows(peer)],
                dst_ref=dst.at[dst_rows(me)],
                send_sem=send_sem.at[sem],
                recv_sem=recv_sem.at[sem],
                device_id=(row, peer),
                device_id_type=MESH,
            ).start()

    def send_forward(phase):
        scatter(phase, lambda e: slot_rows(e, phase), held_rows,
                payloads[phase // splits], recv.at[phase], phase)

    def send_back(phase):
        scatter(phase, held_rows, lambda e: slot_rows(e, phase),
                back.at[phase], returns[phase // splits], phases + phase)

    def wait_all(buf, sem):
        pltpu.make_async_copy(buf, buf, recv_sem.at[sem]).wait()

    def wait_sent(buf, sem):
        rest = pl.ds(0, (n - 1) * piece)
        pltpu.make_async_copy(buf.at[rest], buf.at[rest], send_sem.at[sem]).wait()

    side = SIDE
    col_a, col_b = row % side, row // side
    half = out_ref.shape[2] // 2

    def x_peer(k):
        return col_b * side + lax.rem(col_a + k, side)

    def y_peer(k):
        return lax.rem(col_b + k, side) * side + col_a

    def spread(src, dst, index, peer_of, sem):
        pltpu.make_async_copy(src.at[index], dst.at[index], rs_recv.at[sem]).start()
        for k in range(1, side):
            pltpu.make_async_remote_copy(
                src_ref=src.at[lax.rem(index + k, side)],
                dst_ref=dst.at[index],
                send_sem=rs_send.at[sem],
                recv_sem=rs_recv.at[sem],
                device_id=(peer_of(k), me),
                device_id_type=MESH,
            ).start()

    def scatter_grads():
        for block in range(n_row):
            rounded = grad_ref[:, block * part:(block + 1) * part, :].astype(BF16)
            round_a[block % side, block // side] = rounded[:, :, :half]
            round_b[block // side, block % side] = rounded[:, :, half:]
        spread(round_a, first_a, col_a, x_peer, 0)
        spread(round_b, first_b, col_b, y_peer, 1)

    def reduce_grads():
        pltpu.make_async_copy(first_a, first_a, rs_recv.at[0]).wait()
        total = first_a[0].astype(F32)
        for k in range(1, side):
            total = total + first_a[k].astype(F32)
        part_a[...] = total
        spread(part_a, second_a, col_b, y_peer, 2)
        pltpu.make_async_copy(first_b, first_b, rs_recv.at[1]).wait()
        total = first_b[0].astype(F32)
        for k in range(1, side):
            total = total + first_b[k].astype(F32)
        part_b[...] = total
        spread(part_b, second_b, col_a, x_peer, 3)
        for second, columns, sem in ((second_a, slice(0, half), 2),
                                     (second_b, slice(half, 2 * half), 3)):
            pltpu.make_async_copy(second, second, rs_recv.at[sem]).wait()
            total = second[0]
            for k in range(1, side):
                total = total + second[k]
            out_ref[:, :, columns] = total.astype(BF16)

    def compute(phase):
        held = recv.at[phase]
        rows_in = held[:, :width]
        scaled = held[:, width:]
        w_gate = w_ref[0]
        w_up = w_ref[1]
        w_down = w_ref[2]
        pre_gate = mm(rows_in, w_gate)
        pre_up = mm(rows_in, w_up)
        sigmoid_gate = jax.nn.sigmoid(pre_gate)
        activated = pre_gate * sigmoid_gate
        hidden = (activated * pre_up).astype(BF16)
        hidden_grad = mm(scaled, w_down)
        gate_sum = jnp.sum(hidden.astype(F32) * hidden_grad, axis=1, keepdims=True)
        grad_pre_gate = (
            hidden_grad * pre_up * sigmoid_gate * (1.0 + pre_gate * (1.0 - sigmoid_gate))
        ).astype(BF16)
        grad_pre_up = (hidden_grad * activated).astype(BF16)
        grads = (
            lax.dot_general(rows_in, grad_pre_gate, CONTRACT_FIRST, preferred_element_type=F32),
            lax.dot_general(rows_in, grad_pre_up, CONTRACT_FIRST, preferred_element_type=F32),
            lax.dot_general(scaled, hidden, CONTRACT_FIRST, preferred_element_type=F32),
        )
        for index, value in enumerate(grads):
            if phase == 0:
                grad_ref[index] = value
            else:
                grad_ref[index] += value
        if phase == phases - 1:
            scatter_grads()
        input_grad = (
            lax.dot_general(grad_pre_gate, w_gate, CONTRACT_LAST, preferred_element_type=F32)
            + lax.dot_general(grad_pre_up, w_up, CONTRACT_LAST, preferred_element_type=F32)
        ).astype(BF16)
        out = back.at[phase]
        out[:, :width] = input_grad
        high = gate_sum.astype(BF16).astype(F32)
        low = gate_sum - high
        column = lax.broadcasted_iota(jnp.int32, (input_grad.shape[0], PAD), 1)
        tail = jnp.where(column == 0, high, jnp.where(column == 1, low, 0.0))
        out[:, width:] = tail.astype(BF16)

    send_forward(0)
    pack(1)
    for phase in range(phases):
        wait_all(recv.at[phase], phase)
        if phase + 1 < phases:
            send_forward(phase + 1)
        compute(phase)
        send_back(phase)

    wait_all(back.at[0], phases)
    unpack(0)
    reduce_grads()

    for phase in range(phases):
        if phase > 0:
            wait_all(back.at[phase], phases + phase)
            unpack(phase)
        wait_sent(recv.at[phase], phase)
        wait_sent(back.at[phase], phases + phase)
    results = [
        pltpu.make_async_copy(src, dst, out_sem.at[index])
        for index, (src, dst) in enumerate(((out_ref, out_hbm), (tg_ref, tg_hbm)))
    ]
    for copy in results:
        copy.start()
    rest = pl.ds(0, side - 1)
    for sem, buf in enumerate((first_a, first_b, second_a, second_b)):
        pltpu.make_async_copy(buf.at[rest], buf.at[rest], rs_send.at[sem]).wait()
    for copy in results:
        copy.wait()


def exchange(slots, tokens, cotangent, gates, weights, n_row, capacity):
    n_expert = lax.axis_size("expert")
    rows = n_expert * capacity
    width = weights.shape[1]
    full = 2 * width
    part = width // n_row
    back = (rows, width + PAD)
    share = (weights.shape[0], part, weights.shape[2])
    quarter = (weights.shape[0], part, weights.shape[2] // 2)
    phases = MICRO
    vmem = pl.BlockSpec(memory_space=pltpu.VMEM)
    return pl.pallas_call(
        exchange_kernel,
        out_shape=(
            jax.ShapeDtypeStruct(share, BF16),
            jax.ShapeDtypeStruct(tokens.shape, BF16),
            jax.ShapeDtypeStruct((2, tokens.shape[0]), F32),
        ),
        in_specs=[vmem] * 5,
        out_specs=(
            pl.BlockSpec(memory_space=pl.ANY),
            pl.BlockSpec(memory_space=pl.ANY),
            vmem,
        ),
        scratch_shapes=[
            pltpu.VMEM(share, BF16),
            pltpu.VMEM(tokens.shape, BF16),
            pltpu.SemaphoreType.DMA((2,)),
            pltpu.VMEM((rows, full), BF16),
            pltpu.VMEM((rows, full), BF16),
            pltpu.VMEM(back, BF16),
            pltpu.VMEM(back, BF16),
            pltpu.VMEM((phases, rows, full), BF16),
            pltpu.VMEM((phases,) + back, BF16),
            pltpu.VMEM(weights.shape, F32),
            pltpu.VMEM((SIDE, SIDE) + quarter, BF16),
            pltpu.VMEM((SIDE, SIDE) + quarter, BF16),
            pltpu.VMEM((SIDE, SIDE) + quarter, BF16),
            pltpu.VMEM((SIDE, SIDE) + quarter, BF16),
            pltpu.VMEM((SIDE,) + quarter, F32),
            pltpu.VMEM((SIDE,) + quarter, F32),
            pltpu.VMEM((SIDE,) + quarter, F32),
            pltpu.VMEM((SIDE,) + quarter, F32),
            pltpu.SemaphoreType.DMA((2 * phases,)),
            pltpu.SemaphoreType.DMA((2 * phases,)),
            pltpu.SemaphoreType.DMA((4,)),
            pltpu.SemaphoreType.DMA((4,)),
        ],
        compiler_params=pltpu.CompilerParams(
            collective_id=0, has_side_effects=True, vmem_limit_bytes=62 * 1024 * 1024
        ),
    )(slots, tokens, cotangent, gates, weights)


def route_slot_rows(ids_block, expert_count, capacity):
    flat_ids = ids_block.reshape(-1)
    one_hot = (flat_ids[:, None] == jnp.arange(expert_count, dtype=jnp.int32)[None, :]).astype(
        jnp.int32
    )
    earlier = jnp.cumsum(one_hot, axis=0) - one_hot
    rank_slot = jnp.sum(earlier * one_hot, axis=1)
    return (flat_ids * capacity + rank_slot).reshape(-1, 2).T


def on_device(tokens, cotangent, gates, expert_ids, expert_weights):
    n_expert = lax.axis_size("expert")
    expert_count = n_expert * expert_weights.shape[0]
    batch_rows = tokens.shape[0] // MICRO
    capacity = max(2, 4 * batch_rows // expert_count)
    gate = gates.T.astype(F32)
    weights_grad, token_grad, gate_sums = exchange(
        expert_ids.T, tokens, cotangent, gates.T, expert_weights[0],
        lax.axis_size("dp"), capacity,
    )
    return token_grad, (gate_sums / gate).astype(BF16).T, weights_grad[None]


def solution(mesh):
    placed = (
        P(("dp", "expert"), None),
        P(("dp", "expert"), None),
        P(("dp", "expert"), None),
        P(("dp", "expert"), None),
        P("expert", None, None, None),
    )
    return jax.shard_map(
        on_device,
        mesh=mesh,
        in_specs=placed,
        out_specs=(
            P(("dp", "expert"), None),
            P(("dp", "expert"), None),
            P("expert", None, "dp", None),
        ),
        check_vma=False,
    )
```

```python
import jax
import jax.numpy as jnp
from jax import lax
from jax.experimental import pallas as pl
from jax.experimental.pallas import tpu as pltpu
from jax.sharding import PartitionSpec as P

MICRO = 2
SPLITS = 1
SIDE = 4
PAD = 128

F32 = jnp.float32
BF16 = jnp.bfloat16

CONTRACT_LAST = (((1,), (1,)), ((), ()))
CONTRACT_FIRST = (((0,), (0,)), ((), ()))
MESH = pl.DeviceIdType.MESH


def mm(a, b):
    return jnp.dot(a, b, preferred_element_type=F32)


def route_masks(ids_block, expert_count, capacity):
    flat_ids = ids_block.reshape(-1)
    one_hot = (flat_ids[:, None] == jnp.arange(expert_count, dtype=jnp.int32)[None, :]).astype(
        jnp.int32
    )
    earlier = jnp.cumsum(one_hot, axis=0) - one_hot
    rank_slot = jnp.sum(earlier * one_hot, axis=1)
    route_slot = (flat_ids * capacity + rank_slot).reshape(-1, 2)
    position = jnp.arange(expert_count * capacity, dtype=jnp.int32)[:, None]
    return position == route_slot[None, :, 0], position == route_slot[None, :, 1]


def expert_step(recv, w_gate, w_up, w_down, width):
    rows_in = recv[:, :width]
    scaled = recv[:, width:]
    pre_gate = mm(rows_in, w_gate)
    pre_up = mm(rows_in, w_up)
    sigmoid_gate = jax.nn.sigmoid(pre_gate)
    activated = pre_gate * sigmoid_gate
    hidden = (activated * pre_up).astype(BF16)
    hidden_grad = mm(scaled, w_down)
    gate_sum = jnp.sum(hidden.astype(F32) * hidden_grad, axis=1)
    grad_pre_gate = (
        hidden_grad * pre_up * sigmoid_gate * (1.0 + pre_gate * (1.0 - sigmoid_gate))
    ).astype(BF16)
    grad_pre_up = (hidden_grad * activated).astype(BF16)
    input_grad = (
        lax.dot_general(grad_pre_gate, w_gate, CONTRACT_LAST, preferred_element_type=F32)
        + lax.dot_general(grad_pre_up, w_up, CONTRACT_LAST, preferred_element_type=F32)
    ).astype(BF16)
    grads = (
        lax.dot_general(rows_in, grad_pre_gate, CONTRACT_FIRST, preferred_element_type=F32),
        lax.dot_general(rows_in, grad_pre_up, CONTRACT_FIRST, preferred_element_type=F32),
        lax.dot_general(scaled, hidden, CONTRACT_FIRST, preferred_element_type=F32),
    )
    high = gate_sum.astype(BF16)
    low = (gate_sum - high.astype(F32)).astype(BF16)
    tail = jnp.concatenate(
        [high[:, None], low[:, None], jnp.zeros((recv.shape[0], PAD - 2), BF16)], axis=1
    )
    return jnp.concatenate([input_grad, tail], axis=1), grads


def exchange_kernel(ids_ref, x_ref, cot_ref, gate_ref, w_ref, out_ref, tg_ref, gs_ref,
                    p0, p1, ret0, ret1, recv, back, grad_ref, round_a, round_b, first_a, first_b,
                    part_a, part_b, second_a, second_b, send_sem, recv_sem, rs_send, rs_recv):
    n = lax.axis_size("expert")
    me = lax.axis_index("expert")
    n_row = lax.axis_size("dp")
    row = lax.axis_index("dp")
    phases = recv.shape[0]
    splits = phases // MICRO
    capacity = p0.shape[0] // n
    batch_rows = x_ref.shape[0] // MICRO
    n_experts = n * (p0.shape[0] // n // capacity)
    piece = capacity // splits
    width = w_ref.shape[1]
    part = out_ref.shape[1]
    payloads = (p0, p1)
    returns = (ret0, ret1)

    def selections(micro):
        rows = pl.ds(micro * batch_rows, batch_rows)
        ids = ids_ref[:, rows]
        expert = lax.broadcasted_iota(jnp.int32, (n_experts, batch_rows), 0)
        hot = [jnp.where(expert == ids[k:k + 1, :], 1.0, 0.0) for k in range(2)]
        before = lax.broadcasted_iota(jnp.int32, (batch_rows, batch_rows), 0)
        after = lax.broadcasted_iota(jnp.int32, (batch_rows, batch_rows), 1)
        earlier = jnp.where(before < after, 1.0, 0.0).astype(BF16)
        counts = mm((hot[0] + hot[1]).astype(BF16), earlier)
        position = lax.broadcasted_iota(jnp.int32, (p0.shape[0], batch_rows), 0)
        chosen = []
        for k in range(2):
            rank = jnp.sum(counts * hot[k], axis=0, keepdims=True).astype(jnp.int32)
            chosen.append(position == ids[k:k + 1, :] * capacity + rank)
        return chosen[0], chosen[1]

    def pack(micro):
        first, second = selections(micro)
        rows = pl.ds(micro * batch_rows, batch_rows)
        gate = gate_ref[:, rows].astype(F32)
        both_b = jnp.where(first | second, 1.0, 0.0).astype(BF16)
        gated = jnp.where(first, gate[0:1, :], jnp.where(second, gate[1:2, :], 0.0)).astype(BF16)
        dst = payloads[micro]
        dst[:, :width] = mm(both_b, x_ref[rows, :]).astype(BF16)
        dst[:, width:] = mm(gated, cot_ref[rows, :]).astype(BF16)

    def unpack(micro):
        first, second = selections(micro)
        both_b = jnp.where(first | second, 1.0, 0.0).astype(BF16)
        held = returns[micro][...]
        rows = pl.ds(micro * batch_rows, batch_rows)
        tg_ref[rows, :] = lax.dot_general(
            both_b, held[:, :width], CONTRACT_FIRST, preferred_element_type=F32
        ).astype(BF16)
        gate_sum = held[:, width:width + 1].astype(F32) + held[:, width + 1:width + 2].astype(F32)
        for index, chosen in enumerate((first, second)):
            gs_ref[index:index + 1, rows] = jnp.sum(
                jnp.where(chosen, gate_sum, 0.0), axis=0, keepdims=True
            )

    barrier = pltpu.get_barrier_semaphore()
    for k in range(1, n):
        peer = lax.rem(me + k, n)
        pl.semaphore_signal(barrier, inc=1, device_id=(row, peer), device_id_type=MESH)
    for k in range(1, n_row):
        peer = lax.rem(row + k, n_row)
        pl.semaphore_signal(barrier, inc=1, device_id=(peer, me), device_id_type=MESH)
    pack(0)
    pl.semaphore_wait(barrier, n - 1 + n_row - 1)

    def slot_rows(expert, phase):
        start = expert * capacity + (phase % splits) * piece
        return pl.ds(pl.multiple_of(start, piece), piece)

    def held_rows(source):
        return pl.ds(pl.multiple_of(source * piece, piece), piece)

    def scatter(phase, src_rows, dst_rows, src, dst, sem):
        pltpu.make_async_copy(src.at[src_rows(me)], dst.at[dst_rows(me)], recv_sem.at[sem]).start()
        for k in range(1, n):
            peer = lax.rem(me + k, n)
            pltpu.make_async_remote_copy(
                src_ref=src.at[src_rows(peer)],
                dst_ref=dst.at[dst_rows(me)],
                send_sem=send_sem.at[sem],
                recv_sem=recv_sem.at[sem],
                device_id=(row, peer),
                device_id_type=MESH,
            ).start()

    def send_forward(phase):
        scatter(phase, lambda e: slot_rows(e, phase), held_rows,
                payloads[phase // splits], recv.at[phase], phase)

    def send_back(phase):
        scatter(phase, held_rows, lambda e: slot_rows(e, phase),
                back.at[phase], returns[phase // splits], phases + phase)

    def wait_all(buf, sem):
        pltpu.make_async_copy(buf, buf, recv_sem.at[sem]).wait()

    def wait_sent(buf, sem):
        rest = pl.ds(0, (n - 1) * piece)
        pltpu.make_async_copy(buf.at[rest], buf.at[rest], send_sem.at[sem]).wait()

    side = SIDE
    col_a, col_b = row % side, row // side
    half = out_ref.shape[2] // 2

    def x_peer(k):
        return col_b * side + lax.rem(col_a + k, side)

    def y_peer(k):
        return lax.rem(col_b + k, side) * side + col_a

    def spread(src, dst, index, peer_of, sem):
        pltpu.make_async_copy(src.at[index], dst.at[index], rs_recv.at[sem]).start()
        for k in range(1, side):
            pltpu.make_async_remote_copy(
                src_ref=src.at[lax.rem(index + k, side)],
                dst_ref=dst.at[index],
                send_sem=rs_send.at[sem],
                recv_sem=rs_recv.at[sem],
                device_id=(peer_of(k), me),
                device_id_type=MESH,
            ).start()

    def scatter_grads():
        for block in range(n_row):
            rounded = grad_ref[:, block * part:(block + 1) * part, :].astype(BF16)
            round_a[block % side, block // side] = rounded[:, :, :half]
            round_b[block // side, block % side] = rounded[:, :, half:]
        spread(round_a, first_a, col_a, x_peer, 0)
        spread(round_b, first_b, col_b, y_peer, 1)

    def reduce_grads():
        pltpu.make_async_copy(first_a, first_a, rs_recv.at[0]).wait()
        total = first_a[0].astype(F32)
        for k in range(1, side):
            total = total + first_a[k].astype(F32)
        part_a[...] = total
        spread(part_a, second_a, col_b, y_peer, 2)
        pltpu.make_async_copy(first_b, first_b, rs_recv.at[1]).wait()
        total = first_b[0].astype(F32)
        for k in range(1, side):
            total = total + first_b[k].astype(F32)
        part_b[...] = total
        spread(part_b, second_b, col_a, x_peer, 3)
        for second, columns, sem in ((second_a, slice(0, half), 2),
                                     (second_b, slice(half, 2 * half), 3)):
            pltpu.make_async_copy(second, second, rs_recv.at[sem]).wait()
            total = second[0]
            for k in range(1, side):
                total = total + second[k]
            out_ref[:, :, columns] = total.astype(BF16)

    def compute(phase):
        held = recv.at[phase]
        rows_in = held[:, :width]
        scaled = held[:, width:]
        w_gate = w_ref[0]
        w_up = w_ref[1]
        w_down = w_ref[2]
        pre_gate = mm(rows_in, w_gate)
        pre_up = mm(rows_in, w_up)
        sigmoid_gate = jax.nn.sigmoid(pre_gate)
        activated = pre_gate * sigmoid_gate
        hidden = (activated * pre_up).astype(BF16)
        hidden_grad = mm(scaled, w_down)
        gate_sum = jnp.sum(hidden.astype(F32) * hidden_grad, axis=1, keepdims=True)
        grad_pre_gate = (
            hidden_grad * pre_up * sigmoid_gate * (1.0 + pre_gate * (1.0 - sigmoid_gate))
        ).astype(BF16)
        grad_pre_up = (hidden_grad * activated).astype(BF16)
        grads = (
            lax.dot_general(rows_in, grad_pre_gate, CONTRACT_FIRST, preferred_element_type=F32),
            lax.dot_general(rows_in, grad_pre_up, CONTRACT_FIRST, preferred_element_type=F32),
            lax.dot_general(scaled, hidden, CONTRACT_FIRST, preferred_element_type=F32),
        )
        for index, value in enumerate(grads):
            if phase == 0:
                grad_ref[index] = value
            elif phase < phases - 1:
                grad_ref[index] += value
            else:
                total = grad_ref[index] + value
                for block in range(n_row):
                    rounded = total[block * part:(block + 1) * part, :].astype(BF16)
                    round_a[block % side, block // side, index] = rounded[:, :half]
                    round_b[block // side, block % side, index] = rounded[:, half:]
        if phase == phases - 1:
            spread(round_a, first_a, col_a, x_peer, 0)
            spread(round_b, first_b, col_b, y_peer, 1)
        input_grad = (
            lax.dot_general(grad_pre_gate, w_gate, CONTRACT_LAST, preferred_element_type=F32)
            + lax.dot_general(grad_pre_up, w_up, CONTRACT_LAST, preferred_element_type=F32)
        ).astype(BF16)
        out = back.at[phase]
        out[:, :width] = input_grad
        high = gate_sum.astype(BF16).astype(F32)
        low = gate_sum - high
        column = lax.broadcasted_iota(jnp.int32, (input_grad.shape[0], PAD), 1)
        tail = jnp.where(column == 0, high, jnp.where(column == 1, low, 0.0))
        out[:, width:] = tail.astype(BF16)

    send_forward(0)
    pack(1)
    for phase in range(phases):
        wait_all(recv.at[phase], phase)
        if phase + 1 < phases:
            send_forward(phase + 1)
        compute(phase)
        send_back(phase)

    wait_all(back.at[0], phases)
    unpack(0)
    reduce_grads()

    for phase in range(phases):
        if phase > 0:
            wait_all(back.at[phase], phases + phase)
            unpack(phase)
        wait_sent(recv.at[phase], phase)
        wait_sent(back.at[phase], phases + phase)
    rest = pl.ds(0, side - 1)
    for sem, buf in enumerate((first_a, first_b, second_a, second_b)):
        pltpu.make_async_copy(buf.at[rest], buf.at[rest], rs_send.at[sem]).wait()


def exchange(slots, tokens, cotangent, gates, weights, n_row, capacity):
    n_expert = lax.axis_size("expert")
    rows = n_expert * capacity
    width = weights.shape[1]
    full = 2 * width
    part = width // n_row
    back = (rows, width + PAD)
    share = (weights.shape[0], part, weights.shape[2])
    quarter = (weights.shape[0], part, weights.shape[2] // 2)
    phases = MICRO
    vmem = pl.BlockSpec(memory_space=pltpu.VMEM)
    return pl.pallas_call(
        exchange_kernel,
        out_shape=(
            jax.ShapeDtypeStruct(share, BF16),
            jax.ShapeDtypeStruct(tokens.shape, BF16),
            jax.ShapeDtypeStruct((2, tokens.shape[0]), F32),
        ),
        in_specs=[vmem] * 5,
        out_specs=(vmem, vmem, vmem),
        scratch_shapes=[
            pltpu.VMEM((rows, full), BF16),
            pltpu.VMEM((rows, full), BF16),
            pltpu.VMEM(back, BF16),
            pltpu.VMEM(back, BF16),
            pltpu.VMEM((phases, rows, full), BF16),
            pltpu.VMEM((phases,) + back, BF16),
            pltpu.VMEM(weights.shape, F32),
            pltpu.VMEM((SIDE, SIDE) + quarter, BF16),
            pltpu.VMEM((SIDE, SIDE) + quarter, BF16),
            pltpu.VMEM((SIDE, SIDE) + quarter, BF16),
            pltpu.VMEM((SIDE, SIDE) + quarter, BF16),
            pltpu.VMEM((SIDE,) + quarter, F32),
            pltpu.VMEM((SIDE,) + quarter, F32),
            pltpu.VMEM((SIDE,) + quarter, F32),
            pltpu.VMEM((SIDE,) + quarter, F32),
            pltpu.SemaphoreType.DMA((2 * phases,)),
            pltpu.SemaphoreType.DMA((2 * phases,)),
            pltpu.SemaphoreType.DMA((4,)),
            pltpu.SemaphoreType.DMA((4,)),
        ],
        compiler_params=pltpu.CompilerParams(
            collective_id=0, has_side_effects=True, vmem_limit_bytes=62 * 1024 * 1024
        ),
    )(slots, tokens, cotangent, gates, weights)


def route_slot_rows(ids_block, expert_count, capacity):
    flat_ids = ids_block.reshape(-1)
    one_hot = (flat_ids[:, None] == jnp.arange(expert_count, dtype=jnp.int32)[None, :]).astype(
        jnp.int32
    )
    earlier = jnp.cumsum(one_hot, axis=0) - one_hot
    rank_slot = jnp.sum(earlier * one_hot, axis=1)
    return (flat_ids * capacity + rank_slot).reshape(-1, 2).T


def on_device(tokens, cotangent, gates, expert_ids, expert_weights):
    n_expert = lax.axis_size("expert")
    expert_count = n_expert * expert_weights.shape[0]
    batch_rows = tokens.shape[0] // MICRO
    capacity = max(2, 4 * batch_rows // expert_count)
    gate = gates.T.astype(F32)
    weights_grad, token_grad, gate_sums = exchange(
        expert_ids.T, tokens, cotangent, gates.T, expert_weights[0],
        lax.axis_size("dp"), capacity,
    )
    return token_grad, (gate_sums / gate).astype(BF16).T, weights_grad[None]


def solution(mesh):
    placed = (
        P(("dp", "expert"), None),
        P(("dp", "expert"), None),
        P(("dp", "expert"), None),
        P(("dp", "expert"), None),
        P("expert", None, None, None),
    )
    return jax.shard_map(
        on_device,
        mesh=mesh,
        in_specs=placed,
        out_specs=(
            P(("dp", "expert"), None),
            P(("dp", "expert"), None),
            P("expert", None, "dp", None),
        ),
        check_vma=False,
    )
```
